256 devices in a mesh: seq: 32 (over x, y, core), mp: 8 (over z).
Axes of the slice: x: 4, y: 4, z: 8, core: 2. Of those that a mesh axis runs over, the one named last changes fastest.
Arguments:
- x_branch: bfloat16 [8192, 8192], P('seq', 'mp'), may hold values from -6 to 6
- z_branch: bfloat16 [8192, 8192], P('seq', 'mp'), may hold values from -6 to 6
- conv_weight: float32 [4, 8192], P(None, 'mp'), may hold values from -3 to 3
- conv_bias: float32 [8192], P('mp'), may hold values from -0.5 to 0.5
- xproj_weight: bfloat16 [8192, 544], P('mp'), may hold values from -0.0625 to 0.0625
- dt_weight: bfloat16 [512, 8192], P(None, 'mp'), may hold values from -0.25 to 0.25
- dt_bias: float32 [8192], P('mp'), may hold values from -4 to -2
- decay_rate: float32 [16, 8192], P(None, 'mp'), may hold values from 0.00024414062 to 2
- skip_gain: float32 [8192], P('mp'), may hold values from 0.5 to 1.5
- query_rows: bfloat16 [8192, 8192], P('seq', 'mp'), may hold values from -6 to 6
- key_rows: bfloat16 [8192, 1024], P('seq', 'mp'), may hold values from -6 to 6
- value_rows: bfloat16 [8192, 1024], P('seq', 'mp'), may hold values from -6 to 6
- lengths: int32 [4], replicated, may hold values from 1 to 4096, as said below
- destination: int32 [8192], replicated, may hold values from 0 to 8191, as said below
Outputs:
- mamba_out: bfloat16 [8192, 8192], P('seq', 'mp')
- regrouped: bfloat16 [8192, 8192], P('seq', 'mp')
The draws below stay inside these ranges and needn't reach their ends.
Inputs may be any that keep to these rules, and one draw needn't show every extreme that they name: The 4 lengths sum to 8192, and the second of them equals 4096. destination is a permutation of 0 to 8191. Cut each aligned block of 256 positions into 32 runs of 8 consecutive positions: each run goes in order to consecutive rows of one aligned target block, the runs of block i to the rows that start at i * 8 within their target blocks, and the 32 runs of one block go to 32 different target blocks.
All inputs are finite; a program needn't handle non-finite values.
Results may differ from the reference program's by a relative error of at most 0.02.
Values may be sent and summed in bfloat16 or wider, within the bound.
A program may use at most 128 MiB of HBM per device.

```python
import math
import jax
import jax.numpy as jnp
from jax import lax

DI = 8192
NS = 16
R = 512
KC = 4
QH = 64
KVH = 8
HD = 128
TOK_DEV = 256
TOKENS = 8192
MAXDOC = 4096


def draw_query_rows(key, part):
    drawn_rows = jnp.clip(jax.random.normal(jax.random.fold_in(key, 11), (TOKENS, QH * HD), jnp.float32), -6.0, 6.0)
    return drawn_rows.astype(jnp.bfloat16)


def draw_key_rows(key, part):
    drawn_rows = jnp.clip(jax.random.normal(jax.random.fold_in(key, 12), (TOKENS, KVH * HD), jnp.float32), -6.0, 6.0)
    return drawn_rows.astype(jnp.bfloat16)


def pack_plan(key):
    plan_key = jax.random.fold_in(key, 30)
    first_lo = TOK_DEV + 1
    first_hi = TOKENS // 2 - 2 * TOK_DEV - KC
    first_len = jax.random.randint(jax.random.fold_in(plan_key, 1), (), first_lo, first_hi).astype(jnp.int32)
    after = (TOKENS - MAXDOC - first_len).astype(jnp.int32)
    quarter = after // 4
    third_len = (after // 2 + jax.random.randint(jax.random.fold_in(plan_key, 2), (), -TOK_DEV // 2, TOK_DEV // 2 + 1) * quarter // (TOK_DEV // 2)).astype(jnp.int32)
    lengths = jnp.stack([first_len, jnp.array(MAXDOC, jnp.int32), third_len, (after - third_len).astype(jnp.int32)]).astype(jnp.int32)
    doc_ends = jnp.cumsum(lengths).astype(jnp.int32)
    starts = (doc_ends - lengths).astype(jnp.int32)
    places = jnp.arange(TOKENS, dtype=jnp.int32)
    doc_ids = jnp.sum((places[:, None] >= doc_ends[None, :]).astype(jnp.int32), axis=1)
    depth = places - starts[doc_ids] + 1
    sources = TOKENS // TOK_DEV
    run_rows = TOK_DEV // sources
    block_cost = jnp.sum(depth.reshape(sources, sources, run_rows), axis=2).astype(jnp.int32)

    def place(source, carried):
        load, table = carried
        costs = block_cost[source]
        heavy_first = jnp.argsort(-costs, stable=True).astype(jnp.int32)
        light_first = jnp.argsort(load, stable=True).astype(jnp.int32)
        table = table.at[source, heavy_first].set(light_first)
        load = load.at[light_first].add(costs[heavy_first])
        return (load, table)
    initial = (jnp.zeros((sources,), jnp.int32), jnp.zeros((sources, sources), jnp.int32))
    unused_load, table = lax.fori_loop(0, sources, place, initial)
    source_of = places // TOK_DEV
    run_of = places % TOK_DEV // run_rows
    offset = places % run_rows
    destination = (table[source_of, run_of] * TOK_DEV + source_of * run_rows + offset).astype(jnp.int32)
    return (lengths, destination)


def draw_lengths(key, part):
    return pack_plan(key)[0]


def draw_destination(key, part):
    return pack_plan(key)[1]


def shard_levels(key, extent, cuts, least, top_value):
    def one(axis_at, parts):
        steps = jax.random.uniform(jax.random.fold_in(jax.random.fold_in(key, 6), axis_at), (parts,), jnp.float32, least / len(cuts), top_value / len(cuts))
        return jnp.repeat(jnp.exp(steps), extent[axis_at] // parts).reshape((-1,) + (1,) * (len(extent) - axis_at - 1))

    gain = one(*cuts[0])
    for cut in cuts[1:]:
        gain = gain * one(*cut)
    return gain


def gaussian(stream_key, dims, spread, bound, shards=(), held_as=jnp.bfloat16):
    entries = jax.random.normal(stream_key, dims, jnp.float32) * spread
    if len(shards) > 0:
        entries = shard_levels(stream_key, dims, shards, -0.22, 0.18) * entries
    return jnp.clip(entries, min=-bound, max=bound).astype(held_as)


def setup_inputs(seed: int = 0) -> dict:
    keys = jax.random.split(jax.random.key(seed), 15)
    x_branch = gaussian(keys[0], (TOKENS, DI), 1.0, 6.0, ((0, 32), (1, 8)))
    z_branch = gaussian(keys[1], (TOKENS, DI), 1.0, 6.0, ((0, 32), (1, 8)))
    conv_weight = gaussian(keys[2], (KC, DI), 0.5, 3.0, ((1, 8),), jnp.float32)
    conv_bias = jnp.clip(jax.random.uniform(keys[3], (DI,), jnp.float32, -0.5, 0.5) * shard_levels(keys[3], (DI,), ((0, 8),), -0.4, 0.0), -0.5, 0.5)
    xproj_weight = gaussian(keys[4], (DI, R + 2 * NS), DI ** -0.5, 0.0625, ((0, 8),))
    dt_weight = gaussian(keys[5], (R, DI), R ** -0.5, 0.25, ((1, 8),))
    dt_bias = jnp.clip(-4.0 + 2.0 * jax.random.uniform(keys[6], (DI,), jnp.float32) ** shard_levels(keys[6], (DI,), ((0, 8),), -0.2, 0.2), -4.0, -2.0)
    decay_rate = jnp.clip(jnp.exp(math.log(2.0) - 9.010913 * jax.random.uniform(keys[7], (NS, DI), jnp.float32) ** shard_levels(keys[7], (NS, DI), ((1, 8),), -0.2, 0.2)), 0.00024414062, 2.0)
    skip_gain = jnp.clip(0.5 + 1.0 * jax.random.uniform(keys[8], (DI,), jnp.float32) ** shard_levels(keys[8], (DI,), ((0, 8),), -0.2, 0.2), 0.5, 1.5)
    query_rows = draw_query_rows(jax.random.fold_in(keys[14], 71), 0)
    key_rows = draw_key_rows(jax.random.fold_in(keys[14], 71), 0)
    value_rows = gaussian(keys[11], (TOKENS, KVH * HD), 1.0, 6.0, ((0, 32), (1, 8)))
    lengths = draw_lengths(jax.random.fold_in(keys[14], 71), 0)
    destination = draw_destination(jax.random.fold_in(keys[14], 71), 0)
    return dict(x_branch=x_branch, z_branch=z_branch, conv_weight=conv_weight, conv_bias=conv_bias, xproj_weight=xproj_weight, dt_weight=dt_weight, dt_bias=dt_bias, decay_rate=decay_rate, skip_gain=skip_gain, query_rows=query_rows, key_rows=key_rows, value_rows=value_rows, lengths=lengths, destination=destination)


masked_score = -1.0e30


def doc_lookup(lengths, places):
    doc_ends = jnp.cumsum(lengths).astype(jnp.int32)
    starts = (doc_ends - lengths).astype(jnp.int32)
    doc_ids = jnp.sum((places[:, None] >= doc_ends[None, :]).astype(jnp.int32), axis=1)
    at_start = jnp.any(places[:, None] == starts[None, :], axis=1)
    return doc_ids, at_start


def mamba_mixer(x_branch, z_branch, conv_weight, conv_bias, xproj_weight, dt_weight, dt_bias, decay_rate, skip_gain, lengths):
    places = jnp.arange(TOKENS, dtype=jnp.int32)
    doc_ids, at_start = doc_lookup(lengths, places)
    padded = jnp.concatenate([jnp.zeros((KC - 1, DI), jnp.float32), x_branch.astype(jnp.float32)], axis=0)
    padded_docs, unused = doc_lookup(lengths, jnp.arange(TOKENS + KC - 1, dtype=jnp.int32) - (KC - 1))
    conv_sum = conv_bias[None, :] + jnp.zeros((TOKENS, DI), jnp.float32)
    for lag_step in range(KC):
        window = padded[KC - 1 - lag_step:KC - 1 - lag_step + TOKENS]
        same_doc = padded_docs[KC - 1 - lag_step:KC - 1 - lag_step + TOKENS] == doc_ids
        conv_sum = conv_sum + conv_weight[lag_step][None, :] * jnp.where(same_doc[:, None], window, 0.0)
    inner_act = jax.nn.silu(conv_sum).astype(jnp.bfloat16)
    projected = jnp.dot(inner_act, xproj_weight, preferred_element_type=jnp.float32)
    dt_low = projected[:, :R].astype(jnp.bfloat16)
    step_size = jax.nn.softplus(jnp.dot(dt_low, dt_weight, preferred_element_type=jnp.float32) + dt_bias[None, :])
    b_input = projected[:, R:R + NS]
    c_output = projected[:, R + NS:]
    inner_float = inner_act.astype(jnp.float32)
    drive_term = step_size * inner_float
    keep_mask = jnp.where(at_start, 0.0, 1.0).astype(jnp.float32)

    def advance(carried, inputs):
        step_row, drive_row, keep_row, b_row, c_row = inputs
        decay_now = jnp.exp(-step_row[None, :] * decay_rate) * keep_row
        carried = decay_now * carried + b_row[:, None] * drive_row[None, :]
        return carried, jnp.sum(c_row[:, None] * carried, axis=0)

    initial = jnp.zeros((NS, DI), jnp.float32)
    unused_end, scanned = lax.scan(advance, initial, (step_size, drive_term, keep_mask, b_input, c_output))
    scanned = scanned + skip_gain[None, :] * inner_float
    return (scanned * jax.nn.silu(z_branch.astype(jnp.float32))).astype(jnp.bfloat16), doc_ids


def attend_all(query_rows, key_rows, value_rows, doc_ids):
    group_size = QH // KVH
    span = min(TOKENS, TOK_DEV + MAXDOC)
    factor = HD ** -0.5

    def one_block(block_index):
        query_start = block_index * TOK_DEV
        key_start = jnp.clip(query_start + TOK_DEV - span, 0, TOKENS - span).astype(jnp.int32)
        query_block = lax.dynamic_slice_in_dim(query_rows, query_start, TOK_DEV, 0).astype(jnp.float32).reshape(TOK_DEV, KVH, group_size, HD)
        key_block = lax.dynamic_slice_in_dim(key_rows, key_start, span, 0).astype(jnp.float32).reshape(span, KVH, HD)
        value_block = lax.dynamic_slice_in_dim(value_rows, key_start, span, 0).astype(jnp.float32).reshape(span, KVH, HD)
        query_places = query_start + jnp.arange(TOK_DEV, dtype=jnp.int32)
        key_places = key_start + jnp.arange(span, dtype=jnp.int32)
        query_docs = lax.dynamic_slice_in_dim(doc_ids, query_start, TOK_DEV, 0)
        key_docs = lax.dynamic_slice_in_dim(doc_ids, key_start, span, 0)
        visible = (key_places[None, :] <= query_places[:, None]) & (key_docs[None, :] == query_docs[:, None])
        scores = jnp.einsum("qhgd,khd->hgqk", query_block, key_block) * factor
        scores = jnp.where(visible[None, None], scores, masked_score)
        best_score = jnp.max(scores, axis=3, keepdims=True)
        weights = jnp.where(visible[None, None], jnp.exp(scores - best_score), 0.0)
        weight_sum = jnp.sum(weights, axis=3)
        rounded = lax.optimization_barrier(weights.astype(jnp.bfloat16)).astype(jnp.float32)
        summed = jnp.einsum("hgqk,khd->qhgd", rounded, value_block)
        result = summed / jnp.transpose(weight_sum, (2, 0, 1))[..., None]
        return result.reshape(TOK_DEV, QH * HD).astype(jnp.bfloat16)

    blocks = lax.map(one_block, jnp.arange(TOKENS // TOK_DEV, dtype=jnp.int32))
    return blocks.reshape(TOKENS, QH * HD)


def reference(x_branch, z_branch, conv_weight, conv_bias, xproj_weight, dt_weight, dt_bias, decay_rate, skip_gain, query_rows, key_rows, value_rows, lengths, destination):
    mamba_out, doc_ids = mamba_mixer(x_branch, z_branch, conv_weight, conv_bias, xproj_weight, dt_weight, dt_bias, decay_rate, skip_gain, lengths)
    attended = attend_all(query_rows, key_rows, value_rows, doc_ids)
    regrouped = jnp.zeros((TOKENS, QH * HD), jnp.bfloat16).at[destination].set(attended)
    return (mamba_out, regrouped)
```

```python
import math

import jax
import jax.numpy as jnp
from jax import lax
from jax.experimental import pallas as pl
from jax.experimental.pallas import tpu as pltpu
from jax.sharding import Mesh
from jax.sharding import PartitionSpec as P

SEQ = ("seq_0", "seq_1", "seq_2")
MESH = pl.DeviceIdType.MESH
VM = pltpu.VMEM
F32 = jnp.float32
BF16 = jnp.bfloat16
LOG2E = math.log2(math.e)
NX, NY, NC, NZ = 4, 4, 2, 8
NSEQ = NX * NY * NC
TOK = 256
CH = 1024
LANE = 128
SUB = CH // LANE
NS = 16
RANK = 512
PROJ = RANK + 2 * NS
HD = 128
TAPS = 4
REACH = 16
BIG_STEP = 1.0e7
MASKED = -1.0e30
GROUP = 4
RUN = TOK // NSEQ
BK = 256
VLIM = 60 * 1024 * 1024


def whole(space=VM):
    return pl.BlockSpec(memory_space=space)


def place():
    return (
        lax.axis_index("seq_0"),
        lax.axis_index("seq_1"),
        lax.axis_index("seq_2"),
        lax.axis_index("mp"),
    )


def seq_device(j, z):
    return (j // (NY * NC), (j // NC) % NY, j % NC, z)


def doc_starts(len_ref):
    s1 = len_ref[0]
    s2 = s1 + len_ref[1]
    return s1, s2, s2 + len_ref[2]


def start_of(pos, starts):
    s1, s2, s3 = starts
    return jnp.where(pos >= s3, s3, jnp.where(pos >= s2, s2, jnp.where(pos >= s1, s1, 0)))


def silu(x):
    return x / (1.0 + jnp.exp(-x))


def gather_kernel(
    inv_ref,
    len_ref,
    q_ref,
    k_ref,
    v_ref,
    x_ref,
    cw_ref,
    cb_ref,
    xw_ref,
    q_out,
    kv_out,
    proj_out,
    inner_out,
    kvs,
    qs,
    halo,
    ext,
    part,
    rs,
    own,
    loc_sem,
    halo_sem,
    kv_send,
    kv_recv,
    q_send,
    q_recv,
    rs_send,
    rs_recv,
    ag_send,
    ag_recv,
):
    x, y, c, z = place()
    me = (x * NY + y) * NC + c
    barrier = pltpu.get_barrier_semaphore()
    for k in range(1, NSEQ):
        pl.semaphore_signal(
            barrier, inc=1, device_id=seq_device((me + k) % NSEQ, z), device_id_type=MESH
        )
    for k in range(1, NZ):
        pl.semaphore_signal(
            barrier, inc=1, device_id=(x, y, c, (z + k) % NZ), device_id_type=MESH
        )
    load_k = pltpu.make_async_copy(k_ref, kvs.at[:, pl.ds(0, HD)], loc_sem.at[0])
    load_v = pltpu.make_async_copy(v_ref, kvs.at[:, pl.ds(HD, HD)], loc_sem.at[1])
    load_k.start()
    load_v.start()
    for j in range(NSEQ):
        qs[j] = q_ref[inv_ref[j]]
    load_k.wait()
    load_v.wait()
    pl.semaphore_wait(barrier, NSEQ - 1 + NZ - 1)

    def remote(src, dst, send, recv, device):
        return pltpu.make_async_remote_copy(
            src_ref=src,
            dst_ref=dst,
            send_sem=send,
            recv_sem=recv,
            device_id=device,
            device_id_type=MESH,
        )

    def offset(a, b, core):
        return (x + a * (1 - core) + b * core) % NX, (y + a * core + b * (1 - core)) % NY

    def rows_of(a, b, core):
        px, py = offset(a, b, core)
        return pl.ds(pl.multiple_of(((px * NY + py) * NC + core) * TOK, TOK), TOK)

    partner = (x, y, 1 - c, z)
    after = (me + 1) % NSEQ
    halo_copy = remote(
        x_ref.at[pl.ds(TOK - 16, 16)], halo, halo_sem.at[0], halo_sem.at[1], seq_device(after, z)
    )
    halo_copy.start()
    mine = kv_out.at[rows_of(0, 0, c)]
    sends = []
    for a in range(1, NX):
        px, py = offset(a, 0, c)
        copy = remote(kvs, mine, kv_send.at[a], kv_recv.at[a], (px, py, c, z))
        copy.start()
        sends.append(copy)
    copy = remote(kvs, mine, kv_send.at[16], kv_recv.at[16], partner)
    copy.start()
    sends.append(copy)
    keep_kv = pltpu.make_async_copy(kvs, mine, loc_sem.at[0])
    keep_kv.start()
    q_rows = pl.ds(pl.multiple_of(me * RUN, RUN), RUN)
    for k in range(1, NSEQ):
        j = (me + k) % NSEQ
        copy = remote(qs.at[j], q_out.at[q_rows], q_send.at[k], q_recv.at[k], seq_device(j, z))
        copy.start()
        sends.append(copy)
    keep_q = pltpu.make_async_copy(qs.at[me], q_out.at[q_rows], loc_sem.at[1])
    keep_q.start()

    halo_copy.wait()
    ext[pl.ds(0, 8), :] = halo[pl.ds(8, 8), :].astype(F32)
    starts = doc_starts(len_ref)
    token = me * TOK + lax.broadcasted_iota(jnp.int32, (TOK, LANE), 0)
    depth = token - start_of(token, starts)

    def conv_columns(i, carry):
        cols = pl.ds(pl.multiple_of(i * LANE, LANE), LANE)
        ext[pl.ds(8, TOK), cols] = x_ref[:, cols].astype(F32)
        total = cb_ref[:, cols] + cw_ref[pl.ds(0, 1), cols] * ext[pl.ds(8, TOK), cols]
        for lag in range(1, TAPS):
            window = ext[pl.ds(8 - lag, TOK), cols]
            total = total + cw_ref[pl.ds(lag, 1), cols] * jnp.where(depth >= lag, window, 0.0)
        inner_out[:, cols] = silu(total).astype(BF16)
        return carry

    lax.fori_loop(0, SUB, conv_columns, 0)

    partial = jnp.dot(inner_out[...], xw_ref[...], preferred_element_type=F32).astype(BF16)
    part[...] = partial.reshape(NZ, TOK // NZ, PROJ)
    for k in range(1, NZ):
        j = (z + k) % NZ
        copy = remote(part.at[j], rs.at[k], rs_send.at[k], rs_recv.at[k], (x, y, c, j))
        copy.start()
        sends.append(copy)

    def wait_kv(slot_rows, index):
        remote(kvs, kv_out.at[slot_rows], kv_send.at[0], kv_recv.at[index], partner).wait_recv()

    for a in range(NX):
        if a > 0:
            wait_kv(rows_of(-a, 0, c), a)
        block = kv_out.at[rows_of(-a, 0, c)] if a > 0 else kvs
        target = kv_out.at[rows_of(-a, 0, c)]
        for b in range(1, NY):
            px, py = offset(0, b, c)
            index = b * NX + a
            copy = remote(block, target, kv_send.at[index], kv_recv.at[index], (px, py, c, z))
            copy.start()
            sends.append(copy)
        if a > 0:
            copy = remote(block, target, kv_send.at[16 + a], kv_recv.at[16 + a], partner)
            copy.start()
            sends.append(copy)

    total = part[z].astype(F32)
    for k in range(1, NZ):
        remote(part.at[0], rs.at[k], rs_send.at[k], rs_recv.at[k], partner).wait_recv()
        total = total + rs[k].astype(F32)
    own[...] = total.astype(BF16)
    slice_rows = TOK // NZ
    own_rows = pl.ds(pl.multiple_of(z * slice_rows, slice_rows), slice_rows)
    for k in range(1, NZ):
        copy = remote(
            own, proj_out.at[own_rows], ag_send.at[k], ag_recv.at[k], (x, y, c, (z + k) % NZ)
        )
        copy.start()
        sends.append(copy)
    proj_out[own_rows, :] = own[...]

    for b in range(1, NY):
        for a in range(NX):
            index = b * NX + a
            wait_kv(rows_of(-a, -b, c), index)
            block = kv_out.at[rows_of(-a, -b, c)]
            copy = remote(block, block, kv_send.at[16 + index], kv_recv.at[16 + index], partner)
            copy.start()
            sends.append(copy)
    for k in range(1, NZ):
        rows = pl.ds(pl.multiple_of(((z + NZ - k) % NZ) * slice_rows, slice_rows), slice_rows)
        remote(own, proj_out.at[rows], ag_send.at[k], ag_recv.at[k], partner).wait_recv()
    for k in range(1, NSEQ):
        rows = pl.ds(pl.multiple_of(((me + NSEQ - k) % NSEQ) * RUN, RUN), RUN)
        remote(qs.at[0], q_out.at[rows], q_send.at[k], q_recv.at[k], partner).wait_recv()
    for b in range(NY):
        for a in range(NX):
            wait_kv(rows_of(-a, -b, 1 - c), 16 + b * NX + a)
    for copy in sends:
        copy.wait_send()
    keep_kv.wait()
    keep_q.wait()


def gather_all(inverse, lengths, q, k, v, x, cw, cb, xw):
    dma = pltpu.SemaphoreType.DMA
    return pl.pallas_call(
        gather_kernel,
        out_shape=(
            jax.ShapeDtypeStruct((TOK, CH), BF16),
            jax.ShapeDtypeStruct((NSEQ * TOK, 2 * HD), BF16),
            jax.ShapeDtypeStruct((TOK, PROJ), BF16),
            jax.ShapeDtypeStruct((TOK, CH), BF16),
        ),
        in_specs=[whole(pltpu.SMEM)] * 2
        + [whole()]
        + [whole(pl.ANY)] * 2
        + [whole()] * 4,
        out_specs=(whole(pl.ANY), whole(pl.ANY), whole(), whole()),
        scratch_shapes=[
            VM((TOK, 2 * HD), BF16),
            VM((NSEQ, RUN, CH), BF16),
            VM((16, CH), BF16),
            VM((TOK + 8, CH), F32),
            VM((NZ, TOK // NZ, PROJ), BF16),
            VM((NZ, TOK // NZ, PROJ), BF16),
            VM((TOK // NZ, PROJ), BF16),
            dma((2,)),
            dma((2,)),
            dma((32,)),
            dma((32,)),
            dma((NSEQ,)),
            dma((NSEQ,)),
            dma((NZ,)),
            dma((NZ,)),
            dma((NZ,)),
            dma((NZ,)),
        ],
        compiler_params=pltpu.CompilerParams(
            collective_id=0, has_side_effects=True, vmem_limit_bytes=VLIM
        ),
        name="gather",
    )(inverse, lengths, q, k, v, x, cw, cb, xw)


def spread_columns(proj_ref, first, count):
    row = lax.broadcasted_iota(jnp.int32, (count, count * LANE), 0)
    col = lax.broadcasted_iota(jnp.int32, (count, count * LANE), 1)
    pick = jnp.where(col // LANE == row, 1.0, 0.0).astype(BF16)
    return jnp.dot(proj_ref[:, pl.ds(first, count)], pick, preferred_element_type=F32)


def local_scan_kernel(
    len_ref, me_ref, proj_ref, inner_ref, dtw_ref, dtb_ref, rate_ref, st_out, step_out, drive_out,
    rate_out, bcs, sums,
):
    starts = doc_starts(len_ref)
    token = me_ref[0] * TOK + lax.broadcasted_iota(jnp.int32, (TOK, LANE), 0)
    begins = token == start_of(token, starts)
    for j in range(SUB):
        cols = pl.ds(j * LANE, LANE)
        raw = jnp.dot(proj_ref[:, pl.ds(0, RANK)], dtw_ref[:, cols], preferred_element_type=F32)
        step = jax.nn.softplus(raw + dtb_ref[:, cols])
        drive = step * inner_ref[:, cols].astype(F32)
        step = jnp.where(begins, BIG_STEP, step)
        sums[pl.ds(j, 1), :] = jnp.sum(step, axis=0, keepdims=True)
        step_out[pl.ds(j, TOK, stride=SUB), :] = step
        drive_out[pl.ds(j, TOK, stride=SUB), :] = drive
        rate_out[pl.ds(j, NS, stride=SUB), :] = rate_ref[:, cols] * (-LOG2E)
    spread = spread_columns(proj_ref, RANK, NS)
    for n in range(NS):
        bcs[pl.ds(n * TOK, TOK), :] = spread[:, n * LANE : (n + 1) * LANE]
    rates = [rate_out[pl.ds(n * SUB, SUB), :] for n in range(NS)]

    def advance(t, carried):
        rows = pl.ds(pl.multiple_of(t * SUB, SUB), SUB)
        step = step_out[rows, :]
        drive = drive_out[rows, :]
        result = []
        for n in range(NS):
            b = bcs[pl.ds(n * TOK + t, SUB, stride=0), :]
            result.append(jnp.exp2(step * rates[n]) * carried[n] + b * drive)
        return tuple(result)

    zero = jnp.zeros((SUB, LANE), F32)
    state = lax.fori_loop(0, TOK, advance, (zero,) * NS, unroll=4)
    for n in range(0, NS, 2):
        pair = jnp.concatenate([state[n], state[n + 1]], axis=0)
        st_out[pl.ds(n * SUB, 2 * SUB), :] = pair.astype(BF16)
    total = sums[...]
    high = total.astype(BF16)
    low = total - high.astype(F32)
    st_out[pl.ds(NS * SUB, 2 * SUB), :] = jnp.concatenate([high.astype(F32), low], axis=0).astype(BF16)


def local_scan(lengths, me, proj, inner, dtw, dtb, rate):
    return pl.pallas_call(
        local_scan_kernel,
        out_shape=(
            jax.ShapeDtypeStruct(((NS + 2) * SUB, LANE), BF16),
            jax.ShapeDtypeStruct((TOK * SUB, LANE), F32),
            jax.ShapeDtypeStruct((TOK * SUB, LANE), F32),
            jax.ShapeDtypeStruct((NS * SUB, LANE), F32),
        ),
        in_specs=[whole(pltpu.SMEM)] * 2 + [whole()] * 5,
        out_specs=(whole(),) * 4,
        scratch_shapes=[VM((NS * TOK, LANE), F32), VM((SUB, LANE), F32)],
        compiler_params=pltpu.CompilerParams(vmem_limit_bytes=VLIM),
        name="local_scan",
    )(lengths, me, proj, inner, dtw, dtb, rate)


def enter_kernel(st_ref, rate_ref, in_out, slots, send_sem, recv_sem):
    x, y, c, z = place()
    me = (x * NY + y) * NC + c
    barrier = pltpu.get_barrier_semaphore()
    for k in range(1, REACH + 1):
        pl.semaphore_signal(
            barrier, inc=1, device_id=seq_device((me + NSEQ - k) % NSEQ, z), device_id_type=MESH
        )
    pl.semaphore_wait(barrier, REACH)
    copies = []
    for k in range(1, REACH + 1):
        copy = pltpu.make_async_remote_copy(
            src_ref=st_ref,
            dst_ref=slots.at[k - 1],
            send_sem=send_sem.at[k - 1],
            recv_sem=recv_sem.at[k - 1],
            device_id=seq_device((me + k) % NSEQ, z),
            device_id_type=MESH,
        )
        copy.start()
        copies.append(copy)
    total = jnp.zeros((NS, SUB, LANE), F32)
    rate = rate_ref[...].reshape(NS, SUB, LANE)
    for k in range(REACH, 0, -1):
        copies[k - 1].wait_recv()
        block = slots[k - 1].astype(F32).reshape(NS + 2, SUB, LANE)
        steps = block[NS] + block[NS + 1]
        moved = jnp.exp2(rate * steps[None]) * total + block[:NS]
        total = jnp.where(me >= k, moved, 0.0)
    in_out[...] = total.reshape(NS * SUB, LANE)
    for copy in copies:
        copy.wait_send()


def enter(st, rate):
    dma = pltpu.SemaphoreType.DMA
    return pl.pallas_call(
        enter_kernel,
        out_shape=jax.ShapeDtypeStruct((NS * SUB, LANE), F32),
        in_specs=[whole()] * 2,
        out_specs=whole(),
        scratch_shapes=[VM((REACH, (NS + 2) * SUB, LANE), BF16), dma((REACH,)), dma((REACH,))],
        compiler_params=pltpu.CompilerParams(
            collective_id=1, has_side_effects=True, vmem_limit_bytes=VLIM
        ),
        name="enter",
    )(st, rate)


def output_kernel(
    in_ref, step_ref, drive_ref, rate_ref, proj_ref, inner_ref, z_ref, skip_ref, out, bcs, ys
):
    spread = spread_columns(proj_ref, RANK, 2 * NS)
    for n in range(2 * NS):
        bcs[pl.ds(n * TOK, TOK), :] = spread[:, n * LANE : (n + 1) * LANE]
    rates = [rate_ref[pl.ds(n * SUB, SUB), :] for n in range(NS)]

    def advance(t, carried):
        rows = pl.ds(pl.multiple_of(t * SUB, SUB), SUB)
        step = step_ref[rows, :]
        drive = drive_ref[rows, :]
        result = []
        total = None
        for n in range(NS):
            b = bcs[pl.ds(n * TOK + t, SUB, stride=0), :]
            weight = bcs[pl.ds((NS + n) * TOK + t, SUB, stride=0), :]
            state = jnp.exp2(step * rates[n]) * carried[n] + b * drive
            result.append(state)
            total = weight * state if total is None else total + weight * state
        ys[rows, :] = total
        return tuple(result)

    first = tuple(in_ref[pl.ds(n * SUB, SUB), :] for n in range(NS))
    lax.fori_loop(0, TOK, advance, first, unroll=4)
    for j in range(SUB):
        cols = pl.ds(j * LANE, LANE)
        scanned = ys[pl.ds(j, TOK, stride=SUB), :] + skip_ref[:, cols] * inner_ref[:, cols].astype(F32)
        out[:, cols] = (scanned * silu(z_ref[:, cols].astype(F32))).astype(BF16)


def scan_output(h_in, step, drive, rate, proj, inner, z, skip):
    return pl.pallas_call(
        output_kernel,
        out_shape=jax.ShapeDtypeStruct((TOK, CH), BF16),
        in_specs=[whole()] * 8,
        out_specs=whole(),
        scratch_shapes=[VM((2 * NS * TOK, LANE), F32), VM((TOK * SUB, LANE), F32)],
        compiler_params=pltpu.CompilerParams(vmem_limit_bytes=VLIM),
        name="scan_output",
    )(h_in, step, drive, rate, proj, inner, z, skip)


def attend_kernel(pos_ref, len_ref, q_ref, kv_ref, out):
    g = pl.program_id(0)
    heads = CH // HD
    rows = GROUP * RUN
    starts = doc_starts(len_ref)
    bases = [pos_ref[g * GROUP + i] for i in range(GROUP)]
    row = lax.broadcasted_iota(jnp.int32, (rows, BK), 0)
    col = lax.broadcasted_iota(jnp.int32, (rows, BK), 1)
    base = bases[0]
    for i in range(1, GROUP):
        base = jnp.where(row >= i * RUN, bases[i], base)
    pos = base + row % RUN
    start = start_of(pos, starts)
    first = start_of(bases[0], starts) // BK
    last = (bases[GROUP - 1] + RUN - 1) // BK
    q = jnp.concatenate([q_ref[:, h * HD : (h + 1) * HD] for h in range(heads)], axis=0)
    scale = HD**-0.5 * LOG2E

    def absorb(kb, carried):
        best, weight_sum, summed = carried
        key_rows = pl.ds(pl.multiple_of(kb * BK, BK), BK)
        keys = kv_ref[key_rows, pl.ds(0, HD)]
        values = kv_ref[key_rows, pl.ds(HD, HD)]
        scores = lax.dot_general(
            q, keys, (((1,), (1,)), ((), ())), preferred_element_type=F32
        ).reshape(heads, rows, BK)
        places = col + kb * BK
        visible = (places <= pos) & (places >= start)
        scores = jnp.where(visible[None], scores * scale, MASKED).reshape(heads * rows, BK)
        new_best = jnp.maximum(best, jnp.max(scores, axis=1, keepdims=True))
        weights = jnp.exp2(scores - new_best)
        rescale = jnp.exp2(best - new_best)
        weight_sum = weight_sum * rescale + jnp.sum(weights, axis=1, keepdims=True)
        product = jnp.dot(weights.astype(BF16), values, preferred_element_type=F32)
        return new_best, weight_sum, summed * rescale + product

    initial = (
        jnp.full((heads * rows, 1), MASKED, F32),
        jnp.zeros((heads * rows, 1), F32),
        jnp.zeros((heads * rows, HD), F32),
    )
    best, weight_sum, summed = lax.fori_loop(first, last + 1, absorb, initial)
    result = (summed / weight_sum).astype(BF16)
    for h in range(heads):
        out[:, h * HD : (h + 1) * HD] = result[h * rows : (h + 1) * rows]


def attend(positions, lengths, q, kv):
    rows = GROUP * RUN
    return pl.pallas_call(
        attend_kernel,
        out_shape=jax.ShapeDtypeStruct((TOK, CH), BF16),
        grid=(NSEQ // GROUP,),
        in_specs=[
            whole(pltpu.SMEM),
            whole(pltpu.SMEM),
            pl.BlockSpec((rows, CH), lambda g: (g, 0)),
            whole(),
        ],
        out_specs=pl.BlockSpec((rows, CH), lambda g: (g, 0)),
        compiler_params=pltpu.CompilerParams(vmem_limit_bytes=VLIM),
        name="attend",
    )(positions, lengths, q, kv)


def local(
    x_branch,
    z_branch,
    conv_weight,
    conv_bias,
    xproj_weight,
    dt_weight,
    dt_bias,
    decay_rate,
    skip_gain,
    query_rows,
    key_rows,
    value_rows,
    lengths,
    destination,
):
    me = lax.axis_index(SEQ)
    targets = destination.reshape(NSEQ, NSEQ, RUN)[:, :, 0] // TOK
    runs = jnp.arange(NSEQ, dtype=jnp.int32)
    own = lax.dynamic_slice_in_dim(targets, me, 1, 0)
    inverse = jnp.sum(jnp.where(own == runs[:, None], runs[None, :], 0), axis=1)
    positions = runs * TOK + RUN * jnp.sum(jnp.where(targets == me, runs[None, :], 0), axis=1)
    q, kv, proj, inner = gather_all(
        inverse,
        lengths,
        query_rows.reshape(NSEQ, RUN, CH),
        key_rows,
        value_rows,
        x_branch,
        conv_weight,
        conv_bias.reshape(1, CH),
        xproj_weight,
    )
    st, step, drive, rate = local_scan(
        lengths,
        me.reshape(1).astype(jnp.int32),
        proj,
        inner,
        dt_weight,
        dt_bias.reshape(1, CH),
        decay_rate,
    )
    h_in = enter(st, rate)
    mamba_out = scan_output(
        h_in, step, drive, rate, proj, inner, z_branch, skip_gain.reshape(1, CH)
    )
    regrouped = attend(positions, lengths, q, kv)
    return (mamba_out, regrouped)


def solution(mesh):
    torus = Mesh(mesh.devices.reshape(NX, NY, NC, mesh.shape["mp"]), (*SEQ, "mp"))
    in_specs = (
        P(SEQ, "mp"),
        P(SEQ, "mp"),
        P(None, "mp"),
        P("mp"),
        P("mp", None),
        P(None, "mp"),
        P("mp"),
        P(None, "mp"),
        P("mp"),
        P(SEQ, "mp"),
        P(SEQ, "mp"),
        P(SEQ, "mp"),
        P(),
        P(),
    )
    out_specs = (P(SEQ, "mp"), P(SEQ, "mp"))
    return jax.shard_map(local, mesh=torus, in_specs=in_specs, out_specs=out_specs, check_vma=False)
```

```python
import math

import jax
import jax.numpy as jnp
from jax import lax
from jax.experimental import pallas as pl
from jax.experimental.pallas import tpu as pltpu
from jax.sharding import Mesh
from jax.sharding import PartitionSpec as P

SEQ = ("seq_0", "seq_1", "seq_2")
MESH = pl.DeviceIdType.MESH
VM = pltpu.VMEM
F32 = jnp.float32
BF16 = jnp.bfloat16
LOG2E = math.log2(math.e)
NX, NY, NC, NZ = 4, 4, 2, 8
NSEQ = NX * NY * NC
TOK = 256
CH = 1024
LANE = 128
SUB = CH // LANE
NS = 16
RANK = 512
PROJ = RANK + 2 * NS
HD = 128
TAPS = 4
REACH = 16
BIG_STEP = 1.0e7
MASKED = -1.0e30
GROUP = 8
RUN = TOK // NSEQ
BK = 512
VLIM = 60 * 1024 * 1024


def whole(space=VM):
    return pl.BlockSpec(memory_space=space)


def place():
    return (
        lax.axis_index("seq_0"),
        lax.axis_index("seq_1"),
        lax.axis_index("seq_2"),
        lax.axis_index("mp"),
    )


def seq_device(j, z):
    return (j // (NY * NC), (j // NC) % NY, j % NC, z)


def doc_starts(len_ref):
    s1 = len_ref[0]
    s2 = s1 + len_ref[1]
    return s1, s2, s2 + len_ref[2]


def start_of(pos, starts):
    s1, s2, s3 = starts
    return jnp.where(pos >= s3, s3, jnp.where(pos >= s2, s2, jnp.where(pos >= s1, s1, 0)))


def silu(x):
    return x / (1.0 + jnp.exp(-x))


def gather_kernel(
    inv_ref,
    len_ref,
    q_ref,
    k_ref,
    v_ref,
    x_ref,
    cw_ref,
    cb_ref,
    xw_ref,
    q_out,
    kv_out,
    proj_out,
    inner_out,
    kvs,
    qs,
    halo,
    ext,
    part,
    rs,
    own,
    loc_sem,
    halo_sem,
    kv_send,
    kv_recv,
    q_send,
    q_recv,
    rs_send,
    rs_recv,
    ag_send,
    ag_recv,
):
    x, y, c, z = place()
    me = (x * NY + y) * NC + c
    barrier = pltpu.get_barrier_semaphore()
    for k in range(1, NSEQ):
        pl.semaphore_signal(
            barrier, inc=1, device_id=seq_device((me + k) % NSEQ, z), device_id_type=MESH
        )
    for k in range(1, NZ):
        pl.semaphore_signal(
            barrier, inc=1, device_id=(x, y, c, (z + k) % NZ), device_id_type=MESH
        )
    load_k = pltpu.make_async_copy(k_ref, kvs.at[:, pl.ds(0, HD)], loc_sem.at[0])
    load_k.start()
    for half in range(TOK // HD):
        kvs[pl.ds(half * HD, HD), pl.ds(HD, HD)] = v_ref[pl.ds(half * HD, HD), :].T
    for j in range(NSEQ):
        qs[j] = q_ref[inv_ref[j]]
    load_k.wait()
    pl.semaphore_wait(barrier, NSEQ - 1 + NZ - 1)

    def remote(src, dst, send, recv, device):
        return pltpu.make_async_remote_copy(
            src_ref=src,
            dst_ref=dst,
            send_sem=send,
            recv_sem=recv,
            device_id=device,
            device_id_type=MESH,
        )

    def offset(a, b, core):
        return (x + a * (1 - core) + b * core) % NX, (y + a * core + b * (1 - core)) % NY

    def rows_of(a, b, core):
        px, py = offset(a, b, core)
        return pl.ds(pl.multiple_of(((px * NY + py) * NC + core) * TOK, TOK), TOK)

    partner = (x, y, 1 - c, z)
    after = (me + 1) % NSEQ
    halo_copy = remote(
        x_ref.at[pl.ds(TOK - 16, 16)], halo, halo_sem.at[0], halo_sem.at[1], seq_device(after, z)
    )
    halo_copy.start()
    mine = kv_out.at[rows_of(0, 0, c)]
    sends = []
    for a in range(1, NX):
        px, py = offset(a, 0, c)
        copy = remote(kvs, mine, kv_send.at[a], kv_recv.at[a], (px, py, c, z))
        copy.start()
        sends.append(copy)
    copy = remote(kvs, mine, kv_send.at[16], kv_recv.at[16], partner)
    copy.start()
    sends.append(copy)
    keep_kv = pltpu.make_async_copy(kvs, mine, loc_sem.at[0])
    keep_kv.start()
    q_rows = pl.ds(pl.multiple_of(me * RUN, RUN), RUN)
    for k in range(1, NSEQ):
        j = (me + k) % NSEQ
        copy = remote(qs.at[j], q_out.at[q_rows], q_send.at[k], q_recv.at[k], seq_device(j, z))
        copy.start()
        sends.append(copy)
    keep_q = pltpu.make_async_copy(qs.at[me], q_out.at[q_rows], loc_sem.at[1])
    keep_q.start()

    halo_copy.wait()
    ext[pl.ds(0, 8), :] = halo[pl.ds(8, 8), :].astype(F32)
    starts = doc_starts(len_ref)
    token = me * TOK + lax.broadcasted_iota(jnp.int32, (TOK, LANE), 0)
    depth = token - start_of(token, starts)

    def conv_columns(i, carry):
        cols = pl.ds(pl.multiple_of(i * LANE, LANE), LANE)
        ext[pl.ds(8, TOK), cols] = x_ref[:, cols].astype(F32)
        total = cb_ref[:, cols] + cw_ref[pl.ds(0, 1), cols] * ext[pl.ds(8, TOK), cols]
        for lag in range(1, TAPS):
            window = ext[pl.ds(8 - lag, TOK), cols]
            total = total + cw_ref[pl.ds(lag, 1), cols] * jnp.where(depth >= lag, window, 0.0)
        inner_out[:, cols] = silu(total).astype(BF16)
        return carry

    lax.fori_loop(0, SUB, conv_columns, 0)

    partial = jnp.dot(inner_out[...], xw_ref[...], preferred_element_type=F32).astype(BF16)
    part[...] = partial.reshape(NZ, TOK // NZ, PROJ)
    for k in range(1, NZ):
        j = (z + k) % NZ
        copy = remote(part.at[j], rs.at[k], rs_send.at[k], rs_recv.at[k], (x, y, c, j))
        copy.start()
        sends.append(copy)

    def wait_kv(slot_rows, index):
        remote(kvs, kv_out.at[slot_rows], kv_send.at[0], kv_recv.at[index], partner).wait_recv()

    for a in range(NX):
        if a > 0:
            wait_kv(rows_of(-a, 0, c), a)
        block = kv_out.at[rows_of(-a, 0, c)] if a > 0 else kvs
        target = kv_out.at[rows_of(-a, 0, c)]
        for b in range(1, NY):
            px, py = offset(0, b, c)
            index = b * NX + a
            copy = remote(block, target, kv_send.at[index], kv_recv.at[index], (px, py, c, z))
            copy.start()
            sends.append(copy)
        if a > 0:
            copy = remote(block, target, kv_send.at[16 + a], kv_recv.at[16 + a], partner)
            copy.start()
            sends.append(copy)

    total = part[z].astype(F32)
    for k in range(1, NZ):
        remote(part.at[0], rs.at[k], rs_send.at[k], rs_recv.at[k], partner).wait_recv()
        total = total + rs[k].astype(F32)
    own[...] = total.astype(BF16)
    slice_rows = TOK // NZ
    own_rows = pl.ds(pl.multiple_of(z * slice_rows, slice_rows), slice_rows)
    for k in range(1, NZ):
        copy = remote(
            own, proj_out.at[own_rows], ag_send.at[k], ag_recv.at[k], (x, y, c, (z + k) % NZ)
        )
        copy.start()
        sends.append(copy)
    proj_out[own_rows, :] = own[...]

    for b in range(1, NY):
        for a in range(NX):
            index = b * NX + a
            wait_kv(rows_of(-a, -b, c), index)
            block = kv_out.at[rows_of(-a, -b, c)]
            copy = remote(block, block, kv_send.at[16 + index], kv_recv.at[16 + index], partner)
            copy.start()
            sends.append(copy)
    for k in range(1, NZ):
        rows = pl.ds(pl.multiple_of(((z + NZ - k) % NZ) * slice_rows, slice_rows), slice_rows)
        remote(own, proj_out.at[rows], ag_send.at[k], ag_recv.at[k], partner).wait_recv()
    for k in range(1, NSEQ):
        rows = pl.ds(pl.multiple_of(((me + NSEQ - k) % NSEQ) * RUN, RUN), RUN)
        remote(qs.at[0], q_out.at[rows], q_send.at[k], q_recv.at[k], partner).wait_recv()
    for b in range(NY):
        for a in range(NX):
            wait_kv(rows_of(-a, -b, 1 - c), 16 + b * NX + a)
    for copy in sends:
        copy.wait_send()
    keep_kv.wait()
    keep_q.wait()


def gather_all(inverse, lengths, q, k, v, x, cw, cb, xw):
    dma = pltpu.SemaphoreType.DMA
    return pl.pallas_call(
        gather_kernel,
        out_shape=(
            jax.ShapeDtypeStruct((TOK, CH), BF16),
            jax.ShapeDtypeStruct((NSEQ * TOK, 2 * HD), BF16),
            jax.ShapeDtypeStruct((TOK, PROJ), BF16),
            jax.ShapeDtypeStruct((TOK, CH), BF16),
        ),
        in_specs=[whole(pltpu.SMEM)] * 2 + [whole(), whole(pl.ANY)] + [whole()] * 5,
        out_specs=(whole(pl.ANY), whole(pl.ANY), whole(), whole()),
        scratch_shapes=[
            VM((TOK, 2 * HD), BF16),
            VM((NSEQ, RUN, CH), BF16),
            VM((16, CH), BF16),
            VM((TOK + 8, CH), F32),
            VM((NZ, TOK // NZ, PROJ), BF16),
            VM((NZ, TOK // NZ, PROJ), BF16),
            VM((TOK // NZ, PROJ), BF16),
            dma((2,)),
            dma((2,)),
            dma((32,)),
            dma((32,)),
            dma((NSEQ,)),
            dma((NSEQ,)),
            dma((NZ,)),
            dma((NZ,)),
            dma((NZ,)),
            dma((NZ,)),
        ],
        compiler_params=pltpu.CompilerParams(
            collective_id=0, has_side_effects=True, vmem_limit_bytes=VLIM
        ),
        name="gather",
    )(inverse, lengths, q, k, v, x, cw, cb, xw)


def spread_columns(proj_ref, first, count):
    row = lax.broadcasted_iota(jnp.int32, (count, count * LANE), 0)
    col = lax.broadcasted_iota(jnp.int32, (count, count * LANE), 1)
    pick = jnp.where(col // LANE == row, 1.0, 0.0).astype(BF16)
    return jnp.dot(proj_ref[:, pl.ds(first, count)], pick, preferred_element_type=F32)


def local_scan_kernel(
    len_ref, me_ref, proj_ref, inner_ref, dtw_ref, dtb_ref, rate_ref, st_out, step_out, drive_out,
    rate_out, bcs, sums,
):
    starts = doc_starts(len_ref)
    token = me_ref[0] * TOK + lax.broadcasted_iota(jnp.int32, (TOK, LANE), 0)
    begins = token == start_of(token, starts)
    for j in range(SUB):
        cols = pl.ds(j * LANE, LANE)
        raw = jnp.dot(proj_ref[:, pl.ds(0, RANK)], dtw_ref[:, cols], preferred_element_type=F32)
        step = jax.nn.softplus(raw + dtb_ref[:, cols])
        drive = step * inner_ref[:, cols].astype(F32)
        step = jnp.where(begins, BIG_STEP, step)
        sums[pl.ds(j, 1), :] = jnp.sum(step, axis=0, keepdims=True)
        step_out[pl.ds(j, TOK, stride=SUB), :] = step
        drive_out[pl.ds(j, TOK, stride=SUB), :] = drive
        rate_out[pl.ds(j, NS, stride=SUB), :] = rate_ref[:, cols] * (-LOG2E)
    spread = spread_columns(proj_ref, RANK, NS)
    for n in range(NS):
        bcs[pl.ds(n * TOK, TOK), :] = spread[:, n * LANE : (n + 1) * LANE]
    rates = [rate_out[pl.ds(n * SUB, SUB), :] for n in range(NS)]

    def advance(t, carried):
        rows = pl.ds(pl.multiple_of(t * SUB, SUB), SUB)
        step = step_out[rows, :]
        drive = drive_out[rows, :]
        result = []
        for n in range(NS):
            b = bcs[pl.ds(n * TOK + t, SUB, stride=0), :]
            result.append(jnp.exp2(step * rates[n]) * carried[n] + b * drive)
        return tuple(result)

    zero = jnp.zeros((SUB, LANE), F32)
    state = lax.fori_loop(0, TOK, advance, (zero,) * NS, unroll=4)
    for n in range(0, NS, 2):
        pair = jnp.concatenate([state[n], state[n + 1]], axis=0)
        st_out[pl.ds(n * SUB, 2 * SUB), :] = pair.astype(BF16)
    total = sums[...]
    high = total.astype(BF16)
    low = total - high.astype(F32)
    st_out[pl.ds(NS * SUB, 2 * SUB), :] = jnp.concatenate([high.astype(F32), low], axis=0).astype(BF16)


def local_scan(lengths, me, proj, inner, dtw, dtb, rate):
    return pl.pallas_call(
        local_scan_kernel,
        out_shape=(
            jax.ShapeDtypeStruct(((NS + 2) * SUB, LANE), BF16),
            jax.ShapeDtypeStruct((TOK * SUB, LANE), F32),
            jax.ShapeDtypeStruct((TOK * SUB, LANE), F32),
            jax.ShapeDtypeStruct((NS * SUB, LANE), F32),
        ),
        in_specs=[whole(pltpu.SMEM)] * 2 + [whole()] * 5,
        out_specs=(whole(),) * 4,
        scratch_shapes=[VM((NS * TOK, LANE), F32), VM((SUB, LANE), F32)],
        compiler_params=pltpu.CompilerParams(vmem_limit_bytes=VLIM),
        name="local_scan",
    )(lengths, me, proj, inner, dtw, dtb, rate)


def enter_kernel(st_ref, rate_ref, in_out, slots, send_sem, recv_sem):
    x, y, c, z = place()
    me = (x * NY + y) * NC + c
    barrier = pltpu.get_barrier_semaphore()
    for k in range(1, REACH + 1):
        pl.semaphore_signal(
            barrier, inc=1, device_id=seq_device((me + NSEQ - k) % NSEQ, z), device_id_type=MESH
        )
    pl.semaphore_wait(barrier, REACH)
    copies = []
    for k in range(1, REACH + 1):
        copy = pltpu.make_async_remote_copy(
            src_ref=st_ref,
            dst_ref=slots.at[k - 1],
            send_sem=send_sem.at[k - 1],
            recv_sem=recv_sem.at[k - 1],
            device_id=seq_device((me + k) % NSEQ, z),
            device_id_type=MESH,
        )
        copy.start()
        copies.append(copy)
    total = jnp.zeros((NS, SUB, LANE), F32)
    rate = rate_ref[...].reshape(NS, SUB, LANE)
    for k in range(REACH, 0, -1):
        copies[k - 1].wait_recv()
        block = slots[k - 1].astype(F32).reshape(NS + 2, SUB, LANE)
        steps = block[NS] + block[NS + 1]
        moved = jnp.exp2(rate * steps[None]) * total + block[:NS]
        total = jnp.where(me >= k, moved, 0.0)
    in_out[...] = total.reshape(NS * SUB, LANE)
    for copy in copies:
        copy.wait_send()


def enter(st, rate):
    dma = pltpu.SemaphoreType.DMA
    return pl.pallas_call(
        enter_kernel,
        out_shape=jax.ShapeDtypeStruct((NS * SUB, LANE), F32),
        in_specs=[whole()] * 2,
        out_specs=whole(),
        scratch_shapes=[VM((REACH, (NS + 2) * SUB, LANE), BF16), dma((REACH,)), dma((REACH,))],
        compiler_params=pltpu.CompilerParams(
            collective_id=1, has_side_effects=True, vmem_limit_bytes=VLIM
        ),
        name="enter",
    )(st, rate)


def output_kernel(
    in_ref, step_ref, drive_ref, rate_ref, proj_ref, inner_ref, z_ref, skip_ref, out, bcs, ys
):
    spread = spread_columns(proj_ref, RANK, 2 * NS)
    for n in range(2 * NS):
        bcs[pl.ds(n * TOK, TOK), :] = spread[:, n * LANE : (n + 1) * LANE]
    rates = [rate_ref[pl.ds(n * SUB, SUB), :] for n in range(NS)]

    def advance(t, carried):
        rows = pl.ds(pl.multiple_of(t * SUB, SUB), SUB)
        step = step_ref[rows, :]
        drive = drive_ref[rows, :]
        result = []
        total = None
        for n in range(NS):
            b = bcs[pl.ds(n * TOK + t, SUB, stride=0), :]
            weight = bcs[pl.ds((NS + n) * TOK + t, SUB, stride=0), :]
            state = jnp.exp2(step * rates[n]) * carried[n] + b * drive
            result.append(state)
            total = weight * state if total is None else total + weight * state
        ys[rows, :] = total
        return tuple(result)

    first = tuple(in_ref[pl.ds(n * SUB, SUB), :] for n in range(NS))
    lax.fori_loop(0, TOK, advance, first, unroll=4)
    for j in range(SUB):
        cols = pl.ds(j * LANE, LANE)
        scanned = ys[pl.ds(j, TOK, stride=SUB), :] + skip_ref[:, cols] * inner_ref[:, cols].astype(F32)
        out[:, cols] = (scanned * silu(z_ref[:, cols].astype(F32))).astype(BF16)


def scan_output(h_in, step, drive, rate, proj, inner, z, skip):
    return pl.pallas_call(
        output_kernel,
        out_shape=jax.ShapeDtypeStruct((TOK, CH), BF16),
        in_specs=[whole()] * 8,
        out_specs=whole(),
        scratch_shapes=[VM((2 * NS * TOK, LANE), F32), VM((TOK * SUB, LANE), F32)],
        compiler_params=pltpu.CompilerParams(vmem_limit_bytes=VLIM),
        name="scan_output",
    )(h_in, step, drive, rate, proj, inner, z, skip)


def attend_kernel(pos_ref, len_ref, q_ref, kv_ref, out, scores_a, scores_b):
    g = pl.program_id(0)
    heads = CH // HD
    rows = GROUP * RUN
    count = heads * rows
    wide = 2 * BK
    per = TOK * GROUP // wide
    starts = doc_starts(len_ref)
    bases = [pos_ref[g * GROUP + i] for i in range(GROUP)]
    lane = lax.broadcasted_iota(jnp.int32, (1, LANE), 1) % rows
    base = bases[0]
    for i in range(1, GROUP):
        base = jnp.where(lane >= i * RUN, bases[i], base)
    pos = base + lane % RUN
    start = start_of(pos, starts)
    top = g * per
    first = jnp.minimum(start_of(bases[0], starts) // wide, top)
    last_start = start_of(bases[GROUP - 1] + RUN - 1, starts)
    plain = jnp.maximum(jnp.minimum((last_start + wide - 1) // wide, top), first)
    q = jnp.concatenate([q_ref[:, h * HD : (h + 1) * HD] for h in range(heads)], axis=0)
    scale = HD**-0.5 * LOG2E
    key_row = lax.broadcasted_iota(jnp.int32, (BK, LANE), 0)
    ones = jnp.ones((16, BK), BF16)

    def score(into, i):
        keys = kv_ref[pl.ds(pl.multiple_of(i * BK, BK), BK), pl.ds(0, HD)]
        into[...] = lax.dot_general(
            keys, q, (((1,), (1,)), ((), ())), preferred_element_type=F32
        )

    def absorb(taken, i, carried, masked):
        begin = pl.multiple_of(i * BK, BK)
        best, summed = carried
        scores = taken[...]
        if masked:
            visible = (key_row <= pos - begin) & (key_row >= start - begin)
            scores = jnp.concatenate(
                [
                    jnp.where(visible, scores[:, j : j + LANE], MASKED)
                    for j in range(0, count, LANE)
                ],
                axis=1,
            )
        new_best = jnp.maximum(best, jnp.max(scores, axis=0, keepdims=True) * scale)
        weights = jnp.exp2(scores * scale - new_best).astype(BF16)
        rescale = jnp.exp2(best - new_best)
        values = jnp.concatenate(
            [kv_ref[pl.ds(begin + j, HD), pl.ds(HD, HD)] for j in range(0, BK, HD)], axis=1
        )
        values = jnp.concatenate([values, ones], axis=0)
        product = jnp.dot(values, weights, preferred_element_type=F32)
        return new_best, summed * rescale + product

    def pair(i, carried, masked, more=True):
        score(scores_b, 2 * i + 1)
        carried = absorb(scores_a, 2 * i, carried, masked)
        if more:
            score(scores_a, 2 * i + 2)
        return absorb(scores_b, 2 * i + 1, carried, masked)

    carried = (jnp.full((1, count), MASKED * scale, F32), jnp.zeros((HD + 16, count), F32))
    score(scores_a, 2 * first)
    carried = lax.fori_loop(first, plain, lambda i, v: pair(i, v, True), carried)
    carried = lax.fori_loop(plain, top, lambda i, v: pair(i, v, False), carried)
    for i in range(per):
        carried = pair(top + i, carried, True, i < per - 1)
    summed = carried[1]
    result = (summed[:HD] / summed[HD : HD + 1]).T.astype(BF16)
    for h in range(heads):
        out[:, h * HD : (h + 1) * HD] = result[h * rows : (h + 1) * rows]


def attend(positions, lengths, q, kv):
    rows = GROUP * RUN
    return pl.pallas_call(
        attend_kernel,
        out_shape=jax.ShapeDtypeStruct((TOK, CH), BF16),
        grid=(NSEQ // GROUP,),
        in_specs=[
            whole(pltpu.SMEM),
            whole(pltpu.SMEM),
            pl.BlockSpec((rows, CH), lambda g: (g, 0)),
            whole(),
        ],
        out_specs=pl.BlockSpec((rows, CH), lambda g: (g, 0)),
        scratch_shapes=[VM((BK, CH // HD * rows), F32)] * 2,
        compiler_params=pltpu.CompilerParams(vmem_limit_bytes=VLIM),
        name="attend",
    )(positions, lengths, q, kv)


def local(
    x_branch,
    z_branch,
    conv_weight,
    conv_bias,
    xproj_weight,
    dt_weight,
    dt_bias,
    decay_rate,
    skip_gain,
    query_rows,
    key_rows,
    value_rows,
    lengths,
    destination,
):
    me = lax.axis_index(SEQ)
    targets = destination.reshape(NSEQ, NSEQ, RUN)[:, :, 0] // TOK
    runs = jnp.arange(NSEQ, dtype=jnp.int32)
    own = lax.dynamic_slice_in_dim(targets, me, 1, 0)
    inverse = jnp.sum(jnp.where(own == runs[:, None], runs[None, :], 0), axis=1)
    positions = runs * TOK + RUN * jnp.sum(jnp.where(targets == me, runs[None, :], 0), axis=1)
    q, kv, proj, inner = gather_all(
        inverse,
        lengths,
        query_rows.reshape(NSEQ, RUN, CH),
        key_rows,
        value_rows,
        x_branch,
        conv_weight,
        conv_bias.reshape(1, CH),
        xproj_weight,
    )
    st, step, drive, rate = local_scan(
        lengths,
        me.reshape(1).astype(jnp.int32),
        proj,
        inner,
        dt_weight,
        dt_bias.reshape(1, CH),
        decay_rate,
    )
    h_in = enter(st, rate)
    mamba_out = scan_output(
        h_in, step, drive, rate, proj, inner, z_branch, skip_gain.reshape(1, CH)
    )
    regrouped = attend(positions, lengths, q, kv)
    return (mamba_out, regrouped)


def solution(mesh):
    torus = Mesh(mesh.devices.reshape(NX, NY, NC, mesh.shape["mp"]), (*SEQ, "mp"))
    in_specs = (
        P(SEQ, "mp"),
        P(SEQ, "mp"),
        P(None, "mp"),
        P("mp"),
        P("mp", None),
        P(None, "mp"),
        P("mp"),
        P(None, "mp"),
        P("mp"),
        P(SEQ, "mp"),
        P(SEQ, "mp"),
        P(SEQ, "mp"),
        P(),
        P(),
    )
    out_specs = (P(SEQ, "mp"), P(SEQ, "mp"))
    return jax.shard_map(local, mesh=torus, in_specs=in_specs, out_specs=out_specs, check_vma=False)
```

```python
import math

import jax
import jax.numpy as jnp
from jax import lax
from jax.experimental import pallas as pl
from jax.experimental.pallas import tpu as pltpu
from jax.sharding import Mesh
from jax.sharding import PartitionSpec as P

SEQ = ("seq_0", "seq_1", "seq_2")
MESH = pl.DeviceIdType.MESH
VM = pltpu.VMEM
F32 = jnp.float32
BF16 = jnp.bfloat16
LOG2E = math.log2(math.e)
NX, NY, NC, NZ = 4, 4, 2, 8
NSEQ = NX * NY * NC
TOK = 256
CH = 1024
LANE = 128
SUB = CH // LANE
NS = 16
RANK = 512
PROJ = RANK + 2 * NS
HD = 128
TAPS = 4
BIG_STEP = 1.0e7
MASKED = -1.0e30
GROUP = 8
RUN = TOK // NSEQ
BK = 512
VLIM = 60 * 1024 * 1024


def whole(space=VM):
    return pl.BlockSpec(memory_space=space)


def place():
    return (
        lax.axis_index("seq_0"),
        lax.axis_index("seq_1"),
        lax.axis_index("seq_2"),
        lax.axis_index("mp"),
    )


def seq_device(j, z):
    return (j // (NY * NC), (j // NC) % NY, j % NC, z)


def doc_starts(len_ref):
    s1 = len_ref[0]
    s2 = s1 + len_ref[1]
    return s1, s2, s2 + len_ref[2]


def start_of(pos, starts):
    s1, s2, s3 = starts
    return jnp.where(pos >= s3, s3, jnp.where(pos >= s2, s2, jnp.where(pos >= s1, s1, 0)))


def silu(x):
    return x / (1.0 + jnp.exp(-x))


def mixer_kernel(
    dest_ref,
    len_ref,
    q_ref,
    k_ref,
    v_ref,
    x_ref,
    z_ref,
    cw_ref,
    cb_ref,
    xw_ref,
    dtw_ref,
    dtb_ref,
    rate_ref,
    skip_ref,
    q_out,
    kv_out,
    pos_out,
    out,
    kvs,
    qs,
    halo,
    ext,
    inner,
    part,
    rs_plus,
    rs_minus,
    go_plus,
    go_minus,
    proj,
    steps,
    drives,
    rates,
    spread,
    gains,
    ys,
    sums,
    st_own,
    st_pair,
    st_y,
    st_x,
    loc_sem,
    halo_sem,
    kv_send,
    kv_recv,
    q_send,
    q_recv,
    rs_send,
    rs_recv,
    ag_send,
    ag_recv,
    st_send,
    st_recv,
):
    x, y, c, z = place()
    me = (x * NY + y) * NC + c
    anchor = me * TOK
    barrier = pltpu.get_barrier_semaphore()
    for k in range(1, NSEQ):
        pl.semaphore_signal(
            barrier, inc=1, device_id=seq_device((me + k) % NSEQ, z), device_id_type=MESH
        )
    for k in range(1, NZ):
        pl.semaphore_signal(
            barrier, inc=1, device_id=(x, y, c, (z + k) % NZ), device_id_type=MESH
        )
    load_k = pltpu.make_async_copy(k_ref, kvs.at[:, pl.ds(0, HD)], loc_sem.at[0])
    load_k.start()
    for half in range(TOK // HD):
        kvs[pl.ds(half * HD, HD), pl.ds(HD, HD)] = v_ref[pl.ds(half * HD, HD), :].T

    def stage(j, carry):
        run = 0
        for r in range(NSEQ):
            run = jnp.where(dest_ref[anchor + r * RUN] // TOK == j, r, run)
        qs[j] = q_ref[run]
        return carry

    lax.fori_loop(0, NSEQ, stage, 0)

    starts = doc_starts(len_ref)
    token = anchor + lax.broadcasted_iota(jnp.int32, (TOK, LANE), 0)
    depth = token - start_of(token, starts)

    def convolve(count, cols, far):
        total = cb_ref[:, cols] + cw_ref[pl.ds(0, 1), cols] * ext[pl.ds(8, count), cols]
        for lag in range(1, TAPS):
            window = ext[pl.ds(8 - lag, count), cols]
            total = total + cw_ref[pl.ds(lag, 1), cols] * jnp.where(far >= lag, window, 0.0)
        inner[pl.ds(0, count), cols] = silu(total).astype(BF16)

    def conv_columns(i, carry):
        cols = pl.ds(pl.multiple_of(i * LANE, LANE), LANE)
        ext[pl.ds(0, 8), cols] = jnp.zeros((8, LANE), F32)
        ext[pl.ds(8, TOK), cols] = x_ref[:, cols].astype(F32)
        convolve(TOK, cols, depth)
        return carry

    lax.fori_loop(0, SUB, conv_columns, 0)
    load_k.wait()
    pl.semaphore_wait(barrier, NSEQ - 1 + NZ - 1)

    def remote(src, dst, send, recv, device):
        return pltpu.make_async_remote_copy(
            src_ref=src,
            dst_ref=dst,
            send_sem=send,
            recv_sem=recv,
            device_id=device,
            device_id_type=MESH,
        )

    def offset(a, b, core):
        return (x + a * (1 - core) + b * core) % NX, (y + a * core + b * (1 - core)) % NY

    def rows_of(a, b, core):
        px, py = offset(a, b, core)
        return pl.ds(pl.multiple_of(((px * NY + py) * NC + core) * TOK, TOK), TOK)

    partner = (x, y, 1 - c, z)
    after = (me + 1) % NSEQ
    halo_copy = remote(
        x_ref.at[pl.ds(TOK - 16, 16)], halo, halo_sem.at[0], halo_sem.at[1], seq_device(after, z)
    )
    halo_copy.start()
    mine = kv_out.at[rows_of(0, 0, c)]
    sends = []
    for a in range(1, NX):
        px, py = offset(a, 0, c)
        copy = remote(kvs, mine, kv_send.at[a], kv_recv.at[a], (px, py, c, z))
        copy.start()
        sends.append(copy)
    copy = remote(kvs, mine, kv_send.at[16], kv_recv.at[16], partner)
    copy.start()
    sends.append(copy)
    keep_kv = pltpu.make_async_copy(kvs, mine, loc_sem.at[0])
    keep_kv.start()
    q_rows = pl.ds(pl.multiple_of(me * RUN, RUN), RUN)
    for k in range(1, NSEQ):
        j = (me + k) % NSEQ
        copy = remote(qs.at[j], q_out.at[q_rows], q_send.at[k], q_recv.at[k], seq_device(j, z))
        copy.start()
        sends.append(copy)
    keep_q = pltpu.make_async_copy(qs.at[me], q_out.at[q_rows], loc_sem.at[1])
    keep_q.start()

    halo_copy.wait()
    ext[pl.ds(0, 8), :] = halo[pl.ds(8, 8), :].astype(F32)
    near = anchor + lax.broadcasted_iota(jnp.int32, (16, CH), 0)
    convolve(16, pl.ds(0, CH), near - start_of(near, starts))

    partial = lax.dot_general(
        inner[...], xw_ref[...], (((1,), (1,)), ((), ())), preferred_element_type=F32
    ).astype(BF16)
    slice_rows = TOK // NZ
    part[...] = partial.reshape(NZ, slice_rows, PROJ)
    up = (x, y, c, (z + 1) % NZ)
    down = (x, y, c, (z + NZ - 1) % NZ)

    def ring_plus(s):
        src = part.at[(z + 4) % NZ] if s == 1 else go_plus.at[s]
        return remote(src, rs_plus.at[s], rs_send.at[s], rs_recv.at[s], up)

    def ring_minus(s):
        src = part.at[(z + 5) % NZ] if s == 1 else go_minus.at[s]
        return remote(src, rs_minus.at[s], rs_send.at[4 + s], rs_recv.at[4 + s], down)

    plus, minus = ring_plus(1), ring_minus(1)
    plus.start()
    minus.start()
    sends += [plus, minus]

    def wait_kv(slot_rows, index):
        remote(kvs, kv_out.at[slot_rows], kv_send.at[0], kv_recv.at[index], partner).wait_recv()

    for s in range(1, 4):
        plus.wait_recv()
        go_plus[s + 1] = (rs_plus[s].astype(F32) + part[(z + 4 - s) % NZ].astype(F32)).astype(BF16)
        plus = ring_plus(s + 1)
        plus.start()
        sends.append(plus)
        minus.wait_recv()
        if s < 3:
            go_minus[s + 1] = (
                rs_minus[s].astype(F32) + part[(z + 5 + s) % NZ].astype(F32)
            ).astype(BF16)
            minus = ring_minus(s + 1)
            minus.start()
            sends.append(minus)
        if s == 1:
            for a in range(NX):
                if a > 0:
                    wait_kv(rows_of(-a, 0, c), a)
                block = kv_out.at[rows_of(-a, 0, c)] if a > 0 else kvs
                target = kv_out.at[rows_of(-a, 0, c)]
                for b in range(1, NY):
                    px, py = offset(0, b, c)
                    index = b * NX + a
                    copy = remote(
                        block, target, kv_send.at[index], kv_recv.at[index], (px, py, c, z)
                    )
                    copy.start()
                    sends.append(copy)
                if a > 0:
                    copy = remote(
                        block, target, kv_send.at[16 + a], kv_recv.at[16 + a], partner
                    )
                    copy.start()
                    sends.append(copy)
    plus.wait_recv()
    total = part[z].astype(F32) + rs_plus[4].astype(F32) + rs_minus[3].astype(F32)

    def proj_rows(chunk):
        return pl.ds(pl.multiple_of((chunk % NZ) * slice_rows, slice_rows), slice_rows)

    proj[proj_rows(z), :] = total.astype(BF16)

    def pass_plus(s):
        rows = proj.at[proj_rows(z + NZ + 1 - s)]
        return remote(rows, rows, ag_send.at[s], ag_recv.at[s], up)

    def pass_minus(s):
        rows = proj.at[proj_rows(z + s - 1)]
        return remote(rows, rows, ag_send.at[4 + s], ag_recv.at[4 + s], down)

    def got_plus(s):
        rows = proj.at[proj_rows(z + NZ - s)]
        remote(rows, rows, ag_send.at[s], ag_recv.at[s], up).wait_recv()

    def got_minus(s):
        rows = proj.at[proj_rows(z + s)]
        remote(rows, rows, ag_send.at[4 + s], ag_recv.at[4 + s], down).wait_recv()

    for s in range(1, 5):
        if s > 1:
            got_plus(s - 1)
        copy = pass_plus(s)
        copy.start()
        sends.append(copy)
        if s < 4:
            if s > 1:
                got_minus(s - 1)
            copy = pass_minus(s)
            copy.start()
            sends.append(copy)
    for j in range(SUB):
        cols = pl.ds(j * LANE, LANE)
        rates[pl.ds(j, NS, stride=SUB), :] = rate_ref[:, cols] * (-LOG2E)
    got_minus(3)
    got_plus(4)

    begins = depth == 0
    for j in range(SUB):
        cols = pl.ds(j * LANE, LANE)
        raw = jnp.dot(proj[:, pl.ds(0, RANK)], dtw_ref[:, cols], preferred_element_type=F32)
        step = jax.nn.softplus(raw + dtb_ref[:, cols])
        drives[pl.ds(j, TOK, stride=SUB), :] = step * inner[:, cols].astype(F32)
        step = jnp.where(begins, BIG_STEP, step)
        sums[pl.ds(j, 1), :] = jnp.sum(step, axis=0, keepdims=True)
        steps[pl.ds(j, TOK, stride=SUB), :] = step
    row = lax.broadcasted_iota(jnp.int32, (2 * NS, 2 * NS * LANE), 0)
    col = lax.broadcasted_iota(jnp.int32, (2 * NS, 2 * NS * LANE), 1)
    pick = jnp.where(col // LANE == row, 1.0, 0.0).astype(BF16)
    wide = jnp.dot(proj[:, pl.ds(RANK, 2 * NS)], pick, preferred_element_type=F32)
    for n in range(2 * NS):
        spread[pl.ds(n * TOK, TOK), :] = wide[:, n * LANE : (n + 1) * LANE]
    rate = [rates[pl.ds(n * SUB, SUB), :] for n in range(NS)]

    def advance(t, carried):
        rows = pl.ds(pl.multiple_of(t * SUB, SUB), SUB)
        step = steps[rows, :]
        drive = drives[rows, :]
        result = []
        for n in range(NS):
            b = spread[pl.ds(n * TOK + t, SUB, stride=0), :]
            result.append(jnp.exp2(step * rate[n]) * carried[n] + b * drive)
        return tuple(result)

    zero = jnp.zeros((SUB, LANE), F32)
    state = lax.fori_loop(0, TOK, advance, (zero,) * NS, unroll=4)

    def pack(into, states, total):
        for n in range(0, NS, 2):
            pair = jnp.concatenate([states[n], states[n + 1]], axis=0)
            into[pl.ds(n * SUB, 2 * SUB), :] = pair.astype(BF16)
        high = total.astype(BF16).astype(F32)
        pair = jnp.concatenate([high, total - high], axis=0)
        into[pl.ds(NS * SUB, 2 * SUB), :] = pair.astype(BF16)

    def unpack(taken):
        block = taken[...].astype(F32).reshape(NS + 2, SUB, LANE)
        return [block[n] for n in range(NS)], block[NS] + block[NS + 1]

    def follow(states, block, total, passed=None):
        result = []
        for n in range(NS):
            moved = jnp.exp2(rate[n] * total) * states[n] + block[n]
            result.append(moved if passed is None else jnp.where(passed, moved, states[n]))
        return result

    pack(st_own, state, sums[...])
    pair_copy = remote(st_own, st_pair, st_send.at[0], st_recv.at[0], partner)
    pair_copy.start()
    sends.append(pair_copy)

    def local_token(t, carried):
        so_far, states = carried
        rows = pl.ds(pl.multiple_of(t * SUB, SUB), SUB)
        step = steps[rows, :]
        drive = drives[rows, :]
        so_far = so_far + step
        result = []
        total = None
        for n in range(NS):
            r = rates[pl.ds(n * SUB, SUB), :]
            b = spread[pl.ds(n * TOK + t, SUB, stride=0), :]
            weight = spread[pl.ds((NS + n) * TOK + t, SUB, stride=0), :]
            new = jnp.exp2(step * r) * states[n] + b * drive
            result.append(new)
            total = weight * new if total is None else total + weight * new
            gains[t, pl.ds(n * SUB, SUB), :] = weight * jnp.exp2(so_far * r)
        ys[rows, :] = total
        return so_far, tuple(result)

    carried = (zero, (zero,) * NS)
    cuts = (0, 40, 144, TOK)
    carried = lax.fori_loop(cuts[0], cuts[1], local_token, carried, unroll=2)

    pair_copy.wait_recv()
    own_state, own_total = unpack(st_own)
    other_state, other_total = unpack(st_pair)
    first_core = c == 0
    early = [jnp.where(first_core, p, q) for p, q in zip(own_state, other_state)]
    late = [jnp.where(first_core, q, p) for p, q in zip(own_state, other_state)]
    late_total = jnp.where(first_core, other_total, own_total)
    chip_state = follow(early, late, late_total)
    pack(st_y.at[0], chip_state, own_total + other_total)
    level = []
    for k in range(1, NY):
        copy = remote(
            st_y.at[0], st_y.at[k], st_send.at[k], st_recv.at[k], (x, (y + k) % NY, c, z)
        )
        copy.start()
        level.append(copy)
    sends += level
    carried = lax.fori_loop(cuts[1], cuts[2], local_token, carried, unroll=2)

    for copy in level:
        copy.wait_recv()
    column, column_total = unpack(st_y.at[(y + NY) % NY])
    for j in range(1, NY):
        block, total = unpack(st_y.at[(y + NY - j) % NY])
        column = follow(column, block, total)
        column_total = column_total + total
    pack(st_x.at[0], column, column_total)
    level = []
    for k in range(1, NX):
        copy = remote(
            st_x.at[0], st_x.at[k], st_send.at[4 + k], st_recv.at[4 + k], ((x + k) % NX, y, c, z)
        )
        copy.start()
        level.append(copy)
    sends += level
    carried = lax.fori_loop(cuts[2], cuts[3], local_token, carried, unroll=2)

    for b in range(1, NY):
        for a in range(NX):
            index = b * NX + a
            wait_kv(rows_of(-a, -b, c), index)
            block = kv_out.at[rows_of(-a, -b, c)]
            copy = remote(block, block, kv_send.at[16 + index], kv_recv.at[16 + index], partner)
            copy.start()
            sends.append(copy)

    for copy in level:
        copy.wait_recv()
    entering = [zero] * NS
    for j in range(NX - 1):
        block, total = unpack(st_x.at[(x + NX - j) % NX])
        entering = follow(entering, block, total, x > j)
    for j in range(NY - 1):
        block, total = unpack(st_y.at[(y + NY - j) % NY])
        entering = follow(entering, block, total, y > j)
    entering = follow(entering, early, jnp.where(first_core, own_total, other_total), c > 0)

    def correct(t, carry):
        rows = pl.ds(pl.multiple_of(t * SUB, SUB), SUB)
        total = ys[rows, :]
        for n in range(NS):
            total = total + gains[t, pl.ds(n * SUB, SUB), :] * entering[n]
        ys[rows, :] = total
        return carry

    lax.fori_loop(0, TOK, correct, 0, unroll=4)
    for j in range(SUB):
        cols = pl.ds(j * LANE, LANE)
        scanned = ys[pl.ds(j, TOK, stride=SUB), :]
        scanned = scanned + skip_ref[:, cols] * inner[:, cols].astype(F32)
        out[:, cols] = (scanned * silu(z_ref[:, cols].astype(F32))).astype(BF16)

    def locate(i, carry):
        run = 0
        for r in range(NSEQ):
            run = jnp.where(dest_ref[i * TOK + r * RUN] // TOK == me, r, run)
        pos_out[i] = i * TOK + run * RUN
        return carry

    lax.fori_loop(0, NSEQ, locate, 0)
    for k in range(1, NSEQ):
        rows = pl.ds(pl.multiple_of(((me + NSEQ - k) % NSEQ) * RUN, RUN), RUN)
        remote(qs.at[0], q_out.at[rows], q_send.at[k], q_recv.at[k], partner).wait_recv()
    for b in range(NY):
        for a in range(NX):
            wait_kv(rows_of(-a, -b, 1 - c), 16 + b * NX + a)
    for copy in sends:
        copy.wait_send()
    keep_kv.wait()
    keep_q.wait()


def mix(dest, lengths, q, k, v, x, z, cw, cb, xw, dtw, dtb, rate, skip):
    dma = pltpu.SemaphoreType.DMA
    states = ((NS + 2) * SUB, LANE)
    chunk = (TOK // NZ, PROJ)
    return pl.pallas_call(
        mixer_kernel,
        out_shape=(
            jax.ShapeDtypeStruct((TOK, CH), BF16),
            jax.ShapeDtypeStruct((NSEQ * TOK, 2 * HD), BF16),
            jax.ShapeDtypeStruct((NSEQ,), jnp.int32),
            jax.ShapeDtypeStruct((TOK, CH), BF16),
        ),
        in_specs=[whole(pltpu.SMEM)] * 2 + [whole(), whole(pl.ANY)] + [whole()] * 10,
        out_specs=(whole(pl.ANY), whole(pl.ANY), whole(pltpu.SMEM), whole()),
        scratch_shapes=[
            VM((TOK, 2 * HD), BF16),
            VM((NSEQ, RUN, CH), BF16),
            VM((16, CH), BF16),
            VM((TOK + 8, CH), F32),
            VM((TOK, CH), BF16),
            VM((NZ, *chunk), BF16),
            VM((5, *chunk), BF16),
            VM((4, *chunk), BF16),
            VM((5, *chunk), BF16),
            VM((4, *chunk), BF16),
            VM((TOK, PROJ), BF16),
            VM((TOK * SUB, LANE), F32),
            VM((TOK * SUB, LANE), F32),
            VM((NS * SUB, LANE), F32),
            VM((2 * NS * TOK, LANE), F32),
            VM((TOK, NS * SUB, LANE), F32),
            VM((TOK * SUB, LANE), F32),
            VM((SUB, LANE), F32),
            VM(states, BF16),
            VM(states, BF16),
            VM((NY, *states), BF16),
            VM((NX, *states), BF16),
            dma((2,)),
            dma((2,)),
            dma((32,)),
            dma((32,)),
            dma((NSEQ,)),
            dma((NSEQ,)),
            dma((NZ,)),
            dma((NZ,)),
            dma((NZ,)),
            dma((NZ,)),
            dma((NZ,)),
            dma((NZ,)),
        ],
        compiler_params=pltpu.CompilerParams(
            collective_id=0, has_side_effects=True, vmem_limit_bytes=VLIM
        ),
        name="mixer",
    )(dest, lengths, q, k, v, x, z, cw, cb, xw, dtw, dtb, rate, skip)


def attend_kernel(pos_ref, len_ref, q_ref, kv_ref, out, scores_a, scores_b):
    g = pl.program_id(0)
    heads = CH // HD
    rows = GROUP * RUN
    count = heads * rows
    wide = 2 * BK
    per = TOK * GROUP // wide
    starts = doc_starts(len_ref)
    bases = [pos_ref[g * GROUP + i] for i in range(GROUP)]
    lane = lax.broadcasted_iota(jnp.int32, (1, LANE), 1) % rows
    base = bases[0]
    for i in range(1, GROUP):
        base = jnp.where(lane >= i * RUN, bases[i], base)
    pos = base + lane % RUN
    start = start_of(pos, starts)
    top = g * per
    first = jnp.minimum(start_of(bases[0], starts) // wide, top)
    last_start = start_of(bases[GROUP - 1] + RUN - 1, starts)
    plain = jnp.maximum(jnp.minimum((last_start + wide - 1) // wide, top), first)
    q = jnp.concatenate([q_ref[:, h * HD : (h + 1) * HD] for h in range(heads)], axis=0)
    scale = HD**-0.5 * LOG2E
    key_row = lax.broadcasted_iota(jnp.int32, (BK, LANE), 0)
    ones = jnp.ones((16, BK), BF16)

    def score(into, i):
        keys = kv_ref[pl.ds(pl.multiple_of(i * BK, BK), BK), pl.ds(0, HD)]
        into[...] = lax.dot_general(
            keys, q, (((1,), (1,)), ((), ())), preferred_element_type=F32
        )

    def absorb(taken, i, carried, masked):
        begin = pl.multiple_of(i * BK, BK)
        best, summed = carried
        scores = taken[...]
        if masked:
            visible = (key_row <= pos - begin) & (key_row >= start - begin)
            scores = jnp.concatenate(
                [
                    jnp.where(visible, scores[:, j : j + LANE], MASKED)
                    for j in range(0, count, LANE)
                ],
                axis=1,
            )
        new_best = jnp.maximum(best, jnp.max(scores, axis=0, keepdims=True) * scale)
        weights = jnp.exp2(scores * scale - new_best).astype(BF16)
        rescale = jnp.exp2(best - new_best)
        values = jnp.concatenate(
            [kv_ref[pl.ds(begin + j, HD), pl.ds(HD, HD)] for j in range(0, BK, HD)], axis=1
        )
        values = jnp.concatenate([values, ones], axis=0)
        product = jnp.dot(values, weights, preferred_element_type=F32)
        return new_best, summed * rescale + product

    def pair(i, carried, masked, more=True):
        score(scores_b, 2 * i + 1)
        carried = absorb(scores_a, 2 * i, carried, masked)
        if more:
            score(scores_a, 2 * i + 2)
        return absorb(scores_b, 2 * i + 1, carried, masked)

    carried = (jnp.full((1, count), MASKED * scale, F32), jnp.zeros((HD + 16, count), F32))
    score(scores_a, 2 * first)
    carried = lax.fori_loop(first, plain, lambda i, v: pair(i, v, True), carried)
    carried = lax.fori_loop(plain, top, lambda i, v: pair(i, v, False), carried)
    for i in range(per):
        carried = pair(top + i, carried, True, i < per - 1)
    summed = carried[1]
    result = (summed[:HD] / summed[HD : HD + 1]).T.astype(BF16)
    for h in range(heads):
        out[:, h * HD : (h + 1) * HD] = result[h * rows : (h + 1) * rows]


def attend(positions, lengths, q, kv):
    rows = GROUP * RUN
    return pl.pallas_call(
        attend_kernel,
        out_shape=jax.ShapeDtypeStruct((TOK, CH), BF16),
        grid=(NSEQ // GROUP,),
        in_specs=[
            whole(pltpu.SMEM),
            whole(pltpu.SMEM),
            pl.BlockSpec((rows, CH), lambda g: (g, 0)),
            whole(),
        ],
        out_specs=pl.BlockSpec((rows, CH), lambda g: (g, 0)),
        scratch_shapes=[VM((BK, CH // HD * rows), F32)] * 2,
        compiler_params=pltpu.CompilerParams(vmem_limit_bytes=VLIM),
        name="attend",
    )(positions, lengths, q, kv)


def local(
    x_branch,
    z_branch,
    conv_weight,
    conv_bias,
    xproj_weight,
    dt_weight,
    dt_bias,
    decay_rate,
    skip_gain,
    query_rows,
    key_rows,
    value_rows,
    lengths,
    destination,
):
    q, kv, positions, mamba_out = mix(
        destination,
        lengths,
        query_rows.reshape(NSEQ, RUN, CH),
        key_rows,
        value_rows,
        x_branch,
        z_branch,
        conv_weight,
        conv_bias.reshape(1, CH),
        xproj_weight.T,
        dt_weight,
        dt_bias.reshape(1, CH),
        decay_rate,
        skip_gain.reshape(1, CH),
    )
    regrouped = attend(positions, lengths, q, kv)
    return (mamba_out, regrouped)


def solution(mesh):
    torus = Mesh(mesh.devices.reshape(NX, NY, NC, mesh.shape["mp"]), (*SEQ, "mp"))
    in_specs = (
        P(SEQ, "mp"),
        P(SEQ, "mp"),
        P(None, "mp"),
        P("mp"),
        P("mp", None),
        P(None, "mp"),
        P("mp"),
        P(None, "mp"),
        P("mp"),
        P(SEQ, "mp"),
        P(SEQ, "mp"),
        P(SEQ, "mp"),
        P(),
        P(),
    )
    out_specs = (P(SEQ, "mp"), P(SEQ, "mp"))
    return jax.shard_map(local, mesh=torus, in_specs=in_specs, out_specs=out_specs, check_vma=False)
```

```python
import math

import jax
import jax.numpy as jnp
from jax import lax
from jax.experimental import pallas as pl
from jax.experimental.pallas import tpu as pltpu
from jax.sharding import Mesh
from jax.sharding import PartitionSpec as P

SEQ = ("seq_0", "seq_1", "seq_2")
MESH = pl.DeviceIdType.MESH
VM = pltpu.VMEM
F32 = jnp.float32
BF16 = jnp.bfloat16
LOG2E = math.log2(math.e)
NX, NY, NC, NZ = 4, 4, 2, 8
NSEQ = NX * NY * NC
TOK = 256
TOK_BITS = 8
TOKENS = NSEQ * TOK
CH = 1024
LANE = 128
SUB = CH // LANE
NS = 16
RANK = 512
PROJ = RANK + 2 * NS
HD = 128
TAPS = 4
BIG_STEP = 1.0e7
MASKED = -1.0e30
GROUP = 8
RUN = TOK // NSEQ
BK = 512
VLIM = 60 * 1024 * 1024


def whole(space=VM):
    return pl.BlockSpec(memory_space=space)


def place():
    return (
        lax.axis_index("seq_0"),
        lax.axis_index("seq_1"),
        lax.axis_index("seq_2"),
        lax.axis_index("mp"),
    )


def seq_device(j, z):
    return (j // (NY * NC), (j // NC) % NY, j % NC, z)


def doc_starts(len_ref):
    s1 = len_ref[0]
    s2 = s1 + len_ref[1]
    return s1, s2, s2 + len_ref[2]


def start_of(pos, starts):
    s1, s2, s3 = starts
    return jnp.where(pos >= s3, s3, jnp.where(pos >= s2, s2, jnp.where(pos >= s1, s1, 0)))


def silu(x):
    return x / (1.0 + jnp.exp(-x))


def mixer_kernel(
    dest_ref,
    len_ref,
    q_ref,
    k_ref,
    v_ref,
    x_ref,
    z_ref,
    cw_ref,
    cb_ref,
    xw_ref,
    dtw_ref,
    dtb_ref,
    rate_ref,
    skip_ref,
    q_out,
    kv_out,
    pos_out,
    out,
    kvs,
    qs,
    halo,
    ext,
    inner,
    part,
    rs_plus,
    rs_minus,
    go_plus,
    go_minus,
    proj,
    steps,
    drives,
    rates,
    spread,
    gains,
    ys,
    sums,
    st_own,
    st_pair,
    st_y,
    st_x,
    loc_sem,
    halo_sem,
    kv_send,
    kv_recv,
    q_send,
    q_recv,
    rs_send,
    rs_recv,
    ag_send,
    ag_recv,
    st_send,
    st_recv,
):
    x, y, c, z = place()
    me = (x * NY + y) * NC + c
    anchor = me * TOK
    barrier = pltpu.get_barrier_semaphore()
    for k in range(1, NSEQ):
        pl.semaphore_signal(
            barrier, inc=1, device_id=seq_device((me + k) % NSEQ, z), device_id_type=MESH
        )
    for k in range(1, NZ):
        pl.semaphore_signal(
            barrier, inc=1, device_id=(x, y, c, (z + k) % NZ), device_id_type=MESH
        )
    load_k = pltpu.make_async_copy(k_ref, kvs.at[:, pl.ds(0, HD)], loc_sem.at[0])
    load_k.start()
    for half in range(TOK // HD):
        kvs[pl.ds(half * HD, HD), pl.ds(HD, HD)] = v_ref[pl.ds(half * HD, HD), :].T

    halves = TOK // LANE
    goal = lax.shift_right_logical(dest_ref[pl.ds(me * halves, halves), :], TOK_BITS) * RUN
    goal = goal + lax.broadcasted_iota(jnp.int32, (halves, LANE), 1) % RUN
    slot = lax.broadcasted_iota(jnp.int32, (TOK, LANE), 0)
    choice = jnp.concatenate(
        [jnp.where(slot == goal[i : i + 1], 1.0, 0.0) for i in range(halves)], axis=1
    )
    staged = jnp.dot(choice.astype(BF16), q_ref[...], preferred_element_type=F32)
    qs[...] = staged.astype(BF16).reshape(NSEQ, RUN, CH)

    starts = doc_starts(len_ref)
    token = anchor + lax.broadcasted_iota(jnp.int32, (TOK, LANE), 0)
    depth = token - start_of(token, starts)

    def convolve(count, cols, far):
        total = cb_ref[:, cols] + cw_ref[pl.ds(0, 1), cols] * ext[pl.ds(8, count), cols]
        for lag in range(1, TAPS):
            window = ext[pl.ds(8 - lag, count), cols]
            total = total + cw_ref[pl.ds(lag, 1), cols] * jnp.where(far >= lag, window, 0.0)
        inner[pl.ds(0, count), cols] = silu(total).astype(BF16)

    def conv_columns(i, carry):
        cols = pl.ds(pl.multiple_of(i * LANE, LANE), LANE)
        ext[pl.ds(0, 8), cols] = jnp.zeros((8, LANE), F32)
        ext[pl.ds(8, TOK), cols] = x_ref[:, cols].astype(F32)
        convolve(TOK, cols, depth)
        return carry

    lax.fori_loop(0, SUB, conv_columns, 0)
    load_k.wait()
    pl.semaphore_wait(barrier, NSEQ - 1 + NZ - 1)

    def remote(src, dst, send, recv, device):
        return pltpu.make_async_remote_copy(
            src_ref=src,
            dst_ref=dst,
            send_sem=send,
            recv_sem=recv,
            device_id=device,
            device_id_type=MESH,
        )

    def offset(a, b, core):
        return (x + a * (1 - core) + b * core) % NX, (y + a * core + b * (1 - core)) % NY

    def rows_of(a, b, core):
        px, py = offset(a, b, core)
        return pl.ds(pl.multiple_of(((px * NY + py) * NC + core) * TOK, TOK), TOK)

    partner = (x, y, 1 - c, z)
    after = (me + 1) % NSEQ
    halo_copy = remote(
        x_ref.at[pl.ds(TOK - 16, 16)], halo, halo_sem.at[0], halo_sem.at[1], seq_device(after, z)
    )
    halo_copy.start()
    mine = kv_out.at[rows_of(0, 0, c)]
    sends = []
    for a in range(1, NX):
        px, py = offset(a, 0, c)
        copy = remote(kvs, mine, kv_send.at[a], kv_recv.at[a], (px, py, c, z))
        copy.start()
        sends.append(copy)
    copy = remote(kvs, mine, kv_send.at[16], kv_recv.at[16], partner)
    copy.start()
    sends.append(copy)
    keep_kv = pltpu.make_async_copy(kvs, mine, loc_sem.at[0])
    keep_kv.start()
    q_rows = pl.ds(pl.multiple_of(me * RUN, RUN), RUN)
    for k in range(1, NSEQ):
        j = (me + k) % NSEQ
        copy = remote(qs.at[j], q_out.at[q_rows], q_send.at[k], q_recv.at[k], seq_device(j, z))
        copy.start()
        sends.append(copy)
    keep_q = pltpu.make_async_copy(qs.at[me], q_out.at[q_rows], loc_sem.at[1])
    keep_q.start()

    halo_copy.wait()
    ext[pl.ds(0, 8), :] = halo[pl.ds(8, 8), :].astype(F32)
    near = anchor + lax.broadcasted_iota(jnp.int32, (16, CH), 0)
    convolve(16, pl.ds(0, CH), near - start_of(near, starts))

    partial = lax.dot_general(
        inner[...], xw_ref[...], (((1,), (1,)), ((), ())), preferred_element_type=F32
    ).astype(BF16)
    slice_rows = TOK // NZ
    part[...] = partial.reshape(NZ, slice_rows, PROJ)
    up = (x, y, c, (z + 1) % NZ)
    down = (x, y, c, (z + NZ - 1) % NZ)

    def ring_plus(s):
        src = part.at[(z + 4) % NZ] if s == 1 else go_plus.at[s]
        return remote(src, rs_plus.at[s], rs_send.at[s], rs_recv.at[s], up)

    def ring_minus(s):
        src = part.at[(z + 5) % NZ] if s == 1 else go_minus.at[s]
        return remote(src, rs_minus.at[s], rs_send.at[4 + s], rs_recv.at[4 + s], down)

    plus, minus = ring_plus(1), ring_minus(1)
    plus.start()
    minus.start()
    sends += [plus, minus]

    def wait_kv(slot_rows, index):
        remote(kvs, kv_out.at[slot_rows], kv_send.at[0], kv_recv.at[index], partner).wait_recv()

    for s in range(1, 4):
        plus.wait_recv()
        go_plus[s + 1] = (rs_plus[s].astype(F32) + part[(z + 4 - s) % NZ].astype(F32)).astype(BF16)
        plus = ring_plus(s + 1)
        plus.start()
        sends.append(plus)
        minus.wait_recv()
        if s < 3:
            go_minus[s + 1] = (
                rs_minus[s].astype(F32) + part[(z + 5 + s) % NZ].astype(F32)
            ).astype(BF16)
            minus = ring_minus(s + 1)
            minus.start()
            sends.append(minus)
        if s == 1:
            for a in range(NX):
                if a > 0:
                    wait_kv(rows_of(-a, 0, c), a)
                block = kv_out.at[rows_of(-a, 0, c)] if a > 0 else kvs
                target = kv_out.at[rows_of(-a, 0, c)]
                for b in range(1, NY):
                    px, py = offset(0, b, c)
                    index = b * NX + a
                    copy = remote(
                        block, target, kv_send.at[index], kv_recv.at[index], (px, py, c, z)
                    )
                    copy.start()
                    sends.append(copy)
                if a > 0:
                    copy = remote(
                        block, target, kv_send.at[16 + a], kv_recv.at[16 + a], partner
                    )
                    copy.start()
                    sends.append(copy)
    plus.wait_recv()
    total = part[z].astype(F32) + rs_plus[4].astype(F32) + rs_minus[3].astype(F32)

    def proj_rows(chunk):
        return pl.ds(pl.multiple_of((chunk % NZ) * slice_rows, slice_rows), slice_rows)

    proj[proj_rows(z), :] = total.astype(BF16)

    def pass_plus(s):
        rows = proj.at[proj_rows(z + NZ + 1 - s)]
        return remote(rows, rows, ag_send.at[s], ag_recv.at[s], up)

    def pass_minus(s):
        rows = proj.at[proj_rows(z + s - 1)]
        return remote(rows, rows, ag_send.at[4 + s], ag_recv.at[4 + s], down)

    def got_plus(s):
        rows = proj.at[proj_rows(z + NZ - s)]
        remote(rows, rows, ag_send.at[s], ag_recv.at[s], up).wait_recv()

    def got_minus(s):
        rows = proj.at[proj_rows(z + s)]
        remote(rows, rows, ag_send.at[4 + s], ag_recv.at[4 + s], down).wait_recv()

    for s in range(1, 5):
        if s > 1:
            got_plus(s - 1)
        copy = pass_plus(s)
        copy.start()
        sends.append(copy)
        if s < 4:
            if s > 1:
                got_minus(s - 1)
            copy = pass_minus(s)
            copy.start()
            sends.append(copy)
    spots = (TOKENS // LANE, LANE)
    spot = lax.broadcasted_iota(jnp.int32, spots, 1)
    ours = (lax.shift_right_logical(dest_ref[...], TOK_BITS) == me) & (spot % RUN == 0)
    spot = spot + LANE * lax.broadcasted_iota(jnp.int32, spots, 0)
    found = jnp.sum(jnp.where(ours, spot, 0).astype(F32), axis=1, keepdims=True)
    pos_out[...] = jnp.broadcast_to(found, spots).astype(jnp.int32)
    for j in range(SUB):
        cols = pl.ds(j * LANE, LANE)
        rates[pl.ds(j, NS, stride=SUB), :] = rate_ref[:, cols] * (-LOG2E)
    got_minus(3)
    got_plus(4)

    begins = depth == 0
    for j in range(SUB):
        cols = pl.ds(j * LANE, LANE)
        raw = jnp.dot(proj[:, pl.ds(0, RANK)], dtw_ref[:, cols], preferred_element_type=F32)
        step = jax.nn.softplus(raw + dtb_ref[:, cols])
        drives[pl.ds(j, TOK, stride=SUB), :] = step * inner[:, cols].astype(F32)
        step = jnp.where(begins, BIG_STEP, step)
        sums[pl.ds(j, 1), :] = jnp.sum(step, axis=0, keepdims=True)
        steps[pl.ds(j, TOK, stride=SUB), :] = step
    row = lax.broadcasted_iota(jnp.int32, (2 * NS, 2 * NS * LANE), 0)
    col = lax.broadcasted_iota(jnp.int32, (2 * NS, 2 * NS * LANE), 1)
    pick = jnp.where(col // LANE == row, 1.0, 0.0).astype(BF16)
    wide = jnp.dot(proj[:, pl.ds(RANK, 2 * NS)], pick, preferred_element_type=F32)
    for n in range(2 * NS):
        spread[pl.ds(n * TOK, TOK), :] = wide[:, n * LANE : (n + 1) * LANE]
    rate = [rates[pl.ds(n * SUB, SUB), :] for n in range(NS)]

    def advance(t, carried):
        rows = pl.ds(pl.multiple_of(t * SUB, SUB), SUB)
        step = steps[rows, :]
        drive = drives[rows, :]
        result = []
        for n in range(NS):
            b = spread[pl.ds(n * TOK + t, SUB, stride=0), :]
            result.append(jnp.exp2(step * rate[n]) * carried[n] + b * drive)
        return tuple(result)

    zero = jnp.zeros((SUB, LANE), F32)
    state = lax.fori_loop(0, TOK, advance, (zero,) * NS, unroll=4)

    def pack(into, states, total):
        for n in range(0, NS, 2):
            pair = jnp.concatenate([states[n], states[n + 1]], axis=0)
            into[pl.ds(n * SUB, 2 * SUB), :] = pair.astype(BF16)
        high = total.astype(BF16).astype(F32)
        pair = jnp.concatenate([high, total - high], axis=0)
        into[pl.ds(NS * SUB, 2 * SUB), :] = pair.astype(BF16)

    def unpack(taken):
        block = taken[...].astype(F32).reshape(NS + 2, SUB, LANE)
        return [block[n] for n in range(NS)], block[NS] + block[NS + 1]

    def follow(states, block, total, passed=None):
        result = []
        for n in range(NS):
            moved = jnp.exp2(rate[n] * total) * states[n] + block[n]
            result.append(moved if passed is None else jnp.where(passed, moved, states[n]))
        return result

    pack(st_own, state, sums[...])
    pair_copy = remote(st_own, st_pair, st_send.at[0], st_recv.at[0], partner)
    pair_copy.start()
    sends.append(pair_copy)

    def local_token(t, carried):
        so_far, states = carried
        rows = pl.ds(pl.multiple_of(t * SUB, SUB), SUB)
        step = steps[rows, :]
        drive = drives[rows, :]
        so_far = so_far + step
        result = []
        total = None
        for n in range(NS):
            r = rates[pl.ds(n * SUB, SUB), :]
            b = spread[pl.ds(n * TOK + t, SUB, stride=0), :]
            weight = spread[pl.ds((NS + n) * TOK + t, SUB, stride=0), :]
            new = jnp.exp2(step * r) * states[n] + b * drive
            result.append(new)
            total = weight * new if total is None else total + weight * new
            gains[t, pl.ds(n * SUB, SUB), :] = weight * jnp.exp2(so_far * r)
        ys[rows, :] = total
        return so_far, tuple(result)

    carried = (zero, (zero,) * NS)
    cuts = (0, 40, 144, TOK)
    carried = lax.fori_loop(cuts[0], cuts[1], local_token, carried, unroll=2)

    pair_copy.wait_recv()
    own_state, own_total = unpack(st_own)
    other_state, other_total = unpack(st_pair)
    first_core = c == 0
    early = [jnp.where(first_core, p, q) for p, q in zip(own_state, other_state)]
    late = [jnp.where(first_core, q, p) for p, q in zip(own_state, other_state)]
    late_total = jnp.where(first_core, other_total, own_total)
    chip_state = follow(early, late, late_total)
    pack(st_y.at[0], chip_state, own_total + other_total)
    level = []
    for k in range(1, NY):
        copy = remote(
            st_y.at[0], st_y.at[k], st_send.at[k], st_recv.at[k], (x, (y + k) % NY, c, z)
        )
        copy.start()
        level.append(copy)
    sends += level
    carried = lax.fori_loop(cuts[1], cuts[2], local_token, carried, unroll=2)

    for copy in level:
        copy.wait_recv()
    column, column_total = unpack(st_y.at[(y + NY) % NY])
    for j in range(1, NY):
        block, total = unpack(st_y.at[(y + NY - j) % NY])
        column = follow(column, block, total)
        column_total = column_total + total
    pack(st_x.at[0], column, column_total)
    level = []
    for k in range(1, NX):
        copy = remote(
            st_x.at[0], st_x.at[k], st_send.at[4 + k], st_recv.at[4 + k], ((x + k) % NX, y, c, z)
        )
        copy.start()
        level.append(copy)
    sends += level
    carried = lax.fori_loop(cuts[2], cuts[3], local_token, carried, unroll=2)

    for b in range(1, NY):
        for a in range(NX):
            index = b * NX + a
            wait_kv(rows_of(-a, -b, c), index)
            block = kv_out.at[rows_of(-a, -b, c)]
            copy = remote(block, block, kv_send.at[16 + index], kv_recv.at[16 + index], partner)
            copy.start()
            sends.append(copy)

    for copy in level:
        copy.wait_recv()
    entering = [zero] * NS
    for j in range(NX - 1):
        block, total = unpack(st_x.at[(x + NX - j) % NX])
        entering = follow(entering, block, total, x > j)
    for j in range(NY - 1):
        block, total = unpack(st_y.at[(y + NY - j) % NY])
        entering = follow(entering, block, total, y > j)
    entering = follow(entering, early, jnp.where(first_core, own_total, other_total), c > 0)

    def correct(t, carry):
        rows = pl.ds(pl.multiple_of(t * SUB, SUB), SUB)
        total = ys[rows, :]
        for n in range(NS):
            total = total + gains[t, pl.ds(n * SUB, SUB), :] * entering[n]
        ys[rows, :] = total
        return carry

    lax.fori_loop(0, TOK, correct, 0, unroll=4)
    for j in range(SUB):
        cols = pl.ds(j * LANE, LANE)
        scanned = ys[pl.ds(j, TOK, stride=SUB), :]
        scanned = scanned + skip_ref[:, cols] * inner[:, cols].astype(F32)
        out[:, cols] = (scanned * silu(z_ref[:, cols].astype(F32))).astype(BF16)

    for k in range(1, NSEQ):
        rows = pl.ds(pl.multiple_of(((me + NSEQ - k) % NSEQ) * RUN, RUN), RUN)
        remote(qs.at[0], q_out.at[rows], q_send.at[k], q_recv.at[k], partner).wait_recv()
    for b in range(NY):
        for a in range(NX):
            wait_kv(rows_of(-a, -b, 1 - c), 16 + b * NX + a)
    for copy in sends:
        copy.wait_send()
    keep_kv.wait()
    keep_q.wait()


def mix(dest, lengths, q, k, v, x, z, cw, cb, xw, dtw, dtb, rate, skip):
    dma = pltpu.SemaphoreType.DMA
    states = ((NS + 2) * SUB, LANE)
    chunk = (TOK // NZ, PROJ)
    return pl.pallas_call(
        mixer_kernel,
        out_shape=(
            jax.ShapeDtypeStruct((TOK, CH), BF16),
            jax.ShapeDtypeStruct((NSEQ * TOK, 2 * HD), BF16),
            jax.ShapeDtypeStruct((TOKENS // LANE, LANE), jnp.int32),
            jax.ShapeDtypeStruct((TOK, CH), BF16),
        ),
        in_specs=[whole(), whole(pltpu.SMEM), whole(), whole(pl.ANY)] + [whole()] * 10,
        out_specs=(whole(pl.ANY), whole(pl.ANY), whole(), whole()),
        scratch_shapes=[
            VM((TOK, 2 * HD), BF16),
            VM((NSEQ, RUN, CH), BF16),
            VM((16, CH), BF16),
            VM((TOK + 8, CH), F32),
            VM((TOK, CH), BF16),
            VM((NZ, *chunk), BF16),
            VM((5, *chunk), BF16),
            VM((4, *chunk), BF16),
            VM((5, *chunk), BF16),
            VM((4, *chunk), BF16),
            VM((TOK, PROJ), BF16),
            VM((TOK * SUB, LANE), F32),
            VM((TOK * SUB, LANE), F32),
            VM((NS * SUB, LANE), F32),
            VM((2 * NS * TOK, LANE), F32),
            VM((TOK, NS * SUB, LANE), F32),
            VM((TOK * SUB, LANE), F32),
            VM((SUB, LANE), F32),
            VM(states, BF16),
            VM(states, BF16),
            VM((NY, *states), BF16),
            VM((NX, *states), BF16),
            dma((2,)),
            dma((2,)),
            dma((32,)),
            dma((32,)),
            dma((NSEQ,)),
            dma((NSEQ,)),
            dma((NZ,)),
            dma((NZ,)),
            dma((NZ,)),
            dma((NZ,)),
            dma((NZ,)),
            dma((NZ,)),
        ],
        compiler_params=pltpu.CompilerParams(
            collective_id=0, has_side_effects=True, vmem_limit_bytes=VLIM
        ),
        name="mixer",
    )(dest, lengths, q, k, v, x, z, cw, cb, xw, dtw, dtb, rate, skip)


def attend_kernel(pos_ref, len_ref, q_ref, kv_ref, out, scores_a, scores_b):
    g = pl.program_id(0)
    heads = CH // HD
    rows = GROUP * RUN
    count = heads * rows
    wide = 2 * BK
    per = TOK * GROUP // wide
    starts = doc_starts(len_ref)
    halves = TOK // LANE
    bases = [
        sum(pos_ref[(g * GROUP + i) * halves + j, 0] for j in range(halves)) for i in range(GROUP)
    ]
    lane = lax.broadcasted_iota(jnp.int32, (1, LANE), 1) % rows
    base = bases[0]
    for i in range(1, GROUP):
        base = jnp.where(lane >= i * RUN, bases[i], base)
    pos = base + lane % RUN
    start = start_of(pos, starts)
    top = g * per
    first = jnp.minimum(start_of(bases[0], starts) // wide, top)
    last_start = start_of(bases[GROUP - 1] + RUN - 1, starts)
    plain = jnp.maximum(jnp.minimum((last_start + wide - 1) // wide, top), first)
    q = jnp.concatenate([q_ref[:, h * HD : (h + 1) * HD] for h in range(heads)], axis=0)
    scale = HD**-0.5 * LOG2E
    key_row = lax.broadcasted_iota(jnp.int32, (BK, LANE), 0)
    ones = jnp.ones((16, BK), BF16)

    def score(into, i):
        keys = kv_ref[pl.ds(pl.multiple_of(i * BK, BK), BK), pl.ds(0, HD)]
        into[...] = lax.dot_general(
            keys, q, (((1,), (1,)), ((), ())), preferred_element_type=F32
        )

    def absorb(taken, i, carried, masked):
        begin = pl.multiple_of(i * BK, BK)
        best, summed = carried
        scores = taken[...]
        if masked:
            visible = (key_row <= pos - begin) & (key_row >= start - begin)
            scores = jnp.concatenate(
                [
                    jnp.where(visible, scores[:, j : j + LANE], MASKED)
                    for j in range(0, count, LANE)
                ],
                axis=1,
            )
        new_best = jnp.maximum(best, jnp.max(scores, axis=0, keepdims=True) * scale)
        weights = jnp.exp2(scores * scale - new_best).astype(BF16)
        rescale = jnp.exp2(best - new_best)
        values = jnp.concatenate(
            [kv_ref[pl.ds(begin + j, HD), pl.ds(HD, HD)] for j in range(0, BK, HD)], axis=1
        )
        values = jnp.concatenate([values, ones], axis=0)
        product = jnp.dot(values, weights, preferred_element_type=F32)
        return new_best, summed * rescale + product

    def pair(i, carried, masked, more=True):
        score(scores_b, 2 * i + 1)
        carried = absorb(scores_a, 2 * i, carried, masked)
        if more:
            score(scores_a, 2 * i + 2)
        return absorb(scores_b, 2 * i + 1, carried, masked)

    carried = (jnp.full((1, count), MASKED * scale, F32), jnp.zeros((HD + 16, count), F32))
    score(scores_a, 2 * first)
    carried = lax.fori_loop(first, plain, lambda i, v: pair(i, v, True), carried)
    carried = lax.fori_loop(plain, top, lambda i, v: pair(i, v, False), carried)
    for i in range(per):
        carried = pair(top + i, carried, True, i < per - 1)
    summed = carried[1]
    result = (summed[:HD] / summed[HD : HD + 1]).T.astype(BF16)
    for h in range(heads):
        out[:, h * HD : (h + 1) * HD] = result[h * rows : (h + 1) * rows]


def attend(positions, lengths, q, kv):
    rows = GROUP * RUN
    return pl.pallas_call(
        attend_kernel,
        out_shape=jax.ShapeDtypeStruct((TOK, CH), BF16),
        grid=(NSEQ // GROUP,),
        in_specs=[
            whole(pltpu.SMEM),
            whole(pltpu.SMEM),
            pl.BlockSpec((rows, CH), lambda g: (g, 0)),
            whole(),
        ],
        out_specs=pl.BlockSpec((rows, CH), lambda g: (g, 0)),
        scratch_shapes=[VM((BK, CH // HD * rows), F32)] * 2,
        compiler_params=pltpu.CompilerParams(vmem_limit_bytes=VLIM),
        name="attend",
    )(positions, lengths, q, kv)


def local(
    x_branch,
    z_branch,
    conv_weight,
    conv_bias,
    xproj_weight,
    dt_weight,
    dt_bias,
    decay_rate,
    skip_gain,
    query_rows,
    key_rows,
    value_rows,
    lengths,
    destination,
):
    q, kv, positions, mamba_out = mix(
        destination.reshape(TOKENS // LANE, LANE),
        lengths,
        query_rows,
        key_rows,
        value_rows,
        x_branch,
        z_branch,
        conv_weight,
        conv_bias.reshape(1, CH),
        xproj_weight.T,
        dt_weight,
        dt_bias.reshape(1, CH),
        decay_rate,
        skip_gain.reshape(1, CH),
    )
    regrouped = attend(positions, lengths, q, kv)
    return (mamba_out, regrouped)


def solution(mesh):
    torus = Mesh(mesh.devices.reshape(NX, NY, NC, mesh.shape["mp"]), (*SEQ, "mp"))
    in_specs = (
        P(SEQ, "mp"),
        P(SEQ, "mp"),
        P(None, "mp"),
        P("mp"),
        P("mp", None),
        P(None, "mp"),
        P("mp"),
        P(None, "mp"),
        P("mp"),
        P(SEQ, "mp"),
        P(SEQ, "mp"),
        P(SEQ, "mp"),
        P(),
        P(),
    )
    out_specs = (P(SEQ, "mp"), P(SEQ, "mp"))
    return jax.shard_map(local, mesh=torus, in_specs=in_specs, out_specs=out_specs, check_vma=False)
```

```python
import math

import jax
import jax.numpy as jnp
from jax import lax
from jax.experimental import pallas as pl
from jax.experimental.pallas import tpu as pltpu
from jax.sharding import Mesh
from jax.sharding import PartitionSpec as P

SEQ = ("seq_0", "seq_1", "seq_2")
MESH = pl.DeviceIdType.MESH
VM = pltpu.VMEM
F32 = jnp.float32
BF16 = jnp.bfloat16
LOG2E = math.log2(math.e)
NX, NY, NC, NZ = 4, 4, 2, 8
NSEQ = NX * NY * NC
TOK = 256
TOK_BITS = 8
TOKENS = NSEQ * TOK
CH = 1024
LANE = 128
SUB = CH // LANE
NS = 16
RANK = 512
PROJ = RANK + 2 * NS
HD = 128
TAPS = 4
BIG_STEP = 1.0e7
MASKED = -1.0e30
GROUP = 8
RUN = TOK // NSEQ
BK = 512
VLIM = 60 * 1024 * 1024


def whole(space=VM):
    return pl.BlockSpec(memory_space=space)


def place():
    return (
        lax.axis_index("seq_0"),
        lax.axis_index("seq_1"),
        lax.axis_index("seq_2"),
        lax.axis_index("mp"),
    )


def seq_device(j, z):
    chip = lax.div(j, NC)
    return (lax.div(chip, NY), lax.rem(chip, NY), lax.rem(j, NC), z)


def doc_starts(len_ref):
    s1 = len_ref[0]
    s2 = s1 + len_ref[1]
    return s1, s2, s2 + len_ref[2]


def start_of(pos, starts):
    s1, s2, s3 = starts
    return jnp.where(pos >= s3, s3, jnp.where(pos >= s2, s2, jnp.where(pos >= s1, s1, 0)))


def silu(x):
    half = 0.5 * x
    return half * jnp.tanh(half) + half


def mixer_kernel(
    dest_ref,
    len_ref,
    q_ref,
    k_ref,
    v_ref,
    x_ref,
    z_hbm,
    cw_ref,
    cb_ref,
    xw_hbm,
    dtw_hbm,
    dtb_ref,
    rate_ref,
    skip_ref,
    q_out,
    kv_out,
    pos_out,
    out,
    kvs,
    qs,
    halo,
    ext,
    inner,
    part,
    rs_plus,
    rs_minus,
    go_plus,
    go_minus,
    proj,
    steps,
    drives,
    rates,
    spread,
    gains,
    ys,
    sums,
    st_own,
    st_pair,
    st_y,
    st_x,
    decays,
    z_ref,
    xw_ref,
    dtw_ref,
    loc_sem,
    halo_sem,
    kv_send,
    kv_recv,
    q_send,
    q_recv,
    rs_send,
    rs_recv,
    ag_send,
    ag_recv,
    st_send,
    st_recv,
):
    x, y, c, z = place()
    me = (x * NY + y) * NC + c
    anchor = me * TOK
    barrier = pltpu.get_barrier_semaphore()
    for k in range(1, NSEQ):
        pl.semaphore_signal(
            barrier, inc=1, device_id=seq_device(lax.rem(me + k, NSEQ), z), device_id_type=MESH
        )
    for k in range(1, NZ):
        pl.semaphore_signal(
            barrier, inc=1, device_id=(x, y, c, lax.rem(z + k, NZ)), device_id_type=MESH
        )
    load_k = pltpu.make_async_copy(k_ref, kvs.at[:, pl.ds(0, HD)], loc_sem.at[0])
    load_k.start()
    load_x = pltpu.make_async_copy(xw_hbm, xw_ref, loc_sem.at[2])
    load_x.start()
    load_d = pltpu.make_async_copy(dtw_hbm, dtw_ref, loc_sem.at[3])
    load_d.start()
    load_z = pltpu.make_async_copy(z_hbm, z_ref, loc_sem.at[4])
    load_z.start()
    for half in range(TOK // HD):
        kvs[pl.ds(half * HD, HD), pl.ds(HD, HD)] = v_ref[pl.ds(half * HD, HD), :].T

    halves = TOK // LANE
    goal = lax.shift_right_logical(dest_ref[pl.ds(me * halves, halves), :], TOK_BITS) * RUN
    goal = goal + lax.broadcasted_iota(jnp.int32, (halves, LANE), 1) % RUN
    slot = lax.broadcasted_iota(jnp.int32, (TOK, LANE), 0)
    choice = jnp.concatenate(
        [jnp.where(slot == goal[i : i + 1], 1.0, 0.0) for i in range(halves)], axis=1
    )
    staged = jnp.dot(choice.astype(BF16), q_ref[...], preferred_element_type=F32)
    qs[...] = staged.astype(BF16).reshape(NSEQ, RUN, CH)

    starts = doc_starts(len_ref)
    token = anchor + lax.broadcasted_iota(jnp.int32, (TOK, LANE), 0)
    depth = token - start_of(token, starts)

    def convolve(count, cols, far):
        total = cb_ref[:, cols] + cw_ref[pl.ds(0, 1), cols] * ext[pl.ds(8, count), cols]
        for lag in range(1, TAPS):
            window = ext[pl.ds(8 - lag, count), cols]
            total = total + cw_ref[pl.ds(lag, 1), cols] * jnp.where(far >= lag, window, 0.0)
        inner[pl.ds(0, count), cols] = silu(total).astype(BF16)

    def conv_columns(i, carry):
        cols = pl.ds(pl.multiple_of(i * LANE, LANE), LANE)
        ext[pl.ds(0, 8), cols] = jnp.zeros((8, LANE), F32)
        ext[pl.ds(8, TOK), cols] = x_ref[:, cols].astype(F32)
        convolve(TOK, cols, depth)
        return carry

    lax.fori_loop(0, SUB, conv_columns, 0)
    load_k.wait()
    pl.semaphore_wait(barrier, NSEQ - 1 + NZ - 1)

    def remote(src, dst, send, recv, device):
        return pltpu.make_async_remote_copy(
            src_ref=src,
            dst_ref=dst,
            send_sem=send,
            recv_sem=recv,
            device_id=device,
            device_id_type=MESH,
        )

    def offset(a, b, core):
        a, b = a % NX, b % NY
        return (
            lax.rem(x + a * (1 - core) + b * core, NX),
            lax.rem(y + a * core + b * (1 - core), NY),
        )

    def rows_of(a, b, core):
        px, py = offset(a, b, core)
        return pl.ds(pl.multiple_of(((px * NY + py) * NC + core) * TOK, TOK), TOK)

    partner = (x, y, 1 - c, z)
    after = lax.rem(me + 1, NSEQ)
    halo_copy = remote(
        x_ref.at[pl.ds(TOK - 16, 16)], halo, halo_sem.at[0], halo_sem.at[1], seq_device(after, z)
    )
    halo_copy.start()
    mine = kv_out.at[rows_of(0, 0, c)]
    sends = []
    for a in range(1, NX):
        px, py = offset(a, 0, c)
        copy = remote(kvs, mine, kv_send.at[a], kv_recv.at[a], (px, py, c, z))
        copy.start()
        sends.append(copy)
    copy = remote(kvs, mine, kv_send.at[16], kv_recv.at[16], partner)
    copy.start()
    sends.append(copy)
    keep_kv = pltpu.make_async_copy(kvs, mine, loc_sem.at[0])
    keep_kv.start()
    q_rows = pl.ds(pl.multiple_of(me * RUN, RUN), RUN)
    for k in range(1, NSEQ):
        j = lax.rem(me + k, NSEQ)
        copy = remote(qs.at[j], q_out.at[q_rows], q_send.at[k], q_recv.at[k], seq_device(j, z))
        copy.start()
        sends.append(copy)
    keep_q = pltpu.make_async_copy(qs.at[me], q_out.at[q_rows], loc_sem.at[1])
    keep_q.start()

    halo_copy.wait()
    ext[pl.ds(0, 8), :] = halo[pl.ds(8, 8), :].astype(F32)
    near = anchor + lax.broadcasted_iota(jnp.int32, (16, CH), 0)
    convolve(16, pl.ds(0, CH), near - start_of(near, starts))

    load_x.wait()
    partial = lax.dot_general(
        inner[...], xw_ref[...], (((1,), (1,)), ((), ())), preferred_element_type=F32
    ).astype(BF16)
    slice_rows = TOK // NZ
    part[...] = partial.reshape(NZ, slice_rows, PROJ)
    up = (x, y, c, lax.rem(z + 1, NZ))
    down = (x, y, c, lax.rem(z + NZ - 1, NZ))

    def ring_plus(s):
        src = part.at[lax.rem(z + 4, NZ)] if s == 1 else go_plus.at[s]
        return remote(src, rs_plus.at[s], rs_send.at[s], rs_recv.at[s], up)

    def ring_minus(s):
        src = part.at[lax.rem(z + 5, NZ)] if s == 1 else go_minus.at[s]
        return remote(src, rs_minus.at[s], rs_send.at[4 + s], rs_recv.at[4 + s], down)

    plus, minus = ring_plus(1), ring_minus(1)
    plus.start()
    minus.start()
    sends += [plus, minus]

    def wait_kv(slot_rows, index):
        remote(kvs, kv_out.at[slot_rows], kv_send.at[0], kv_recv.at[index], partner).wait_recv()

    for s in range(1, 4):
        plus.wait_recv()
        go_plus[s + 1] = (rs_plus[s].astype(F32) + part[lax.rem(z + 4 - s, NZ)].astype(F32)).astype(BF16)
        plus = ring_plus(s + 1)
        plus.start()
        sends.append(plus)
        minus.wait_recv()
        if s < 3:
            go_minus[s + 1] = (
                rs_minus[s].astype(F32) + part[lax.rem(z + 5 + s, NZ)].astype(F32)
            ).astype(BF16)
            minus = ring_minus(s + 1)
            minus.start()
            sends.append(minus)
        if s == 1:
            for a in range(NX):
                if a > 0:
                    wait_kv(rows_of(-a, 0, c), a)
                block = kv_out.at[rows_of(-a, 0, c)] if a > 0 else kvs
                target = kv_out.at[rows_of(-a, 0, c)]
                for b in range(1, NY):
                    px, py = offset(0, b, c)
                    index = b * NX + a
                    copy = remote(
                        block, target, kv_send.at[index], kv_recv.at[index], (px, py, c, z)
                    )
                    copy.start()
                    sends.append(copy)
                if a > 0:
                    copy = remote(
                        block, target, kv_send.at[16 + a], kv_recv.at[16 + a], partner
                    )
                    copy.start()
                    sends.append(copy)
    plus.wait_recv()
    total = part[z].astype(F32) + rs_plus[4].astype(F32) + rs_minus[3].astype(F32)

    def proj_rows(chunk):
        return pl.ds(pl.multiple_of(lax.rem(chunk, NZ) * slice_rows, slice_rows), slice_rows)

    proj[proj_rows(z), :] = total.astype(BF16)

    def pass_plus(s):
        rows = proj.at[proj_rows(z + NZ + 1 - s)]
        return remote(rows, rows, ag_send.at[s], ag_recv.at[s], up)

    def pass_minus(s):
        rows = proj.at[proj_rows(z + s - 1)]
        return remote(rows, rows, ag_send.at[4 + s], ag_recv.at[4 + s], down)

    def got_plus(s):
        rows = proj.at[proj_rows(z + NZ - s)]
        remote(rows, rows, ag_send.at[s], ag_recv.at[s], up).wait_recv()

    def got_minus(s):
        rows = proj.at[proj_rows(z + s)]
        remote(rows, rows, ag_send.at[4 + s], ag_recv.at[4 + s], down).wait_recv()

    for s in range(1, 5):
        if s > 1:
            got_plus(s - 1)
        copy = pass_plus(s)
        copy.start()
        sends.append(copy)
        if s < 4:
            if s > 1:
                got_minus(s - 1)
            copy = pass_minus(s)
            copy.start()
            sends.append(copy)
    spots = (TOKENS // LANE, LANE)
    spot = lax.broadcasted_iota(jnp.int32, spots, 1)
    ours = (lax.shift_right_logical(dest_ref[...], TOK_BITS) == me) & (spot % RUN == 0)
    spot = spot + LANE * lax.broadcasted_iota(jnp.int32, spots, 0)
    found = jnp.sum(jnp.where(ours, spot, 0).astype(F32), axis=1, keepdims=True)
    pos_out[...] = jnp.broadcast_to(found, spots).astype(jnp.int32)
    for j in range(SUB):
        cols = pl.ds(j * LANE, LANE)
        rates[pl.ds(j, NS, stride=SUB), :] = rate_ref[:, cols] * (-LOG2E)
    got_minus(3)
    got_plus(4)

    load_d.wait()
    begins = depth == 0
    low = proj[:, pl.ds(0, RANK)]
    for j in range(SUB):
        cols = pl.ds(j * LANE, LANE)
        if j % 2 == 0:
            both = pl.ds(j * LANE, 2 * LANE)
            raw = jnp.dot(low, dtw_ref[:, both], preferred_element_type=F32)
        value = raw[:, j % 2 * LANE : (j % 2 + 1) * LANE] + dtb_ref[:, cols]
        fade = jnp.exp2(jnp.abs(value) * (-LOG2E))
        series = fade - (0.5 * fade) * fade
        tail = jnp.where(fade < 1.0e-3, series, jnp.log(1.0 + fade))
        step = jnp.maximum(value, 0.0) + tail
        drives[pl.ds(j, TOK, stride=SUB), :] = step * inner[:, cols].astype(F32)
        step = jnp.where(begins, BIG_STEP, step)
        sums[pl.ds(j, 1), :] = jnp.sum(step, axis=0, keepdims=True)
        steps[pl.ds(j, TOK, stride=SUB), :] = step

    def widen(first):
        row = lax.broadcasted_iota(jnp.int32, (2 * NS, NS * LANE), 0)
        col = lax.broadcasted_iota(jnp.int32, (2 * NS, NS * LANE), 1)
        pick = jnp.where(lax.div(col, LANE) + first == row, 1.0, 0.0).astype(BF16)
        wide = jnp.dot(proj[:, pl.ds(RANK, 2 * NS)], pick, preferred_element_type=F32)
        for n in range(NS):
            spread[pl.ds((first + n) * TOK, TOK), :] = wide[:, n * LANE : (n + 1) * LANE]

    widen(0)
    rate = [rates[pl.ds(n * SUB, SUB), :] for n in range(NS)]

    def advance(t, carried):
        rows = pl.ds(pl.multiple_of(t * SUB, SUB), SUB)
        step = steps[rows, :]
        drive = drives[rows, :]
        result = []
        for n in range(NS):
            b = spread[pl.ds(n * TOK + t, SUB, stride=0), :]
            decay = jnp.exp2(step * rate[n])
            decays[t, pl.ds(n * SUB, SUB), :] = decay
            result.append(decay * carried[n] + b * drive)
        return tuple(result)

    zero = jnp.zeros((SUB, LANE), F32)
    state = lax.fori_loop(0, TOK, advance, (zero,) * NS, unroll=4)

    def pack(into, states, total):
        for n in range(0, NS, 2):
            pair = jnp.concatenate([states[n], states[n + 1]], axis=0)
            into[pl.ds(n * SUB, 2 * SUB), :] = pair.astype(BF16)
        high = total.astype(BF16).astype(F32)
        pair = jnp.concatenate([high, total - high], axis=0)
        into[pl.ds(NS * SUB, 2 * SUB), :] = pair.astype(BF16)

    def unpack(taken):
        block = taken[...].astype(F32).reshape(NS + 2, SUB, LANE)
        return [block[n] for n in range(NS)], block[NS] + block[NS + 1]

    def follow(states, block, total, passed=None):
        result = []
        for n in range(NS):
            moved = jnp.exp2(rate[n] * total) * states[n] + block[n]
            result.append(moved if passed is None else jnp.where(passed, moved, states[n]))
        return result

    pack(st_own, state, sums[...])
    pair_copy = remote(st_own, st_pair, st_send.at[0], st_recv.at[0], partner)
    pair_copy.start()
    sends.append(pair_copy)

    widen(NS)

    def local_token(t, carried):
        so_far, states = carried
        rows = pl.ds(pl.multiple_of(t * SUB, SUB), SUB)
        drive = drives[rows, :]
        passed = []
        result = []
        total = None
        for n in range(NS):
            decay = decays[t, pl.ds(n * SUB, SUB), :]
            b = spread[pl.ds(n * TOK + t, SUB, stride=0), :]
            weight = spread[pl.ds((NS + n) * TOK + t, SUB, stride=0), :]
            new = decay * states[n] + b * drive
            result.append(new)
            total = weight * new if total is None else total + weight * new
            left = so_far[n] * decay
            passed.append(left)
            gains[t, pl.ds(n * SUB, SUB), :] = weight * left
        ys[rows, :] = total
        return tuple(passed), tuple(result)

    carried = ((jnp.ones((SUB, LANE), F32),) * NS, (zero,) * NS)
    cuts = (0, 40, 144, TOK)
    carried = lax.fori_loop(cuts[0], cuts[1], local_token, carried, unroll=2)

    pair_copy.wait_recv()
    own_state, own_total = unpack(st_own)
    other_state, other_total = unpack(st_pair)
    first_core = c == 0
    early = [jnp.where(first_core, p, q) for p, q in zip(own_state, other_state)]
    late = [jnp.where(first_core, q, p) for p, q in zip(own_state, other_state)]
    late_total = jnp.where(first_core, other_total, own_total)
    chip_state = follow(early, late, late_total)
    pack(st_y.at[0], chip_state, own_total + other_total)
    level = []
    for k in range(1, NY):
        copy = remote(
            st_y.at[0], st_y.at[k], st_send.at[k], st_recv.at[k], (x, lax.rem(y + k, NY), c, z)
        )
        copy.start()
        level.append(copy)
    sends += level
    carried = lax.fori_loop(cuts[1], cuts[2], local_token, carried, unroll=2)

    for copy in level:
        copy.wait_recv()
    column, column_total = unpack(st_y.at[lax.rem(y + NY, NY)])
    for j in range(1, NY):
        block, total = unpack(st_y.at[lax.rem(y + NY - j, NY)])
        column = follow(column, block, total)
        column_total = column_total + total
    pack(st_x.at[0], column, column_total)
    level = []
    for k in range(1, NX):
        copy = remote(
            st_x.at[0], st_x.at[k], st_send.at[4 + k], st_recv.at[4 + k], (lax.rem(x + k, NX), y, c, z)
        )
        copy.start()
        level.append(copy)
    sends += level
    carried = lax.fori_loop(cuts[2], cuts[3], local_token, carried, unroll=2)

    for b in range(1, NY):
        for a in range(NX):
            index = b * NX + a
            wait_kv(rows_of(-a, -b, c), index)
            block = kv_out.at[rows_of(-a, -b, c)]
            copy = remote(block, block, kv_send.at[16 + index], kv_recv.at[16 + index], partner)
            copy.start()
            sends.append(copy)

    for copy in level:
        copy.wait_recv()
    entering = [zero] * NS
    for j in range(NX - 1):
        block, total = unpack(st_x.at[lax.rem(x + NX - j, NX)])
        entering = follow(entering, block, total, x > j)
    for j in range(NY - 1):
        block, total = unpack(st_y.at[lax.rem(y + NY - j, NY)])
        entering = follow(entering, block, total, y > j)
    entering = follow(entering, early, jnp.where(first_core, own_total, other_total), c > 0)

    def correct(t, carry):
        rows = pl.ds(pl.multiple_of(t * SUB, SUB), SUB)
        total = ys[rows, :]
        for n in range(NS):
            total = total + gains[t, pl.ds(n * SUB, SUB), :] * entering[n]
        ys[rows, :] = total
        return carry

    lax.fori_loop(0, TOK, correct, 0, unroll=4)
    load_z.wait()
    for j in range(SUB):
        cols = pl.ds(j * LANE, LANE)
        scanned = ys[pl.ds(j, TOK, stride=SUB), :]
        scanned = scanned + skip_ref[:, cols] * inner[:, cols].astype(F32)
        out[:, cols] = (scanned * silu(z_ref[:, cols].astype(F32))).astype(BF16)

    for k in range(1, NSEQ):
        rows = pl.ds(pl.multiple_of(lax.rem(me + NSEQ - k, NSEQ) * RUN, RUN), RUN)
        remote(qs.at[0], q_out.at[rows], q_send.at[k], q_recv.at[k], partner).wait_recv()
    for b in range(NY):
        for a in range(NX):
            wait_kv(rows_of(-a, -b, 1 - c), 16 + b * NX + a)
    for copy in sends:
        copy.wait_send()
    keep_kv.wait()
    keep_q.wait()


def mix(dest, lengths, q, k, v, x, z, cw, cb, xw, dtw, dtb, rate, skip):
    dma = pltpu.SemaphoreType.DMA
    states = ((NS + 2) * SUB, LANE)
    chunk = (TOK // NZ, PROJ)
    return pl.pallas_call(
        mixer_kernel,
        out_shape=(
            jax.ShapeDtypeStruct((TOK, CH), BF16),
            jax.ShapeDtypeStruct((NSEQ * TOK, 2 * HD), BF16),
            jax.ShapeDtypeStruct((TOKENS // LANE, LANE), jnp.int32),
            jax.ShapeDtypeStruct((TOK, CH), BF16),
        ),
        in_specs=[
            whole(),
            whole(pltpu.SMEM),
            whole(),
            whole(pl.ANY),
            whole(),
            whole(),
            whole(pl.ANY),
            whole(),
            whole(),
            whole(pl.ANY),
            whole(pl.ANY),
        ]
        + [whole()] * 3,
        out_specs=(whole(pl.ANY), whole(pl.ANY), whole(), whole()),
        scratch_shapes=[
            VM((TOK, 2 * HD), BF16),
            VM((NSEQ, RUN, CH), BF16),
            VM((16, CH), BF16),
            VM((TOK + 8, CH), F32),
            VM((TOK, CH), BF16),
            VM((NZ, *chunk), BF16),
            VM((5, *chunk), BF16),
            VM((4, *chunk), BF16),
            VM((5, *chunk), BF16),
            VM((4, *chunk), BF16),
            VM((TOK, PROJ), BF16),
            VM((TOK * SUB, LANE), F32),
            VM((TOK * SUB, LANE), F32),
            VM((NS * SUB, LANE), F32),
            VM((2 * NS * TOK, LANE), F32),
            VM((TOK, NS * SUB, LANE), F32),
            VM((TOK * SUB, LANE), F32),
            VM((SUB, LANE), F32),
            VM(states, BF16),
            VM(states, BF16),
            VM((NY, *states), BF16),
            VM((NX, *states), BF16),
            VM((TOK, NS * SUB, LANE), F32),
            VM((TOK, CH), BF16),
            VM((PROJ, CH), BF16),
            VM((RANK, CH), BF16),
            dma((5,)),
            dma((2,)),
            dma((32,)),
            dma((32,)),
            dma((NSEQ,)),
            dma((NSEQ,)),
            dma((NZ,)),
            dma((NZ,)),
            dma((NZ,)),
            dma((NZ,)),
            dma((NZ,)),
            dma((NZ,)),
        ],
        compiler_params=pltpu.CompilerParams(
            collective_id=0, has_side_effects=True, vmem_limit_bytes=VLIM
        ),
        name="mixer",
    )(dest, lengths, q, k, v, x, z, cw, cb, xw, dtw, dtb, rate, skip)


def attend_kernel(pos_ref, len_ref, q_ref, kv_ref, out, scores_a, scores_b):
    g = pl.program_id(0)
    heads = CH // HD
    rows = GROUP * RUN
    count = heads * rows
    wide = 2 * BK
    per = TOK * GROUP // wide
    starts = doc_starts(len_ref)
    halves = TOK // LANE
    bases = [
        sum(pos_ref[(g * GROUP + i) * halves + j, 0] for j in range(halves)) for i in range(GROUP)
    ]
    lane = lax.broadcasted_iota(jnp.int32, (1, LANE), 1) % rows
    base = bases[0]
    for i in range(1, GROUP):
        base = jnp.where(lane >= i * RUN, bases[i], base)
    pos = base + lane % RUN
    start = start_of(pos, starts)
    top = g * per
    first = jnp.minimum(start_of(bases[0], starts) // wide, top)
    last_start = start_of(bases[GROUP - 1] + RUN - 1, starts)
    plain = jnp.maximum(jnp.minimum((last_start + wide - 1) // wide, top), first)
    q = jnp.concatenate([q_ref[:, h * HD : (h + 1) * HD] for h in range(heads)], axis=0)
    scale = HD**-0.5 * LOG2E
    key_row = lax.broadcasted_iota(jnp.int32, (BK, LANE), 0)
    ones = jnp.ones((16, BK), BF16)

    def score(into, i):
        keys = kv_ref[pl.ds(pl.multiple_of(i * BK, BK), BK), pl.ds(0, HD)]
        into[...] = lax.dot_general(
            keys, q, (((1,), (1,)), ((), ())), preferred_element_type=F32
        )

    def absorb(taken, i, carried, masked):
        begin = pl.multiple_of(i * BK, BK)
        best, summed = carried
        scores = taken[...]
        if masked:
            visible = (key_row <= pos - begin) & (key_row >= start - begin)
            scores = jnp.concatenate(
                [
                    jnp.where(visible, scores[:, j : j + LANE], MASKED)
                    for j in range(0, count, LANE)
                ],
                axis=1,
            )
        new_best = jnp.maximum(best, jnp.max(scores, axis=0, keepdims=True) * scale)
        weights = jnp.exp2(scores * scale - new_best).astype(BF16)
        rescale = jnp.exp2(best - new_best)
        values = jnp.concatenate(
            [kv_ref[pl.ds(begin + j, HD), pl.ds(HD, HD)] for j in range(0, BK, HD)], axis=1
        )
        values = jnp.concatenate([values, ones], axis=0)
        product = jnp.dot(values, weights, preferred_element_type=F32)
        return new_best, summed * rescale + product

    def pair(i, carried, masked, more=True):
        score(scores_b, 2 * i + 1)
        carried = absorb(scores_a, 2 * i, carried, masked)
        if more:
            score(scores_a, 2 * i + 2)
        return absorb(scores_b, 2 * i + 1, carried, masked)

    carried = (jnp.full((1, count), MASKED * scale, F32), jnp.zeros((HD + 16, count), F32))
    score(scores_a, 2 * first)
    carried = lax.fori_loop(first, plain, lambda i, v: pair(i, v, True), carried)
    carried = lax.fori_loop(plain, top, lambda i, v: pair(i, v, False), carried)
    for i in range(per):
        carried = pair(top + i, carried, True, i < per - 1)
    summed = carried[1]
    result = (summed[:HD] / summed[HD : HD + 1]).T.astype(BF16)
    for h in range(heads):
        out[:, h * HD : (h + 1) * HD] = result[h * rows : (h + 1) * rows]


def attend(positions, lengths, q, kv):
    rows = GROUP * RUN
    return pl.pallas_call(
        attend_kernel,
        out_shape=jax.ShapeDtypeStruct((TOK, CH), BF16),
        grid=(NSEQ // GROUP,),
        in_specs=[
            whole(pltpu.SMEM),
            whole(pltpu.SMEM),
            pl.BlockSpec((rows, CH), lambda g: (g, 0)),
            whole(),
        ],
        out_specs=pl.BlockSpec((rows, CH), lambda g: (g, 0)),
        scratch_shapes=[VM((BK, CH // HD * rows), F32)] * 2,
        compiler_params=pltpu.CompilerParams(vmem_limit_bytes=VLIM),
        name="attend",
    )(positions, lengths, q, kv)


def local(
    x_branch,
    z_branch,
    conv_weight,
    conv_bias,
    xproj_weight,
    dt_weight,
    dt_bias,
    decay_rate,
    skip_gain,
    query_rows,
    key_rows,
    value_rows,
    lengths,
    destination,
):
    q, kv, positions, mamba_out = mix(
        destination.reshape(TOKENS // LANE, LANE),
        lengths,
        query_rows,
        key_rows,
        value_rows,
        x_branch,
        z_branch,
        conv_weight,
        conv_bias.reshape(1, CH),
        xproj_weight.T,
        dt_weight,
        dt_bias.reshape(1, CH),
        decay_rate,
        skip_gain.reshape(1, CH),
    )
    regrouped = attend(positions, lengths, q, kv)
    return (mamba_out, regrouped)


def solution(mesh):
    torus = Mesh(mesh.devices.reshape(NX, NY, NC, mesh.shape["mp"]), (*SEQ, "mp"))
    in_specs = (
        P(SEQ, "mp"),
        P(SEQ, "mp"),
        P(None, "mp"),
        P("mp"),
        P("mp", None),
        P(None, "mp"),
        P("mp"),
        P(None, "mp"),
        P("mp"),
        P(SEQ, "mp"),
        P(SEQ, "mp"),
        P(SEQ, "mp"),
        P(),
        P(),
    )
    out_specs = (P(SEQ, "mp"), P(SEQ, "mp"))
    return jax.shard_map(local, mesh=torus, in_specs=in_specs, out_specs=out_specs, check_vma=False)
```

```python
import math

import jax
import jax.numpy as jnp
from jax import lax
from jax.experimental import pallas as pl
from jax.experimental.pallas import tpu as pltpu
from jax.sharding import Mesh
from jax.sharding import PartitionSpec as P

SEQ = ("seq_0", "seq_1", "seq_2")
MESH = pl.DeviceIdType.MESH
VM = pltpu.VMEM
F32 = jnp.float32
BF16 = jnp.bfloat16
LOG2E = math.log2(math.e)
NX, NY, NC, NZ = 4, 4, 2, 8
NSEQ = NX * NY * NC
TOK = 256
TOK_BITS = 8
TOKENS = NSEQ * TOK
CH = 1024
LANE = 128
SUB = CH // LANE
NS = 16
RANK = 512
PROJ = RANK + 2 * NS
HD = 128
TAPS = 4
HALVES = 2
BIG_STEP = 1.0e7
MASKED = -1.0e30
GROUP = 8
RUN = TOK // NSEQ
BK = 512
VLIM = 60 * 1024 * 1024


def whole(space=VM):
    return pl.BlockSpec(memory_space=space)


def place():
    return (
        lax.axis_index("seq_0"),
        lax.axis_index("seq_1"),
        lax.axis_index("seq_2"),
        lax.axis_index("mp"),
    )


def seq_device(j, z):
    chip = lax.div(j, NC)
    return (lax.div(chip, NY), lax.rem(chip, NY), lax.rem(j, NC), z)


def doc_starts(len_ref):
    s1 = len_ref[0]
    s2 = s1 + len_ref[1]
    return s1, s2, s2 + len_ref[2]


def start_of(pos, starts):
    s1, s2, s3 = starts
    return jnp.where(pos >= s3, s3, jnp.where(pos >= s2, s2, jnp.where(pos >= s1, s1, 0)))


def silu(x):
    half = 0.5 * x
    return half * jnp.tanh(half) + half


def mixer_kernel(
    dest_ref,
    len_ref,
    q_ref,
    k_ref,
    v_ref,
    x_ref,
    z_hbm,
    cw_ref,
    cb_ref,
    xw_hbm,
    dtw_hbm,
    dtb_ref,
    rate_ref,
    skip_ref,
    q_out,
    kv_out,
    pos_out,
    out,
    kvs,
    qs,
    halo,
    ext,
    inner,
    part,
    rs_plus,
    rs_minus,
    go_plus,
    go_minus,
    proj,
    steps,
    drives,
    rates,
    spread,
    gains,
    ys,
    sums,
    st_own,
    st_pair,
    st_y,
    st_x,
    decays,
    gates,
    z_ref,
    xw_ref,
    dtw_ref,
    loc_sem,
    halo_sem,
    kv_send,
    kv_recv,
    q_send,
    q_recv,
    rs_send,
    rs_recv,
    ag_send,
    ag_recv,
    st_send,
    st_recv,
):
    x, y, c, z = place()
    me = (x * NY + y) * NC + c
    anchor = me * TOK
    barrier = pltpu.get_barrier_semaphore()
    for k in range(1, NSEQ):
        pl.semaphore_signal(
            barrier, inc=1, device_id=seq_device(lax.rem(me + k, NSEQ), z), device_id_type=MESH
        )
    for k in range(1, NZ):
        pl.semaphore_signal(
            barrier, inc=1, device_id=(x, y, c, lax.rem(z + k, NZ)), device_id_type=MESH
        )
    load_k = pltpu.make_async_copy(k_ref, kvs.at[:, pl.ds(0, HD)], loc_sem.at[0])
    load_k.start()
    load_x = pltpu.make_async_copy(xw_hbm, xw_ref, loc_sem.at[2])
    load_x.start()
    load_d = pltpu.make_async_copy(dtw_hbm, dtw_ref, loc_sem.at[3])
    load_d.start()
    load_z = pltpu.make_async_copy(z_hbm, z_ref, loc_sem.at[4])
    load_z.start()
    starts = doc_starts(len_ref)
    token = anchor + lax.broadcasted_iota(jnp.int32, (TOK, LANE), 0)
    depth = token - start_of(token, starts)

    def convolve(count, cols, far):
        total = cb_ref[:, cols] + cw_ref[pl.ds(0, 1), cols] * ext[pl.ds(8, count), cols]
        for lag in range(1, TAPS):
            window = ext[pl.ds(8 - lag, count), cols]
            total = total + cw_ref[pl.ds(lag, 1), cols] * jnp.where(far >= lag, window, 0.0)
        inner[pl.ds(0, count), cols] = silu(total).astype(BF16)

    def conv_columns(i, carry):
        cols = pl.ds(pl.multiple_of(i * LANE, LANE), LANE)
        ext[pl.ds(0, 8), cols] = jnp.zeros((8, LANE), F32)
        ext[pl.ds(8, TOK), cols] = x_ref[:, cols].astype(F32)
        convolve(TOK, cols, depth)
        return carry

    lax.fori_loop(0, SUB, conv_columns, 0)
    pl.semaphore_wait(barrier, NSEQ - 1 + NZ - 1)

    def remote(src, dst, send, recv, device):
        return pltpu.make_async_remote_copy(
            src_ref=src,
            dst_ref=dst,
            send_sem=send,
            recv_sem=recv,
            device_id=device,
            device_id_type=MESH,
        )

    def offset(a, b, core):
        a, b = a % NX, b % NY
        return (
            lax.rem(x + a * (1 - core) + b * core, NX),
            lax.rem(y + a * core + b * (1 - core), NY),
        )

    def rows_of(a, b, core):
        px, py = offset(a, b, core)
        return pl.ds(pl.multiple_of(((px * NY + py) * NC + core) * TOK, TOK), TOK)

    partner = (x, y, 1 - c, z)
    after = lax.rem(me + 1, NSEQ)
    halo_copy = remote(
        x_ref.at[pl.ds(TOK - 16, 16)], halo, halo_sem.at[0], halo_sem.at[1], seq_device(after, z)
    )
    halo_copy.start()
    for half in range(TOK // HD):
        kvs[pl.ds(half * HD, HD), pl.ds(HD, HD)] = v_ref[pl.ds(half * HD, HD), :].T

    halves = TOK // LANE
    goal = lax.shift_right_logical(dest_ref[pl.ds(me * halves, halves), :], TOK_BITS) * RUN
    goal = goal + lax.broadcasted_iota(jnp.int32, (halves, LANE), 1) % RUN
    slot = lax.broadcasted_iota(jnp.int32, (TOK, LANE), 0)
    choice = jnp.concatenate(
        [jnp.where(slot == goal[i : i + 1], 1.0, 0.0) for i in range(halves)], axis=1
    )
    staged = jnp.dot(choice.astype(BF16), q_ref[...], preferred_element_type=F32)
    qs[...] = staged.astype(BF16).reshape(NSEQ, RUN, CH)
    load_k.wait()
    mine = kv_out.at[rows_of(0, 0, c)]
    sends = []
    for a in range(1, NX):
        px, py = offset(a, 0, c)
        copy = remote(kvs, mine, kv_send.at[a], kv_recv.at[a], (px, py, c, z))
        copy.start()
        sends.append(copy)
    copy = remote(kvs, mine, kv_send.at[16], kv_recv.at[16], partner)
    copy.start()
    sends.append(copy)
    keep_kv = pltpu.make_async_copy(kvs, mine, loc_sem.at[0])
    keep_kv.start()
    q_rows = pl.ds(pl.multiple_of(me * RUN, RUN), RUN)
    for k in range(1, NSEQ):
        j = lax.rem(me + k, NSEQ)
        copy = remote(qs.at[j], q_out.at[q_rows], q_send.at[k], q_recv.at[k], seq_device(j, z))
        copy.start()
        sends.append(copy)
    keep_q = pltpu.make_async_copy(qs.at[me], q_out.at[q_rows], loc_sem.at[1])
    keep_q.start()

    halo_copy.wait()
    ext[pl.ds(0, 8), :] = halo[pl.ds(8, 8), :].astype(F32)
    near = anchor + lax.broadcasted_iota(jnp.int32, (16, CH), 0)
    convolve(16, pl.ds(0, CH), near - start_of(near, starts))

    load_x.wait()
    partial = lax.dot_general(
        inner[...], xw_ref[...], (((1,), (1,)), ((), ())), preferred_element_type=F32
    ).astype(BF16)
    slice_rows = TOK // NZ
    part_rows = slice_rows // HALVES
    part[...] = partial.reshape(NZ, HALVES, part_rows, PROJ)
    up = (x, y, c, lax.rem(z + 1, NZ))
    down = (x, y, c, lax.rem(z + NZ - 1, NZ))

    def ring_plus(s, h):
        src = part.at[lax.rem(z + 4, NZ), h] if s == 1 else go_plus.at[s, h]
        index = h * NZ + s
        return remote(src, rs_plus.at[s, h], rs_send.at[index], rs_recv.at[index], up)

    def ring_minus(s, h):
        src = part.at[lax.rem(z + 5, NZ), h] if s == 1 else go_minus.at[s, h]
        index = h * NZ + 4 + s
        return remote(src, rs_minus.at[s, h], rs_send.at[index], rs_recv.at[index], down)

    def begin(copy):
        copy.start()
        sends.append(copy)
        return copy

    plus, minus = [], []
    for h in range(HALVES):
        plus.append(begin(ring_plus(1, h)))
        minus.append(begin(ring_minus(1, h)))

    def wait_kv(slot_rows, index):
        remote(kvs, kv_out.at[slot_rows], kv_send.at[0], kv_recv.at[index], partner).wait_recv()

    for s in range(1, 4):
        for h in range(HALVES):
            plus[h].wait_recv()
            ours = part[lax.rem(z + 4 - s, NZ), h].astype(F32)
            go_plus[s + 1, h] = (rs_plus[s, h].astype(F32) + ours).astype(BF16)
            plus[h] = begin(ring_plus(s + 1, h))
            minus[h].wait_recv()
            if s < 3:
                ours = part[lax.rem(z + 5 + s, NZ), h].astype(F32)
                go_minus[s + 1, h] = (rs_minus[s, h].astype(F32) + ours).astype(BF16)
                minus[h] = begin(ring_minus(s + 1, h))
        if s == 2:
            for a in range(NX):
                if a > 0:
                    wait_kv(rows_of(-a, 0, c), a)
                block = kv_out.at[rows_of(-a, 0, c)] if a > 0 else kvs
                target = kv_out.at[rows_of(-a, 0, c)]
                for b in range(1, NY):
                    px, py = offset(0, b, c)
                    index = b * NX + a
                    copy = remote(
                        block, target, kv_send.at[index], kv_recv.at[index], (px, py, c, z)
                    )
                    copy.start()
                    sends.append(copy)
                if a > 0:
                    copy = remote(
                        block, target, kv_send.at[16 + a], kv_recv.at[16 + a], partner
                    )
                    copy.start()
                    sends.append(copy)

    def proj_rows(chunk, h):
        first = lax.rem(chunk, NZ) * slice_rows + h * part_rows
        return pl.ds(pl.multiple_of(first, part_rows), part_rows)

    def pass_plus(s, h):
        rows = proj.at[proj_rows(z + NZ + 1 - s, h)]
        index = h * NZ + s
        return remote(rows, rows, ag_send.at[index], ag_recv.at[index], up)

    def pass_minus(s, h):
        rows = proj.at[proj_rows(z + s - 1, h)]
        index = h * NZ + 4 + s
        return remote(rows, rows, ag_send.at[index], ag_recv.at[index], down)

    def got_plus(s, h):
        rows = proj.at[proj_rows(z + NZ - s, h)]
        index = h * NZ + s
        remote(rows, rows, ag_send.at[index], ag_recv.at[index], up).wait_recv()

    def got_minus(s, h):
        rows = proj.at[proj_rows(z + s, h)]
        index = h * NZ + 4 + s
        remote(rows, rows, ag_send.at[index], ag_recv.at[index], down).wait_recv()

    for h in range(HALVES):
        plus[h].wait_recv()
        total = part[z, h].astype(F32) + rs_plus[4, h].astype(F32) + rs_minus[3, h].astype(F32)
        proj[proj_rows(z, h), :] = total.astype(BF16)
        begin(pass_plus(1, h))
        begin(pass_minus(1, h))
    for s in range(2, 5):
        for h in range(HALVES):
            got_plus(s - 1, h)
            begin(pass_plus(s, h))
            if s < 4:
                got_minus(s - 1, h)
                begin(pass_minus(s, h))
    spots = (TOKENS // LANE, LANE)
    spot = lax.broadcasted_iota(jnp.int32, spots, 1)
    ours = (lax.shift_right_logical(dest_ref[...], TOK_BITS) == me) & (spot % RUN == 0)
    spot = spot + LANE * lax.broadcasted_iota(jnp.int32, spots, 0)
    found = jnp.sum(jnp.where(ours, spot, 0).astype(F32), axis=1, keepdims=True)
    pos_out[...] = jnp.broadcast_to(found, spots).astype(jnp.int32)
    for j in range(SUB):
        cols = pl.ds(j * LANE, LANE)
        rates[pl.ds(j, NS, stride=SUB), :] = rate_ref[:, cols] * (-LOG2E)
    for h in range(HALVES):
        got_minus(3, h)
        got_plus(4, h)

    load_d.wait()
    begins = depth == 0
    low = proj[:, pl.ds(0, RANK)]
    for j in range(SUB):
        cols = pl.ds(j * LANE, LANE)
        if j % 2 == 0:
            both = pl.ds(j * LANE, 2 * LANE)
            raw = jnp.dot(low, dtw_ref[:, both], preferred_element_type=F32)
        value = raw[:, j % 2 * LANE : (j % 2 + 1) * LANE] + dtb_ref[:, cols]
        fade = jnp.exp2(jnp.abs(value) * (-LOG2E))
        series = fade - (0.5 * fade) * fade
        tail = jnp.where(fade < 1.0e-3, series, jnp.log(1.0 + fade))
        step = jnp.maximum(value, 0.0) + tail
        drives[pl.ds(j, TOK, stride=SUB), :] = step * inner[:, cols].astype(F32)
        step = jnp.where(begins, BIG_STEP, step)
        sums[pl.ds(j, 1), :] = jnp.sum(step, axis=0, keepdims=True)
        steps[pl.ds(j, TOK, stride=SUB), :] = step

    def widen(first):
        row = lax.broadcasted_iota(jnp.int32, (2 * NS, NS * LANE), 0)
        col = lax.broadcasted_iota(jnp.int32, (2 * NS, NS * LANE), 1)
        pick = jnp.where(lax.div(col, LANE) + first == row, 1.0, 0.0).astype(BF16)
        wide = jnp.dot(proj[:, pl.ds(RANK, 2 * NS)], pick, preferred_element_type=F32)
        for n in range(NS):
            spread[pl.ds((first + n) * TOK, TOK), :] = wide[:, n * LANE : (n + 1) * LANE]

    widen(0)
    rate = [rates[pl.ds(n * SUB, SUB), :] for n in range(NS)]

    def advance(t, carried):
        rows = pl.ds(pl.multiple_of(t * SUB, SUB), SUB)
        step = steps[rows, :]
        drive = drives[rows, :]
        result = []
        for n in range(NS):
            b = spread[pl.ds(n * TOK + t, SUB, stride=0), :]
            decay = jnp.exp2(step * rate[n])
            decays[t, pl.ds(n * SUB, SUB), :] = decay
            result.append(decay * carried[n] + b * drive)
        return tuple(result)

    zero = jnp.zeros((SUB, LANE), F32)
    state = lax.fori_loop(0, TOK, advance, (zero,) * NS, unroll=4)

    def pack(into, states, total):
        for n in range(0, NS, 2):
            pair = jnp.concatenate([states[n], states[n + 1]], axis=0)
            into[pl.ds(n * SUB, 2 * SUB), :] = pair.astype(BF16)
        high = total.astype(BF16).astype(F32)
        pair = jnp.concatenate([high, total - high], axis=0)
        into[pl.ds(NS * SUB, 2 * SUB), :] = pair.astype(BF16)

    def unpack(taken):
        block = taken[...].astype(F32).reshape(NS + 2, SUB, LANE)
        return [block[n] for n in range(NS)], block[NS] + block[NS + 1]

    def follow(states, block, total, passed=None):
        result = []
        for n in range(NS):
            moved = jnp.exp2(rate[n] * total) * states[n] + block[n]
            result.append(moved if passed is None else jnp.where(passed, moved, states[n]))
        return result

    pack(st_own, state, sums[...])
    pair_copy = remote(st_own, st_pair, st_send.at[0], st_recv.at[0], partner)
    pair_copy.start()
    sends.append(pair_copy)

    widen(NS)

    def local_token(t, carried):
        so_far, states = carried
        rows = pl.ds(pl.multiple_of(t * SUB, SUB), SUB)
        drive = drives[rows, :]
        passed = []
        result = []
        total = None
        for n in range(NS):
            decay = decays[t, pl.ds(n * SUB, SUB), :]
            b = spread[pl.ds(n * TOK + t, SUB, stride=0), :]
            weight = spread[pl.ds((NS + n) * TOK + t, SUB, stride=0), :]
            new = decay * states[n] + b * drive
            result.append(new)
            total = weight * new if total is None else total + weight * new
            left = so_far[n] * decay
            passed.append(left)
            gains[t, pl.ds(n * SUB, SUB), :] = weight * left
        ys[rows, :] = total
        return tuple(passed), tuple(result)

    carried = ((jnp.ones((SUB, LANE), F32),) * NS, (zero,) * NS)
    cuts = (0, 40, 144, TOK)
    carried = lax.fori_loop(cuts[0], cuts[1], local_token, carried, unroll=2)

    pair_copy.wait_recv()
    own_state, own_total = unpack(st_own)
    other_state, other_total = unpack(st_pair)
    first_core = c == 0
    early = [jnp.where(first_core, p, q) for p, q in zip(own_state, other_state)]
    late = [jnp.where(first_core, q, p) for p, q in zip(own_state, other_state)]
    late_total = jnp.where(first_core, other_total, own_total)
    chip_state = follow(early, late, late_total)
    pack(st_y.at[0], chip_state, own_total + other_total)
    level = []
    for k in range(1, NY):
        copy = remote(
            st_y.at[0], st_y.at[k], st_send.at[k], st_recv.at[k], (x, lax.rem(y + k, NY), c, z)
        )
        copy.start()
        level.append(copy)
    sends += level
    carried = lax.fori_loop(cuts[1], cuts[2], local_token, carried, unroll=2)

    for copy in level:
        copy.wait_recv()
    column, column_total = unpack(st_y.at[lax.rem(y + NY, NY)])
    for j in range(1, NY):
        block, total = unpack(st_y.at[lax.rem(y + NY - j, NY)])
        column = follow(column, block, total)
        column_total = column_total + total
    pack(st_x.at[0], column, column_total)
    level = []
    for k in range(1, NX):
        copy = remote(
            st_x.at[0], st_x.at[k], st_send.at[4 + k], st_recv.at[4 + k], (lax.rem(x + k, NX), y, c, z)
        )
        copy.start()
        level.append(copy)
    sends += level
    carried = lax.fori_loop(cuts[2], cuts[3], local_token, carried, unroll=2)

    for b in range(1, NY):
        for a in range(NX):
            index = b * NX + a
            wait_kv(rows_of(-a, -b, c), index)
            block = kv_out.at[rows_of(-a, -b, c)]
            copy = remote(block, block, kv_send.at[16 + index], kv_recv.at[16 + index], partner)
            copy.start()
            sends.append(copy)

    load_z.wait()
    for j in range(SUB):
        cols = pl.ds(j * LANE, LANE)
        gates[:, cols] = silu(z_ref[:, cols].astype(F32))
        inner_gain = skip_ref[:, cols] * inner[:, cols].astype(F32)
        kept = ys[pl.ds(j, TOK, stride=SUB), :]
        ys[pl.ds(j, TOK, stride=SUB), :] = kept + inner_gain
    for copy in level:
        copy.wait_recv()
    entering = [zero] * NS
    for j in range(NX - 1):
        block, total = unpack(st_x.at[lax.rem(x + NX - j, NX)])
        entering = follow(entering, block, total, x > j)
    for j in range(NY - 1):
        block, total = unpack(st_y.at[lax.rem(y + NY - j, NY)])
        entering = follow(entering, block, total, y > j)
    entering = follow(entering, early, jnp.where(first_core, own_total, other_total), c > 0)

    def correct(t, carry):
        rows = pl.ds(pl.multiple_of(t * SUB, SUB), SUB)
        total = ys[rows, :]
        for n in range(NS):
            total = total + gains[t, pl.ds(n * SUB, SUB), :] * entering[n]
        ys[rows, :] = total
        return carry

    lax.fori_loop(0, TOK, correct, 0, unroll=4)
    for j in range(SUB):
        cols = pl.ds(j * LANE, LANE)
        out[:, cols] = (ys[pl.ds(j, TOK, stride=SUB), :] * gates[:, cols]).astype(BF16)

    for k in range(1, NSEQ):
        rows = pl.ds(pl.multiple_of(lax.rem(me + NSEQ - k, NSEQ) * RUN, RUN), RUN)
        remote(qs.at[0], q_out.at[rows], q_send.at[k], q_recv.at[k], partner).wait_recv()
    for b in range(NY):
        for a in range(NX):
            wait_kv(rows_of(-a, -b, 1 - c), 16 + b * NX + a)
    for copy in sends:
        copy.wait_send()
    keep_kv.wait()
    keep_q.wait()


def mix(dest, lengths, q, k, v, x, z, cw, cb, xw, dtw, dtb, rate, skip):
    dma = pltpu.SemaphoreType.DMA
    states = ((NS + 2) * SUB, LANE)
    chunk = (HALVES, TOK // NZ // HALVES, PROJ)
    return pl.pallas_call(
        mixer_kernel,
        out_shape=(
            jax.ShapeDtypeStruct((TOK, CH), BF16),
            jax.ShapeDtypeStruct((NSEQ * TOK, 2 * HD), BF16),
            jax.ShapeDtypeStruct((TOKENS // LANE, LANE), jnp.int32),
            jax.ShapeDtypeStruct((TOK, CH), BF16),
        ),
        in_specs=[
            whole(),
            whole(pltpu.SMEM),
            whole(),
            whole(pl.ANY),
            whole(),
            whole(),
            whole(pl.ANY),
            whole(),
            whole(),
            whole(pl.ANY),
            whole(pl.ANY),
        ]
        + [whole()] * 3,
        out_specs=(whole(pl.ANY), whole(pl.ANY), whole(), whole()),
        scratch_shapes=[
            VM((TOK, 2 * HD), BF16),
            VM((NSEQ, RUN, CH), BF16),
            VM((16, CH), BF16),
            VM((TOK + 8, CH), F32),
            VM((TOK, CH), BF16),
            VM((NZ, *chunk), BF16),
            VM((5, *chunk), BF16),
            VM((4, *chunk), BF16),
            VM((5, *chunk), BF16),
            VM((4, *chunk), BF16),
            VM((TOK, PROJ), BF16),
            VM((TOK * SUB, LANE), F32),
            VM((TOK * SUB, LANE), F32),
            VM((NS * SUB, LANE), F32),
            VM((2 * NS * TOK, LANE), F32),
            VM((TOK, NS * SUB, LANE), F32),
            VM((TOK * SUB, LANE), F32),
            VM((SUB, LANE), F32),
            VM(states, BF16),
            VM(states, BF16),
            VM((NY, *states), BF16),
            VM((NX, *states), BF16),
            VM((TOK, NS * SUB, LANE), F32),
            VM((TOK, CH), F32),
            VM((TOK, CH), BF16),
            VM((PROJ, CH), BF16),
            VM((RANK, CH), BF16),
            dma((5,)),
            dma((2,)),
            dma((32,)),
            dma((32,)),
            dma((NSEQ,)),
            dma((NSEQ,)),
            dma((HALVES * NZ,)),
            dma((HALVES * NZ,)),
            dma((HALVES * NZ,)),
            dma((HALVES * NZ,)),
            dma((NZ,)),
            dma((NZ,)),
        ],
        compiler_params=pltpu.CompilerParams(
            collective_id=0, has_side_effects=True, vmem_limit_bytes=VLIM
        ),
        name="mixer",
    )(dest, lengths, q, k, v, x, z, cw, cb, xw, dtw, dtb, rate, skip)


def attend_kernel(pos_ref, len_ref, q_ref, kv_hbm, out, scores_a, scores_b, kv_ref, sems):
    g = pl.program_id(0)
    heads = CH // HD
    rows = GROUP * RUN
    count = heads * rows
    half = count // 2
    half_rows = rows // 2
    wide = 2 * BK
    span = TOK * GROUP
    halves = TOK // LANE

    def load(i):
        part = pl.ds(pl.multiple_of(i * span, span), span)
        return pltpu.make_async_copy(kv_hbm.at[part], kv_ref.at[part], sems.at[i])

    @pl.when(g == 0)
    def _():
        for i in range(NSEQ // GROUP):
            load(i).start()

    starts = doc_starts(len_ref)
    bases = [
        sum(pos_ref[(g * GROUP + i) * halves + j, 0] for j in range(halves)) for i in range(GROUP)
    ]
    lane = lax.broadcasted_iota(jnp.int32, (1, LANE), 1) % half_rows

    def lanes(firsts):
        base = firsts[0]
        for i in range(1, GROUP // 2):
            base = jnp.where(lane >= i * RUN, firsts[i], base)
        pos = base + lane % RUN
        return pos, start_of(pos, starts)

    bounds = (lanes(bases[: GROUP // 2]), lanes(bases[GROUP // 2 :]))
    top = g * (span // wide)
    first = jnp.minimum(lax.div(start_of(bases[0], starts), wide), top)
    last_start = start_of(bases[GROUP - 1] + RUN - 1, starts)
    plain = jnp.maximum(jnp.minimum(lax.div(last_start + wide - 1, wide), top), first)
    q = jnp.concatenate(
        [
            q_ref[i * half_rows : (i + 1) * half_rows, h * HD : (h + 1) * HD]
            for i in range(2)
            for h in range(heads)
        ],
        axis=0,
    )
    scale = HD**-0.5 * LOG2E
    key_row = lax.broadcasted_iota(jnp.int32, (BK, LANE), 0)
    ones = jnp.ones((16, BK), BF16)

    def score(into, i, low=0):
        keys = kv_ref[pl.ds(pl.multiple_of(i * BK, BK), BK), pl.ds(0, HD)]
        into[:, low:count] = lax.dot_general(
            keys, q[low:], (((1,), (1,)), ((), ())), preferred_element_type=F32
        )

    def absorb(taken, i, carried, masked, low=0):
        begin = pl.multiple_of(i * BK, BK)
        best, summed = carried
        scores = taken[:, low:count]
        if masked:
            visible = [(key_row <= pos - begin) & (key_row >= at - begin) for pos, at in bounds]
            scores = jnp.concatenate(
                [
                    jnp.where(visible[(j + low) // half], scores[:, j : j + LANE], MASKED)
                    for j in range(0, count - low, LANE)
                ],
                axis=1,
            )
        new_best = jnp.maximum(best, jnp.max(scores, axis=0, keepdims=True) * scale)
        weights = jnp.exp2(scores * scale - new_best).astype(BF16)
        rescale = jnp.exp2(best - new_best)
        values = jnp.concatenate(
            [kv_ref[pl.ds(begin + j, HD), pl.ds(HD, HD)] for j in range(0, BK, HD)], axis=1
        )
        values = jnp.concatenate([values, ones], axis=0)
        product = jnp.dot(values, weights, preferred_element_type=F32)
        return new_best, summed * rescale + product

    def pair(i, carried, masked):
        score(scores_b, 2 * i + 1)
        carried = absorb(scores_a, 2 * i, carried, masked)
        score(scores_a, 2 * i + 2)
        return absorb(scores_b, 2 * i + 1, carried, masked)

    carried = (jnp.full((1, count), MASKED * scale, F32), jnp.zeros((HD + 16, count), F32))
    load(g).wait()
    score(scores_a, 2 * first)
    carried = lax.fori_loop(first, plain, lambda i, v: pair(i, v, True), carried)
    carried = lax.fori_loop(plain, top, lambda i, v: pair(i, v, False), carried)
    score(scores_b, 2 * top + 1)
    carried = absorb(scores_a, 2 * top, carried, True)
    score(scores_a, 2 * top + 2, half)
    best, summed = absorb(scores_b, 2 * top + 1, carried, True)
    later = (best[:, half:], summed[:, half:])
    score(scores_b, 2 * top + 3, half)
    later = absorb(scores_a, 2 * top + 2, later, True, half)
    later = absorb(scores_b, 2 * top + 3, later, True, half)
    for i, total in enumerate((summed[:, :half], later[1])):
        result = (total[:HD] / total[HD : HD + 1]).T.astype(BF16)
        for h in range(heads):
            out[i * half_rows : (i + 1) * half_rows, h * HD : (h + 1) * HD] = result[
                h * half_rows : (h + 1) * half_rows
            ]


def attend(positions, lengths, q, kv):
    rows = GROUP * RUN
    return pl.pallas_call(
        attend_kernel,
        out_shape=jax.ShapeDtypeStruct((TOK, CH), BF16),
        grid=(NSEQ // GROUP,),
        in_specs=[
            whole(pltpu.SMEM),
            whole(pltpu.SMEM),
            pl.BlockSpec((rows, CH), lambda g: (g, 0)),
            whole(pl.ANY),
        ],
        out_specs=pl.BlockSpec((rows, CH), lambda g: (g, 0)),
        scratch_shapes=[VM((BK, CH // HD * rows), F32)] * 2
        + [VM((TOKENS, 2 * HD), BF16), pltpu.SemaphoreType.DMA((NSEQ // GROUP,))],
        compiler_params=pltpu.CompilerParams(vmem_limit_bytes=VLIM),
        name="attend",
    )(positions, lengths, q, kv)


def local(
    x_branch,
    z_branch,
    conv_weight,
    conv_bias,
    xproj_weight,
    dt_weight,
    dt_bias,
    decay_rate,
    skip_gain,
    query_rows,
    key_rows,
    value_rows,
    lengths,
    destination,
):
    q, kv, positions, mamba_out = mix(
        destination.reshape(TOKENS // LANE, LANE),
        lengths,
        query_rows,
        key_rows,
        value_rows,
        x_branch,
        z_branch,
        conv_weight,
        conv_bias.reshape(1, CH),
        xproj_weight.T,
        dt_weight,
        dt_bias.reshape(1, CH),
        decay_rate,
        skip_gain.reshape(1, CH),
    )
    regrouped = attend(positions, lengths, q, kv)
    return (mamba_out, regrouped)


def solution(mesh):
    torus = Mesh(mesh.devices.reshape(NX, NY, NC, mesh.shape["mp"]), (*SEQ, "mp"))
    in_specs = (
        P(SEQ, "mp"),
        P(SEQ, "mp"),
        P(None, "mp"),
        P("mp"),
        P("mp", None),
        P(None, "mp"),
        P("mp"),
        P(None, "mp"),
        P("mp"),
        P(SEQ, "mp"),
        P(SEQ, "mp"),
        P(SEQ, "mp"),
        P(),
        P(),
    )
    out_specs = (P(SEQ, "mp"), P(SEQ, "mp"))
    return jax.shard_map(local, mesh=torus, in_specs=in_specs, out_specs=out_specs, check_vma=False)
```

```python
import math

import jax
import jax.numpy as jnp
from jax import lax
from jax.experimental import pallas as pl
from jax.experimental.pallas import tpu as pltpu
from jax.sharding import Mesh
from jax.sharding import PartitionSpec as P

SEQ = ("seq_0", "seq_1", "seq_2")
MESH = pl.DeviceIdType.MESH
VM = pltpu.VMEM
F32 = jnp.float32
BF16 = jnp.bfloat16
LOG2E = math.log2(math.e)
NX, NY, NC, NZ = 4, 4, 2, 8
NSEQ = NX * NY * NC
TOK = 256
TOK_BITS = 8
TOKENS = NSEQ * TOK
CH = 1024
LANE = 128
SUB = CH // LANE
NS = 16
RANK = 512
PROJ = RANK + 2 * NS
HD = 128
TAPS = 4
BIG_STEP = 1.0e7
MASKED = -1.0e30
GROUP = 8
RUN = TOK // NSEQ
BK = 512
VLIM = 60 * 1024 * 1024


def whole(space=VM):
    return pl.BlockSpec(memory_space=space)


def place():
    return (
        lax.axis_index("seq_0"),
        lax.axis_index("seq_1"),
        lax.axis_index("seq_2"),
        lax.axis_index("mp"),
    )


def seq_device(j, z):
    chip = lax.div(j, NC)
    return (lax.div(chip, NY), lax.rem(chip, NY), lax.rem(j, NC), z)


def doc_starts(len_ref):
    s1 = len_ref[0]
    s2 = s1 + len_ref[1]
    return s1, s2, s2 + len_ref[2]


def start_of(pos, starts):
    s1, s2, s3 = starts
    return jnp.where(pos >= s3, s3, jnp.where(pos >= s2, s2, jnp.where(pos >= s1, s1, 0)))


def silu(x):
    half = 0.5 * x
    return half * jnp.tanh(half) + half


def mixer_kernel(
    dest_ref,
    len_ref,
    q_ref,
    k_ref,
    v_ref,
    x_ref,
    z_hbm,
    cw_ref,
    cb_ref,
    xw_hbm,
    dtw_hbm,
    dtb_ref,
    rate_ref,
    skip_ref,
    q_out,
    kv_out,
    pos_out,
    out,
    kvs,
    qs,
    halo,
    ext,
    inner,
    part,
    taken,
    onward,
    proj,
    steps,
    drives,
    rates,
    spread,
    gains,
    ys,
    sums,
    st_own,
    st_pair,
    st_y,
    st_x,
    decays,
    gates,
    z_ref,
    xw_ref,
    dtw_ref,
    loc_sem,
    halo_sem,
    kv_send,
    kv_recv,
    q_send,
    q_recv,
    rs_send,
    rs_recv,
    ag_send,
    ag_recv,
    st_send,
    st_recv,
):
    x, y, c, z = place()
    me = (x * NY + y) * NC + c
    anchor = me * TOK
    barrier = pltpu.get_barrier_semaphore()
    near_x = [lax.rem(x + d, NX) for d in range(NX)]
    near_y = [lax.rem(y + d, NY) for d in range(NY)]
    near_z = [lax.rem(z + d, NZ) for d in range(NZ)]
    near_c = [c, 1 - c]
    far_first = (2, 1, 3)
    peers = [
        (dx, dy, dc) for dx in (*far_first, 0) for dy in (*far_first, 0) for dc in range(NC)
    ][:-2] + [(0, 0, 1)]
    for dx, dy, dc in peers:
        pl.semaphore_signal(
            barrier, inc=1, device_id=(near_x[dx], near_y[dy], near_c[dc], z), device_id_type=MESH
        )
    for k in range(1, NZ):
        pl.semaphore_signal(barrier, inc=1, device_id=(x, y, c, near_z[k]), device_id_type=MESH)
    load_k = pltpu.make_async_copy(k_ref, kvs.at[:, pl.ds(0, HD)], loc_sem.at[0])
    load_k.start()
    load_x = pltpu.make_async_copy(xw_hbm, xw_ref, loc_sem.at[2])
    load_x.start()
    load_d = pltpu.make_async_copy(dtw_hbm, dtw_ref, loc_sem.at[3])
    load_d.start()
    load_z = pltpu.make_async_copy(z_hbm, z_ref, loc_sem.at[4])
    load_z.start()
    starts = doc_starts(len_ref)
    token = anchor + lax.broadcasted_iota(jnp.int32, (TOK, LANE), 0)
    depth = token - start_of(token, starts)

    def convolve(count, cols, far):
        total = cb_ref[:, cols] + cw_ref[pl.ds(0, 1), cols] * ext[pl.ds(8, count), cols]
        for lag in range(1, TAPS):
            window = ext[pl.ds(8 - lag, count), cols]
            total = total + cw_ref[pl.ds(lag, 1), cols] * jnp.where(far >= lag, window, 0.0)
        inner[pl.ds(0, count), cols] = silu(total).astype(BF16)

    def conv_columns(i, carry):
        cols = pl.ds(pl.multiple_of(i * LANE, LANE), LANE)
        ext[pl.ds(0, 8), cols] = jnp.zeros((8, LANE), F32)
        ext[pl.ds(8, TOK), cols] = x_ref[:, cols].astype(F32)
        convolve(TOK, cols, depth)
        return carry

    lax.fori_loop(0, SUB, conv_columns, 0)
    pl.semaphore_wait(barrier, NSEQ - 1 + NZ - 1)

    def remote(src, dst, send, recv, device):
        return pltpu.make_async_remote_copy(
            src_ref=src,
            dst_ref=dst,
            send_sem=send,
            recv_sem=recv,
            device_id=device,
            device_id_type=MESH,
        )

    def offset(a, b, core):
        a, b = a % NX, b % NY
        return (
            lax.rem(x + a * (1 - core) + b * core, NX),
            lax.rem(y + a * core + b * (1 - core), NY),
        )

    def rows_of(a, b, core):
        px, py = offset(a, b, core)
        return pl.ds(pl.multiple_of(((px * NY + py) * NC + core) * TOK, TOK), TOK)

    partner = (x, y, 1 - c, z)
    after = lax.rem(me + 1, NSEQ)
    halo_copy = remote(
        x_ref.at[pl.ds(TOK - 16, 16)], halo, halo_sem.at[0], halo_sem.at[1], seq_device(after, z)
    )
    halo_copy.start()
    for half in range(TOK // HD):
        kvs[pl.ds(half * HD, HD), pl.ds(HD, HD)] = v_ref[pl.ds(half * HD, HD), :].T

    halves = TOK // LANE
    goal = lax.shift_right_logical(dest_ref[pl.ds(me * halves, halves), :], TOK_BITS) * RUN
    goal = goal + lax.broadcasted_iota(jnp.int32, (halves, LANE), 1) % RUN
    slot = lax.broadcasted_iota(jnp.int32, (TOK, LANE), 0)
    choice = jnp.concatenate(
        [jnp.where(slot == goal[i : i + 1], 1.0, 0.0) for i in range(halves)], axis=1
    )
    staged = jnp.dot(choice.astype(BF16), q_ref[...], preferred_element_type=F32)
    qs[...] = staged.astype(BF16).reshape(NSEQ, RUN, CH)
    load_k.wait()
    mine = kv_out.at[rows_of(0, 0, c)]
    sends = []
    for a in far_first:
        px, py = offset(a, 0, c)
        copy = remote(kvs, mine, kv_send.at[a], kv_recv.at[a], (px, py, c, z))
        copy.start()
        sends.append(copy)
    copy = remote(kvs, mine, kv_send.at[16], kv_recv.at[16], partner)
    copy.start()
    sends.append(copy)
    keep_kv = pltpu.make_async_copy(kvs, mine, loc_sem.at[0])
    keep_kv.start()
    q_rows = pl.ds(pl.multiple_of(me * RUN, RUN), RUN)
    for dx, dy, dc in peers:
        k = (dx * NY + dy) * NC + dc
        j = (near_x[dx] * NY + near_y[dy]) * NC + near_c[dc]
        device = (near_x[dx], near_y[dy], near_c[dc], z)
        copy = remote(qs.at[j], q_out.at[q_rows], q_send.at[k], q_recv.at[k], device)
        copy.start()
        sends.append(copy)
    keep_q = pltpu.make_async_copy(qs.at[me], q_out.at[q_rows], loc_sem.at[1])
    keep_q.start()

    halo_copy.wait()
    ext[pl.ds(0, 8), :] = halo[pl.ds(8, 8), :].astype(F32)
    near = anchor + lax.broadcasted_iota(jnp.int32, (16, CH), 0)
    convolve(16, pl.ds(0, CH), near - start_of(near, starts))

    load_x.wait()
    partial = lax.dot_general(
        inner[...], xw_ref[...], (((1,), (1,)), ((), ())), preferred_element_type=F32
    ).astype(BF16)
    slice_rows = TOK // NZ
    part[...] = partial.reshape(NZ, slice_rows, PROJ)

    def begin(copy):
        copy.start()
        sends.append(copy)
        return copy

    def to_sum(src, slot, d):
        return remote(
            src, taken.at[slot], rs_send.at[slot], rs_recv.at[slot], (x, y, c, near_z[d % NZ])
        )

    far_up = begin(to_sum(part.at[near_z[4]], 1, -2))
    mid_up = begin(to_sum(part.at[near_z[5]], 0, -1))
    mid_down = begin(to_sum(part.at[near_z[3]], 2, 1))
    last = [begin(to_sum(part.at[near_z[7]], 3, -1)), begin(to_sum(part.at[near_z[1]], 4, 1))]

    def wait_kv(slot_rows, index):
        remote(kvs, kv_out.at[slot_rows], kv_send.at[0], kv_recv.at[index], partner).wait_recv()

    mid_down.wait_recv()
    onward[1] = (part[near_z[2]].astype(F32) + taken[2].astype(F32)).astype(BF16)
    last.append(begin(to_sum(onward.at[1], 6, 2)))
    mid_up.wait_recv()
    far_up.wait_recv()
    merged = part[near_z[6]].astype(F32) + taken[0].astype(F32) + taken[1].astype(F32)
    onward[0] = merged.astype(BF16)
    last.append(begin(to_sum(onward.at[0], 5, -2)))
    for a in range(NX):
        if a > 0:
            wait_kv(rows_of(-a, 0, c), a)
        block = kv_out.at[rows_of(-a, 0, c)] if a > 0 else kvs
        target = kv_out.at[rows_of(-a, 0, c)]
        for b in far_first:
            px, py = offset(0, b, c)
            index = b * NX + a
            copy = remote(
                block, target, kv_send.at[index], kv_recv.at[index], (px, py, c, z)
            )
            copy.start()
            sends.append(copy)
        if a > 0:
            copy = remote(
                block, target, kv_send.at[16 + a], kv_recv.at[16 + a], partner
            )
            copy.start()
            sends.append(copy)


    total = part[z].astype(F32)
    for copy in last:
        copy.wait_recv()
    for slot in range(3, 7):
        total = total + taken[slot].astype(F32)

    def proj_rows(d):
        return pl.ds(pl.multiple_of(near_z[d % NZ] * slice_rows, slice_rows), slice_rows)

    def to_gather(chunk, index, d):
        rows = proj.at[proj_rows(chunk)]
        return remote(
            rows, rows, ag_send.at[index], ag_recv.at[index], (x, y, c, near_z[d % NZ])
        )

    proj[proj_rows(0), :] = total.astype(BF16)
    begin(to_gather(0, 0, 2))
    begin(to_gather(0, 1, -2))
    begin(to_gather(0, 2, 1))
    begin(to_gather(0, 3, -1))
    to_gather(-2, 0, 2).wait_recv()
    begin(to_gather(-2, 4, 2))
    begin(to_gather(-2, 5, 1))
    to_gather(2, 1, -2).wait_recv()
    begin(to_gather(2, 6, -1))
    spots = (TOKENS // LANE, LANE)
    spot = lax.broadcasted_iota(jnp.int32, spots, 1)
    ours = (lax.shift_right_logical(dest_ref[...], TOK_BITS) == me) & (spot % RUN == 0)
    spot = spot + LANE * lax.broadcasted_iota(jnp.int32, spots, 0)
    found = jnp.sum(jnp.where(ours, spot, 0).astype(F32), axis=1, keepdims=True)
    pos_out[...] = jnp.broadcast_to(found, spots).astype(jnp.int32)
    for j in range(SUB):
        cols = pl.ds(j * LANE, LANE)
        rates[pl.ds(j, NS, stride=SUB), :] = rate_ref[:, cols] * (-LOG2E)
    for chunk, index in ((-1, 2), (1, 3), (-4, 4), (-3, 5), (3, 6)):
        to_gather(chunk, index, 1).wait_recv()

    load_d.wait()
    begins = depth == 0
    low = proj[:, pl.ds(0, RANK)]
    for j in range(SUB):
        cols = pl.ds(j * LANE, LANE)
        if j % 2 == 0:
            both = pl.ds(j * LANE, 2 * LANE)
            raw = jnp.dot(low, dtw_ref[:, both], preferred_element_type=F32)
        value = raw[:, j % 2 * LANE : (j % 2 + 1) * LANE] + dtb_ref[:, cols]
        fade = jnp.exp2(jnp.abs(value) * (-LOG2E))
        series = fade - (0.5 * fade) * fade
        tail = jnp.where(fade < 1.0e-3, series, jnp.log(1.0 + fade))
        step = jnp.maximum(value, 0.0) + tail
        drives[pl.ds(j, TOK, stride=SUB), :] = step * inner[:, cols].astype(F32)
        step = jnp.where(begins, BIG_STEP, step)
        sums[pl.ds(j, 1), :] = jnp.sum(step, axis=0, keepdims=True)
        steps[pl.ds(j, TOK, stride=SUB), :] = step

    def widen(first):
        row = lax.broadcasted_iota(jnp.int32, (2 * NS, NS * LANE), 0)
        col = lax.broadcasted_iota(jnp.int32, (2 * NS, NS * LANE), 1)
        pick = jnp.where(lax.div(col, LANE) + first == row, 1.0, 0.0).astype(BF16)
        wide = jnp.dot(proj[:, pl.ds(RANK, 2 * NS)], pick, preferred_element_type=F32)
        for n in range(NS):
            spread[pl.ds((first + n) * TOK, TOK), :] = wide[:, n * LANE : (n + 1) * LANE]

    widen(0)
    rate = [rates[pl.ds(n * SUB, SUB), :] for n in range(NS)]

    def advance(t, carried):
        rows = pl.ds(pl.multiple_of(t * SUB, SUB), SUB)
        step = steps[rows, :]
        drive = drives[rows, :]
        result = []
        for n in range(NS):
            b = spread[pl.ds(n * TOK + t, SUB, stride=0), :]
            decay = jnp.exp2(step * rate[n])
            decays[t, pl.ds(n * SUB, SUB), :] = decay
            result.append(decay * carried[n] + b * drive)
        return tuple(result)

    zero = jnp.zeros((SUB, LANE), F32)
    state = lax.fori_loop(0, TOK, advance, (zero,) * NS, unroll=4)

    def pack(into, states, total):
        for n in range(0, NS, 2):
            pair = jnp.concatenate([states[n], states[n + 1]], axis=0)
            into[pl.ds(n * SUB, 2 * SUB), :] = pair.astype(BF16)
        high = total.astype(BF16).astype(F32)
        pair = jnp.concatenate([high, total - high], axis=0)
        into[pl.ds(NS * SUB, 2 * SUB), :] = pair.astype(BF16)

    def unpack(taken):
        block = taken[...].astype(F32).reshape(NS + 2, SUB, LANE)
        return [block[n] for n in range(NS)], block[NS] + block[NS + 1]

    def follow(states, block, total, passed=None):
        result = []
        for n in range(NS):
            moved = jnp.exp2(rate[n] * total) * states[n] + block[n]
            result.append(moved if passed is None else jnp.where(passed, moved, states[n]))
        return result

    pack(st_own, state, sums[...])
    pair_copy = remote(st_own, st_pair, st_send.at[0], st_recv.at[0], partner)
    pair_copy.start()
    sends.append(pair_copy)

    widen(NS)

    def local_token(t, carried):
        so_far, states = carried
        rows = pl.ds(pl.multiple_of(t * SUB, SUB), SUB)
        drive = drives[rows, :]
        passed = []
        result = []
        total = None
        for n in range(NS):
            decay = decays[t, pl.ds(n * SUB, SUB), :]
            b = spread[pl.ds(n * TOK + t, SUB, stride=0), :]
            weight = spread[pl.ds((NS + n) * TOK + t, SUB, stride=0), :]
            new = decay * states[n] + b * drive
            result.append(new)
            total = weight * new if total is None else total + weight * new
            left = so_far[n] * decay
            passed.append(left)
            gains[t, pl.ds(n * SUB, SUB), :] = weight * left
        ys[rows, :] = total
        return tuple(passed), tuple(result)

    carried = ((jnp.ones((SUB, LANE), F32),) * NS, (zero,) * NS)
    cuts = (0, 40, 144, TOK)
    carried = lax.fori_loop(cuts[0], cuts[1], local_token, carried, unroll=2)

    pair_copy.wait_recv()
    own_state, own_total = unpack(st_own)
    other_state, other_total = unpack(st_pair)
    first_core = c == 0
    early = [jnp.where(first_core, p, q) for p, q in zip(own_state, other_state)]
    late = [jnp.where(first_core, q, p) for p, q in zip(own_state, other_state)]
    late_total = jnp.where(first_core, other_total, own_total)
    chip_state = follow(early, late, late_total)
    pack(st_y.at[0], chip_state, own_total + other_total)
    level = []
    for k in far_first:
        copy = remote(
            st_y.at[0], st_y.at[k], st_send.at[k], st_recv.at[k], (x, near_y[k], c, z)
        )
        copy.start()
        level.append(copy)
    sends += level
    carried = lax.fori_loop(cuts[1], cuts[2], local_token, carried, unroll=2)

    for copy in level:
        copy.wait_recv()
    column, column_total = unpack(st_y.at[lax.rem(y + NY, NY)])
    for j in range(1, NY):
        block, total = unpack(st_y.at[lax.rem(y + NY - j, NY)])
        column = follow(column, block, total)
        column_total = column_total + total
    pack(st_x.at[0], column, column_total)
    level = []
    for k in far_first:
        copy = remote(
            st_x.at[0], st_x.at[k], st_send.at[4 + k], st_recv.at[4 + k], (near_x[k], y, c, z)
        )
        copy.start()
        level.append(copy)
    sends += level
    carried = lax.fori_loop(cuts[2], cuts[3], local_token, carried, unroll=2)

    for b in range(1, NY):
        for a in range(NX):
            index = b * NX + a
            wait_kv(rows_of(-a, -b, c), index)
            block = kv_out.at[rows_of(-a, -b, c)]
            copy = remote(block, block, kv_send.at[16 + index], kv_recv.at[16 + index], partner)
            copy.start()
            sends.append(copy)

    load_z.wait()
    for j in range(SUB):
        cols = pl.ds(j * LANE, LANE)
        gates[:, cols] = silu(z_ref[:, cols].astype(F32))
        inner_gain = skip_ref[:, cols] * inner[:, cols].astype(F32)
        kept = ys[pl.ds(j, TOK, stride=SUB), :]
        ys[pl.ds(j, TOK, stride=SUB), :] = kept + inner_gain
    for copy in level:
        copy.wait_recv()
    entering = [zero] * NS
    for j in range(NX - 1):
        block, total = unpack(st_x.at[lax.rem(x + NX - j, NX)])
        entering = follow(entering, block, total, x > j)
    for j in range(NY - 1):
        block, total = unpack(st_y.at[lax.rem(y + NY - j, NY)])
        entering = follow(entering, block, total, y > j)
    entering = follow(entering, early, jnp.where(first_core, own_total, other_total), c > 0)

    def correct(t, carry):
        rows = pl.ds(pl.multiple_of(t * SUB, SUB), SUB)
        total = ys[rows, :]
        for n in range(NS):
            total = total + gains[t, pl.ds(n * SUB, SUB), :] * entering[n]
        ys[rows, :] = total
        return carry

    lax.fori_loop(0, TOK, correct, 0, unroll=4)
    for j in range(SUB):
        cols = pl.ds(j * LANE, LANE)
        out[:, cols] = (ys[pl.ds(j, TOK, stride=SUB), :] * gates[:, cols]).astype(BF16)

    for dx, dy, dc in peers:
        k = (dx * NY + dy) * NC + dc
        source = (near_x[-dx % NX] * NY + near_y[-dy % NY]) * NC + near_c[dc]
        rows = pl.ds(pl.multiple_of(source * RUN, RUN), RUN)
        remote(qs.at[0], q_out.at[rows], q_send.at[k], q_recv.at[k], partner).wait_recv()
    for b in range(NY):
        for a in range(NX):
            wait_kv(rows_of(-a, -b, 1 - c), 16 + b * NX + a)
    for copy in sends:
        copy.wait_send()
    keep_kv.wait()
    keep_q.wait()


def mix(dest, lengths, q, k, v, x, z, cw, cb, xw, dtw, dtb, rate, skip):
    dma = pltpu.SemaphoreType.DMA
    states = ((NS + 2) * SUB, LANE)
    chunk = (TOK // NZ, PROJ)
    return pl.pallas_call(
        mixer_kernel,
        out_shape=(
            jax.ShapeDtypeStruct((TOK, CH), BF16),
            jax.ShapeDtypeStruct((NSEQ * TOK, 2 * HD), BF16),
            jax.ShapeDtypeStruct((TOKENS // LANE, LANE), jnp.int32),
            jax.ShapeDtypeStruct((TOK, CH), BF16),
        ),
        in_specs=[
            whole(),
            whole(pltpu.SMEM),
            whole(),
            whole(pl.ANY),
            whole(),
            whole(),
            whole(pl.ANY),
            whole(),
            whole(),
            whole(pl.ANY),
            whole(pl.ANY),
        ]
        + [whole()] * 3,
        out_specs=(whole(pl.ANY), whole(pl.ANY), whole(), whole()),
        scratch_shapes=[
            VM((TOK, 2 * HD), BF16),
            VM((NSEQ, RUN, CH), BF16),
            VM((16, CH), BF16),
            VM((TOK + 8, CH), F32),
            VM((TOK, CH), BF16),
            VM((NZ, *chunk), BF16),
            VM((NZ, *chunk), BF16),
            VM((2, *chunk), BF16),
            VM((TOK, PROJ), BF16),
            VM((TOK * SUB, LANE), F32),
            VM((TOK * SUB, LANE), F32),
            VM((NS * SUB, LANE), F32),
            VM((2 * NS * TOK, LANE), F32),
            VM((TOK, NS * SUB, LANE), F32),
            VM((TOK * SUB, LANE), F32),
            VM((SUB, LANE), F32),
            VM(states, BF16),
            VM(states, BF16),
            VM((NY, *states), BF16),
            VM((NX, *states), BF16),
            VM((TOK, NS * SUB, LANE), F32),
            VM((TOK, CH), F32),
            VM((TOK, CH), BF16),
            VM((PROJ, CH), BF16),
            VM((RANK, CH), BF16),
            dma((5,)),
            dma((2,)),
            dma((32,)),
            dma((32,)),
            dma((NSEQ,)),
            dma((NSEQ,)),
            dma((NZ,)),
            dma((NZ,)),
            dma((NZ,)),
            dma((NZ,)),
            dma((NZ,)),
            dma((NZ,)),
        ],
        compiler_params=pltpu.CompilerParams(
            collective_id=0, has_side_effects=True, vmem_limit_bytes=VLIM
        ),
        name="mixer",
    )(dest, lengths, q, k, v, x, z, cw, cb, xw, dtw, dtb, rate, skip)


def attend_kernel(pos_ref, len_ref, q_ref, kv_hbm, out, scores_a, scores_b, kv_ref, sems):
    g = pl.program_id(0)
    heads = CH // HD
    rows = GROUP * RUN
    count = heads * rows
    half = count // 2
    half_rows = rows // 2
    wide = 2 * BK
    span = TOK * GROUP
    halves = TOK // LANE

    def load(i):
        part = pl.ds(pl.multiple_of(i * span, span), span)
        return pltpu.make_async_copy(kv_hbm.at[part], kv_ref.at[part], sems.at[i])

    @pl.when(g == 0)
    def _():
        for i in range(NSEQ // GROUP):
            load(i).start()

    starts = doc_starts(len_ref)
    bases = [
        sum(pos_ref[(g * GROUP + i) * halves + j, 0] for j in range(halves)) for i in range(GROUP)
    ]
    lane = lax.broadcasted_iota(jnp.int32, (1, LANE), 1) % half_rows

    def lanes(firsts):
        base = firsts[0]
        for i in range(1, GROUP // 2):
            base = jnp.where(lane >= i * RUN, firsts[i], base)
        pos = base + lane % RUN
        return pos, start_of(pos, starts)

    bounds = (lanes(bases[: GROUP // 2]), lanes(bases[GROUP // 2 :]))
    top = g * (span // wide)
    first = jnp.minimum(lax.div(start_of(bases[0], starts), wide), top)
    last_start = start_of(bases[GROUP - 1] + RUN - 1, starts)
    plain = jnp.maximum(jnp.minimum(lax.div(last_start + wide - 1, wide), top), first)
    q = jnp.concatenate(
        [
            q_ref[i * half_rows : (i + 1) * half_rows, h * HD : (h + 1) * HD]
            for i in range(2)
            for h in range(heads)
        ],
        axis=0,
    )
    scale = HD**-0.5 * LOG2E
    key_row = lax.broadcasted_iota(jnp.int32, (BK, LANE), 0)
    ones = jnp.ones((16, BK), BF16)

    def score(into, i, low=0):
        keys = kv_ref[pl.ds(pl.multiple_of(i * BK, BK), BK), pl.ds(0, HD)]
        into[:, low:count] = lax.dot_general(
            keys, q[low:], (((1,), (1,)), ((), ())), preferred_element_type=F32
        )

    def absorb(taken, i, carried, masked, low=0):
        begin = pl.multiple_of(i * BK, BK)
        best, summed = carried
        scores = taken[:, low:count]
        if masked:
            visible = [(key_row <= pos - begin) & (key_row >= at - begin) for pos, at in bounds]
            scores = jnp.concatenate(
                [
                    jnp.where(visible[(j + low) // half], scores[:, j : j + LANE], MASKED)
                    for j in range(0, count - low, LANE)
                ],
                axis=1,
            )
        new_best = jnp.maximum(best, jnp.max(scores, axis=0, keepdims=True) * scale)
        weights = jnp.exp2(scores * scale - new_best).astype(BF16)
        rescale = jnp.exp2(best - new_best)
        values = jnp.concatenate(
            [kv_ref[pl.ds(begin + j, HD), pl.ds(HD, HD)] for j in range(0, BK, HD)], axis=1
        )
        values = jnp.concatenate([values, ones], axis=0)
        product = jnp.dot(values, weights, preferred_element_type=F32)
        return new_best, summed * rescale + product

    def pair(i, carried, masked):
        score(scores_b, 2 * i + 1)
        carried = absorb(scores_a, 2 * i, carried, masked)
        score(scores_a, 2 * i + 2)
        return absorb(scores_b, 2 * i + 1, carried, masked)

    carried = (jnp.full((1, count), MASKED * scale, F32), jnp.zeros((HD + 16, count), F32))
    load(g).wait()
    score(scores_a, 2 * first)
    carried = lax.fori_loop(first, plain, lambda i, v: pair(i, v, True), carried)
    carried = lax.fori_loop(plain, top, lambda i, v: pair(i, v, False), carried)
    score(scores_b, 2 * top + 1)
    carried = absorb(scores_a, 2 * top, carried, True)
    score(scores_a, 2 * top + 2, half)
    best, summed = absorb(scores_b, 2 * top + 1, carried, True)
    later = (best[:, half:], summed[:, half:])
    score(scores_b, 2 * top + 3, half)
    later = absorb(scores_a, 2 * top + 2, later, True, half)
    later = absorb(scores_b, 2 * top + 3, later, True, half)
    for i, total in enumerate((summed[:, :half], later[1])):
        result = (total[:HD] / total[HD : HD + 1]).T.astype(BF16)
        for h in range(heads):
            out[i * half_rows : (i + 1) * half_rows, h * HD : (h + 1) * HD] = result[
                h * half_rows : (h + 1) * half_rows
            ]


def attend(positions, lengths, q, kv):
    rows = GROUP * RUN
    return pl.pallas_call(
        attend_kernel,
        out_shape=jax.ShapeDtypeStruct((TOK, CH), BF16),
        grid=(NSEQ // GROUP,),
        in_specs=[
            whole(pltpu.SMEM),
            whole(pltpu.SMEM),
            pl.BlockSpec((rows, CH), lambda g: (g, 0)),
            whole(pl.ANY),
        ],
        out_specs=pl.BlockSpec((rows, CH), lambda g: (g, 0)),
        scratch_shapes=[VM((BK, CH // HD * rows), F32)] * 2
        + [VM((TOKENS, 2 * HD), BF16), pltpu.SemaphoreType.DMA((NSEQ // GROUP,))],
        compiler_params=pltpu.CompilerParams(vmem_limit_bytes=VLIM),
        name="attend",
    )(positions, lengths, q, kv)


def local(
    x_branch,
    z_branch,
    conv_weight,
    conv_bias,
    xproj_weight,
    dt_weight,
    dt_bias,
    decay_rate,
    skip_gain,
    query_rows,
    key_rows,
    value_rows,
    lengths,
    destination,
):
    q, kv, positions, mamba_out = mix(
        destination.reshape(TOKENS // LANE, LANE),
        lengths,
        query_rows,
        key_rows,
        value_rows,
        x_branch,
        z_branch,
        conv_weight,
        conv_bias.reshape(1, CH),
        xproj_weight.T,
        dt_weight,
        dt_bias.reshape(1, CH),
        decay_rate,
        skip_gain.reshape(1, CH),
    )
    regrouped = attend(positions, lengths, q, kv)
    return (mamba_out, regrouped)


def solution(mesh):
    torus = Mesh(mesh.devices.reshape(NX, NY, NC, mesh.shape["mp"]), (*SEQ, "mp"))
    in_specs = (
        P(SEQ, "mp"),
        P(SEQ, "mp"),
        P(None, "mp"),
        P("mp"),
        P("mp", None),
        P(None, "mp"),
        P("mp"),
        P(None, "mp"),
        P("mp"),
        P(SEQ, "mp"),
        P(SEQ, "mp"),
        P(SEQ, "mp"),
        P(),
        P(),
    )
    out_specs = (P(SEQ, "mp"), P(SEQ, "mp"))
    return jax.shard_map(local, mesh=torus, in_specs=in_specs, out_specs=out_specs, check_vma=False)
```

```python
import math

import jax
import jax.numpy as jnp
from jax import lax
from jax.experimental import pallas as pl
from jax.experimental.pallas import tpu as pltpu
from jax.sharding import Mesh
from jax.sharding import PartitionSpec as P

SEQ = ("seq_0", "seq_1", "seq_2")
MESH = pl.DeviceIdType.MESH
VM = pltpu.VMEM
F32 = jnp.float32
BF16 = jnp.bfloat16
LOG2E = math.log2(math.e)
NX, NY, NC, NZ = 4, 4, 2, 8
NSEQ = NX * NY * NC
TOK = 256
TOK_BITS = 8
TOKENS = NSEQ * TOK
CH = 1024
LANE = 128
SUB = CH // LANE
NS = 16
RANK = 512
PROJ = RANK + 2 * NS
HD = 128
TAPS = 4
BIG_STEP = 1.0e7
MASKED = -1.0e30
GROUP = 8
RUN = TOK // NSEQ
BK = 512
VLIM = 60 * 1024 * 1024


def whole(space=VM):
    return pl.BlockSpec(memory_space=space)


def place():
    return (
        lax.axis_index("seq_0"),
        lax.axis_index("seq_1"),
        lax.axis_index("seq_2"),
        lax.axis_index("mp"),
    )


def seq_device(j, z):
    chip = lax.div(j, NC)
    return (lax.div(chip, NY), lax.rem(chip, NY), lax.rem(j, NC), z)


def doc_starts(len_ref):
    s1 = len_ref[0]
    s2 = s1 + len_ref[1]
    return s1, s2, s2 + len_ref[2]


def start_of(pos, starts):
    s1, s2, s3 = starts
    return jnp.where(pos >= s3, s3, jnp.where(pos >= s2, s2, jnp.where(pos >= s1, s1, 0)))


def silu(x):
    half = 0.5 * x
    return half * jnp.tanh(half) + half


def mixer_kernel(
    dest_ref,
    len_ref,
    q_hbm,
    k_ref,
    v_ref,
    x_hbm,
    z_hbm,
    cw_ref,
    cb_ref,
    xw_hbm,
    dtw_hbm,
    dtb_ref,
    rate_ref,
    skip_ref,
    q_out,
    kv_out,
    pos_out,
    out,
    kvs,
    qs,
    halo,
    ext,
    inner,
    part,
    taken,
    onward,
    proj,
    steps,
    drives,
    rates,
    spread,
    gains,
    ys,
    sums,
    st_own,
    st_pair,
    st_y,
    st_x,
    decays,
    gates,
    picks,
    q_ref,
    x_ref,
    z_ref,
    xw_ref,
    dtw_ref,
    loc_sem,
    halo_sem,
    kv_send,
    kv_recv,
    q_send,
    q_recv,
    rs_send,
    rs_recv,
    ag_send,
    ag_recv,
    st_send,
    st_recv,
):
    x, y, c, z = place()
    me = (x * NY + y) * NC + c
    anchor = me * TOK
    load_rows = pltpu.make_async_copy(x_hbm, x_ref, loc_sem.at[5])
    load_rows.start()
    load_q = pltpu.make_async_copy(q_hbm, q_ref, loc_sem.at[6])
    load_q.start()
    load_k = pltpu.make_async_copy(k_ref, kvs.at[:, pl.ds(0, HD)], loc_sem.at[0])
    load_k.start()
    load_x = pltpu.make_async_copy(xw_hbm, xw_ref, loc_sem.at[2])
    load_x.start()
    load_d = pltpu.make_async_copy(dtw_hbm, dtw_ref, loc_sem.at[3])
    load_d.start()
    load_z = pltpu.make_async_copy(z_hbm, z_ref, loc_sem.at[4])
    load_z.start()
    barrier = pltpu.get_barrier_semaphore()
    near_x = [lax.rem(x + d, NX) for d in range(NX)]
    near_y = [lax.rem(y + d, NY) for d in range(NY)]
    near_z = [lax.rem(z + d, NZ) for d in range(NZ)]
    near_c = [c, 1 - c]
    far_first = (2, 1, 3)
    peers = [
        (dx, dy, dc) for dx in (*far_first, 0) for dy in (*far_first, 0) for dc in range(NC)
    ][:-2] + [(0, 0, 1)]
    for dx, dy, dc in peers:
        pl.semaphore_signal(
            barrier, inc=1, device_id=(near_x[dx], near_y[dy], near_c[dc], z), device_id_type=MESH
        )
    for k in range(1, NZ):
        pl.semaphore_signal(barrier, inc=1, device_id=(x, y, c, near_z[k]), device_id_type=MESH)
    starts = doc_starts(len_ref)
    token = anchor + lax.broadcasted_iota(jnp.int32, (TOK, LANE), 0)
    depth = token - start_of(token, starts)

    def convolve(count, cols, far):
        total = cb_ref[:, cols] + cw_ref[pl.ds(0, 1), cols] * ext[pl.ds(8, count), cols]
        for lag in range(1, TAPS):
            window = ext[pl.ds(8 - lag, count), cols]
            total = total + cw_ref[pl.ds(lag, 1), cols] * jnp.where(far >= lag, window, 0.0)
        inner[pl.ds(0, count), cols] = silu(total).astype(BF16)

    def conv_columns(i, carry):
        cols = pl.ds(pl.multiple_of(i * LANE, LANE), LANE)
        ext[pl.ds(0, 8), cols] = jnp.zeros((8, LANE), F32)
        ext[pl.ds(8, TOK), cols] = x_ref[:, cols].astype(F32)
        convolve(TOK, cols, depth)
        return carry

    load_rows.wait()
    lax.fori_loop(0, SUB, conv_columns, 0)
    pl.semaphore_wait(barrier, NSEQ - 1 + NZ - 1)

    def remote(src, dst, send, recv, device):
        return pltpu.make_async_remote_copy(
            src_ref=src,
            dst_ref=dst,
            send_sem=send,
            recv_sem=recv,
            device_id=device,
            device_id_type=MESH,
        )

    def offset(a, b, core):
        a, b = a % NX, b % NY
        return (
            lax.rem(x + a * (1 - core) + b * core, NX),
            lax.rem(y + a * core + b * (1 - core), NY),
        )

    def rows_of(a, b, core):
        px, py = offset(a, b, core)
        return pl.ds(pl.multiple_of(((px * NY + py) * NC + core) * TOK, TOK), TOK)

    partner = (x, y, 1 - c, z)
    after = lax.rem(me + 1, NSEQ)
    halo_copy = remote(
        x_ref.at[pl.ds(TOK - 16, 16)], halo, halo_sem.at[0], halo_sem.at[1], seq_device(after, z)
    )
    halo_copy.start()
    for half in range(TOK // HD):
        kvs[pl.ds(half * HD, HD), pl.ds(HD, HD)] = v_ref[pl.ds(half * HD, HD), :].T

    load_q.wait()
    halves = TOK // LANE
    goal = lax.shift_right_logical(dest_ref[pl.ds(me * halves, halves), :], TOK_BITS) * RUN
    goal = goal + lax.broadcasted_iota(jnp.int32, (halves, LANE), 1) % RUN
    slot = lax.broadcasted_iota(jnp.int32, (TOK, LANE), 0)
    choice = jnp.concatenate(
        [jnp.where(slot == goal[i : i + 1], 1.0, 0.0) for i in range(halves)], axis=1
    )
    staged = jnp.dot(choice.astype(BF16), q_ref[...], preferred_element_type=F32)
    qs[...] = staged.astype(BF16).reshape(NSEQ, RUN, CH)
    load_k.wait()
    mine = kv_out.at[rows_of(0, 0, c)]
    sends = []
    for a in far_first:
        px, py = offset(a, 0, c)
        copy = remote(kvs, mine, kv_send.at[a], kv_recv.at[a], (px, py, c, z))
        copy.start()
        sends.append(copy)
    copy = remote(kvs, mine, kv_send.at[16], kv_recv.at[16], partner)
    copy.start()
    sends.append(copy)
    keep_kv = pltpu.make_async_copy(kvs, mine, loc_sem.at[0])
    keep_kv.start()
    q_rows = pl.ds(pl.multiple_of(me * RUN, RUN), RUN)
    for dx, dy, dc in peers:
        k = (dx * NY + dy) * NC + dc
        j = (near_x[dx] * NY + near_y[dy]) * NC + near_c[dc]
        device = (near_x[dx], near_y[dy], near_c[dc], z)
        copy = remote(qs.at[j], q_out.at[q_rows], q_send.at[k], q_recv.at[k], device)
        copy.start()
        sends.append(copy)
    keep_q = pltpu.make_async_copy(qs.at[me], q_out.at[q_rows], loc_sem.at[1])
    keep_q.start()

    slice_rows = TOK // NZ
    load_x.wait()

    def project(rows):
        return lax.dot_general(
            rows, xw_ref[...], (((1,), (1,)), ((), ())), preferred_element_type=F32
        ).astype(BF16)

    later = project(inner[pl.ds(slice_rows, TOK - slice_rows), :])
    part[pl.ds(1, NZ - 1)] = later.reshape(NZ - 1, slice_rows, PROJ)
    halo_copy.wait()
    ext[pl.ds(0, 8), :] = halo[pl.ds(8, 8), :].astype(F32)
    near = anchor + lax.broadcasted_iota(jnp.int32, (16, CH), 0)
    convolve(16, pl.ds(0, CH), near - start_of(near, starts))

    part[0] = project(inner[pl.ds(0, slice_rows), :])

    def begin(copy):
        copy.start()
        sends.append(copy)
        return copy

    def to_sum(src, slot, d):
        return remote(
            src, taken.at[slot], rs_send.at[slot], rs_recv.at[slot], (x, y, c, near_z[d % NZ])
        )

    far_up = begin(to_sum(part.at[near_z[4]], 1, -2))
    mid_up = begin(to_sum(part.at[near_z[5]], 0, -1))
    mid_down = begin(to_sum(part.at[near_z[3]], 2, 1))
    last = [begin(to_sum(part.at[near_z[7]], 3, -1)), begin(to_sum(part.at[near_z[1]], 4, 1))]

    def wait_kv(slot_rows, index):
        remote(kvs, kv_out.at[slot_rows], kv_send.at[0], kv_recv.at[index], partner).wait_recv()

    mid_down.wait_recv()
    onward[1] = (part[near_z[2]].astype(F32) + taken[2].astype(F32)).astype(BF16)
    last.append(begin(to_sum(onward.at[1], 6, 2)))
    mid_up.wait_recv()
    far_up.wait_recv()
    merged = part[near_z[6]].astype(F32) + taken[0].astype(F32) + taken[1].astype(F32)
    onward[0] = merged.astype(BF16)
    last.append(begin(to_sum(onward.at[0], 5, -2)))
    for a in range(NX):
        if a > 0:
            wait_kv(rows_of(-a, 0, c), a)
        block = kv_out.at[rows_of(-a, 0, c)] if a > 0 else kvs
        target = kv_out.at[rows_of(-a, 0, c)]
        for b in far_first:
            px, py = offset(0, b, c)
            index = b * NX + a
            copy = remote(
                block, target, kv_send.at[index], kv_recv.at[index], (px, py, c, z)
            )
            copy.start()
            sends.append(copy)
        if a > 0:
            copy = remote(
                block, target, kv_send.at[16 + a], kv_recv.at[16 + a], partner
            )
            copy.start()
            sends.append(copy)


    total = part[z].astype(F32)
    for copy in last:
        copy.wait_recv()
    for slot in range(3, 7):
        total = total + taken[slot].astype(F32)

    def proj_rows(d):
        return pl.ds(pl.multiple_of(near_z[d % NZ] * slice_rows, slice_rows), slice_rows)

    def to_gather(chunk, index, d):
        rows = proj.at[proj_rows(chunk)]
        return remote(
            rows, rows, ag_send.at[index], ag_recv.at[index], (x, y, c, near_z[d % NZ])
        )

    proj[proj_rows(0), :] = total.astype(BF16)
    begin(to_gather(0, 0, 2))
    begin(to_gather(0, 1, -2))
    begin(to_gather(0, 2, 1))
    begin(to_gather(0, 3, -1))
    to_gather(-2, 0, 2).wait_recv()
    begin(to_gather(-2, 4, 2))
    begin(to_gather(-2, 5, 1))
    to_gather(2, 1, -2).wait_recv()
    begin(to_gather(2, 6, -1))
    row = lax.broadcasted_iota(jnp.int32, (2 * NS, NS * LANE), 0)
    col = lax.div(lax.broadcasted_iota(jnp.int32, (2 * NS, NS * LANE), 1), LANE)
    for i in range(2):
        picks[i] = jnp.where(col + i * NS == row, 1.0, 0.0).astype(BF16)
    spots = (TOKENS // LANE, LANE)
    spot = lax.broadcasted_iota(jnp.int32, spots, 1)
    ours = (lax.shift_right_logical(dest_ref[...], TOK_BITS) == me) & (spot % RUN == 0)
    spot = spot + LANE * lax.broadcasted_iota(jnp.int32, spots, 0)
    found = jnp.sum(jnp.where(ours, spot, 0).astype(F32), axis=1, keepdims=True)
    pos_out[...] = jnp.broadcast_to(found, spots).astype(jnp.int32)
    for j in range(SUB):
        cols = pl.ds(j * LANE, LANE)
        rates[pl.ds(j, NS, stride=SUB), :] = rate_ref[:, cols] * (-LOG2E)
    for chunk, index in ((-1, 2), (1, 3), (-4, 4), (-3, 5), (3, 6)):
        to_gather(chunk, index, 1).wait_recv()

    load_d.wait()
    begins = depth == 0
    low = proj[:, pl.ds(0, RANK)]
    for j in range(SUB):
        cols = pl.ds(j * LANE, LANE)
        if j % 2 == 0:
            both = pl.ds(j * LANE, 2 * LANE)
            raw = jnp.dot(low, dtw_ref[:, both], preferred_element_type=F32)
        value = raw[:, j % 2 * LANE : (j % 2 + 1) * LANE] + dtb_ref[:, cols]
        fade = jnp.exp2(jnp.abs(value) * (-LOG2E))
        series = fade - (0.5 * fade) * fade
        tail = jnp.where(fade < 1.0e-3, series, jnp.log(1.0 + fade))
        step = jnp.maximum(value, 0.0) + tail
        drives[pl.ds(j, TOK, stride=SUB), :] = step * inner[:, cols].astype(F32)
        step = jnp.where(begins, BIG_STEP, step)
        sums[pl.ds(j, 1), :] = jnp.sum(step, axis=0, keepdims=True)
        steps[pl.ds(j, TOK, stride=SUB), :] = step

    def widen(first):
        pick = picks[first // NS]
        wide = jnp.dot(proj[:, pl.ds(RANK, 2 * NS)], pick, preferred_element_type=F32)
        for n in range(NS):
            spread[pl.ds((first + n) * TOK, TOK), :] = wide[:, n * LANE : (n + 1) * LANE]

    widen(0)
    rate = [rates[pl.ds(n * SUB, SUB), :] for n in range(NS)]

    def advance(t, carried):
        rows = pl.ds(pl.multiple_of(t * SUB, SUB), SUB)
        step = steps[rows, :]
        drive = drives[rows, :]
        result = []
        for n in range(NS):
            b = spread[pl.ds(n * TOK + t, SUB, stride=0), :]
            decay = jnp.exp2(step * rate[n])
            decays[t, pl.ds(n * SUB, SUB), :] = decay
            result.append(decay * carried[n] + b * drive)
        return tuple(result)

    zero = jnp.zeros((SUB, LANE), F32)
    state = lax.fori_loop(0, TOK, advance, (zero,) * NS, unroll=4)

    def pack(into, states, total):
        for n in range(0, NS, 2):
            pair = jnp.concatenate([states[n], states[n + 1]], axis=0)
            into[pl.ds(n * SUB, 2 * SUB), :] = pair.astype(BF16)
        high = total.astype(BF16).astype(F32)
        pair = jnp.concatenate([high, total - high], axis=0)
        into[pl.ds(NS * SUB, 2 * SUB), :] = pair.astype(BF16)

    def unpack(taken):
        block = taken[...].astype(F32).reshape(NS + 2, SUB, LANE)
        return [block[n] for n in range(NS)], block[NS] + block[NS + 1]

    def follow(states, block, total, passed=None):
        result = []
        for n in range(NS):
            moved = jnp.exp2(rate[n] * total) * states[n] + block[n]
            result.append(moved if passed is None else jnp.where(passed, moved, states[n]))
        return result

    pack(st_own, state, sums[...])
    pair_copy = remote(st_own, st_pair, st_send.at[0], st_recv.at[0], partner)
    pair_copy.start()
    sends.append(pair_copy)

    widen(NS)

    def local_token(t, carried):
        so_far, states = carried
        rows = pl.ds(pl.multiple_of(t * SUB, SUB), SUB)
        drive = drives[rows, :]
        passed = []
        result = []
        total = None
        for n in range(NS):
            decay = decays[t, pl.ds(n * SUB, SUB), :]
            b = spread[pl.ds(n * TOK + t, SUB, stride=0), :]
            weight = spread[pl.ds((NS + n) * TOK + t, SUB, stride=0), :]
            new = decay * states[n] + b * drive
            result.append(new)
            total = weight * new if total is None else total + weight * new
            left = so_far[n] * decay
            passed.append(left)
            gains[t, pl.ds(n * SUB, SUB), :] = weight * left
        ys[rows, :] = total
        return tuple(passed), tuple(result)

    carried = ((jnp.ones((SUB, LANE), F32),) * NS, (zero,) * NS)
    cuts = (0, 40, 144, TOK)
    carried = lax.fori_loop(cuts[0], cuts[1], local_token, carried, unroll=2)

    pair_copy.wait_recv()
    own_state, own_total = unpack(st_own)
    other_state, other_total = unpack(st_pair)
    first_core = c == 0
    early = [jnp.where(first_core, p, q) for p, q in zip(own_state, other_state)]
    late = [jnp.where(first_core, q, p) for p, q in zip(own_state, other_state)]
    late_total = jnp.where(first_core, other_total, own_total)
    chip_state = follow(early, late, late_total)
    pack(st_y.at[0], chip_state, own_total + other_total)
    level = []
    for k in far_first:
        copy = remote(
            st_y.at[0], st_y.at[k], st_send.at[k], st_recv.at[k], (x, near_y[k], c, z)
        )
        copy.start()
        level.append(copy)
    sends += level
    carried = lax.fori_loop(cuts[1], cuts[2], local_token, carried, unroll=2)

    for copy in level:
        copy.wait_recv()
    column, column_total = unpack(st_y.at[lax.rem(y + NY, NY)])
    for j in range(1, NY):
        block, total = unpack(st_y.at[lax.rem(y + NY - j, NY)])
        column = follow(column, block, total)
        column_total = column_total + total
    pack(st_x.at[0], column, column_total)
    level = []
    for k in far_first:
        copy = remote(
            st_x.at[0], st_x.at[k], st_send.at[4 + k], st_recv.at[4 + k], (near_x[k], y, c, z)
        )
        copy.start()
        level.append(copy)
    sends += level
    carried = lax.fori_loop(cuts[2], cuts[3], local_token, carried, unroll=2)

    for b in range(1, NY):
        for a in range(NX):
            index = b * NX + a
            wait_kv(rows_of(-a, -b, c), index)
            block = kv_out.at[rows_of(-a, -b, c)]
            copy = remote(block, block, kv_send.at[16 + index], kv_recv.at[16 + index], partner)
            copy.start()
            sends.append(copy)

    load_z.wait()
    for j in range(SUB):
        cols = pl.ds(j * LANE, LANE)
        gates[:, cols] = silu(z_ref[:, cols].astype(F32))
        inner_gain = skip_ref[:, cols] * inner[:, cols].astype(F32)
        kept = ys[pl.ds(j, TOK, stride=SUB), :]
        ys[pl.ds(j, TOK, stride=SUB), :] = kept + inner_gain
    for copy in level:
        copy.wait_recv()
    entering = [zero] * NS
    for j in range(NX - 1):
        block, total = unpack(st_x.at[lax.rem(x + NX - j, NX)])
        entering = follow(entering, block, total, x > j)
    for j in range(NY - 1):
        block, total = unpack(st_y.at[lax.rem(y + NY - j, NY)])
        entering = follow(entering, block, total, y > j)
    entering = follow(entering, early, jnp.where(first_core, own_total, other_total), c > 0)

    def correct(t, carry):
        rows = pl.ds(pl.multiple_of(t * SUB, SUB), SUB)
        total = ys[rows, :]
        for n in range(NS):
            total = total + gains[t, pl.ds(n * SUB, SUB), :] * entering[n]
        ys[rows, :] = total
        return carry

    lax.fori_loop(0, TOK, correct, 0, unroll=4)
    for j in range(SUB):
        cols = pl.ds(j * LANE, LANE)
        out[:, cols] = (ys[pl.ds(j, TOK, stride=SUB), :] * gates[:, cols]).astype(BF16)

    for dx, dy, dc in peers:
        k = (dx * NY + dy) * NC + dc
        source = (near_x[-dx % NX] * NY + near_y[-dy % NY]) * NC + near_c[dc]
        rows = pl.ds(pl.multiple_of(source * RUN, RUN), RUN)
        remote(qs.at[0], q_out.at[rows], q_send.at[k], q_recv.at[k], partner).wait_recv()
    for b in range(NY):
        for a in range(NX):
            wait_kv(rows_of(-a, -b, 1 - c), 16 + b * NX + a)
    for copy in sends:
        copy.wait_send()
    keep_kv.wait()
    keep_q.wait()


def mix(dest, lengths, q, k, v, x, z, cw, cb, xw, dtw, dtb, rate, skip):
    dma = pltpu.SemaphoreType.DMA
    states = ((NS + 2) * SUB, LANE)
    chunk = (TOK // NZ, PROJ)
    return pl.pallas_call(
        mixer_kernel,
        out_shape=(
            jax.ShapeDtypeStruct((TOK, CH), BF16),
            jax.ShapeDtypeStruct((NSEQ * TOK, 2 * HD), BF16),
            jax.ShapeDtypeStruct((TOKENS // LANE, LANE), jnp.int32),
            jax.ShapeDtypeStruct((TOK, CH), BF16),
        ),
        in_specs=[
            whole(),
            whole(pltpu.SMEM),
            whole(pl.ANY),
            whole(pl.ANY),
            whole(),
            whole(pl.ANY),
            whole(pl.ANY),
            whole(),
            whole(),
            whole(pl.ANY),
            whole(pl.ANY),
        ]
        + [whole()] * 3,
        out_specs=(whole(pl.ANY), whole(pl.ANY), whole(), whole()),
        scratch_shapes=[
            VM((TOK, 2 * HD), BF16),
            VM((NSEQ, RUN, CH), BF16),
            VM((16, CH), BF16),
            VM((TOK + 8, CH), F32),
            VM((TOK, CH), BF16),
            VM((NZ, *chunk), BF16),
            VM((NZ, *chunk), BF16),
            VM((2, *chunk), BF16),
            VM((TOK, PROJ), BF16),
            VM((TOK * SUB, LANE), F32),
            VM((TOK * SUB, LANE), F32),
            VM((NS * SUB, LANE), F32),
            VM((2 * NS * TOK, LANE), F32),
            VM((TOK, NS * SUB, LANE), F32),
            VM((TOK * SUB, LANE), F32),
            VM((SUB, LANE), F32),
            VM(states, BF16),
            VM(states, BF16),
            VM((NY, *states), BF16),
            VM((NX, *states), BF16),
            VM((TOK, NS * SUB, LANE), F32),
            VM((TOK, CH), F32),
            VM((2, 2 * NS, NS * LANE), BF16),
            VM((TOK, CH), BF16),
            VM((TOK, CH), BF16),
            VM((TOK, CH), BF16),
            VM((PROJ, CH), BF16),
            VM((RANK, CH), BF16),
            dma((7,)),
            dma((2,)),
            dma((32,)),
            dma((32,)),
            dma((NSEQ,)),
            dma((NSEQ,)),
            dma((NZ,)),
            dma((NZ,)),
            dma((NZ,)),
            dma((NZ,)),
            dma((NZ,)),
            dma((NZ,)),
        ],
        compiler_params=pltpu.CompilerParams(
            collective_id=0, has_side_effects=True, vmem_limit_bytes=VLIM
        ),
        name="mixer",
    )(dest, lengths, q, k, v, x, z, cw, cb, xw, dtw, dtb, rate, skip)


def attend_kernel(pos_ref, len_ref, q_ref, kv_hbm, mamba_ref, out, mamba_out, scores_a, scores_b, kv_ref, sems):
    g = pl.program_id(0)
    mamba_out[...] = mamba_ref[...]
    heads = CH // HD
    rows = GROUP * RUN
    count = heads * rows
    half = count // 2
    half_rows = rows // 2
    wide = 2 * BK
    span = TOK * GROUP
    halves = TOK // LANE

    def load(i):
        part = pl.ds(pl.multiple_of(i * span, span), span)
        return pltpu.make_async_copy(kv_hbm.at[part], kv_ref.at[part], sems.at[i])

    @pl.when(g == 0)
    def _():
        for i in range(NSEQ // GROUP):
            load(i).start()

    starts = doc_starts(len_ref)
    bases = [
        sum(pos_ref[(g * GROUP + i) * halves + j, 0] for j in range(halves)) for i in range(GROUP)
    ]
    lane = lax.broadcasted_iota(jnp.int32, (1, LANE), 1) % half_rows

    def lanes(firsts):
        base = firsts[0]
        for i in range(1, GROUP // 2):
            base = jnp.where(lane >= i * RUN, firsts[i], base)
        pos = base + lane % RUN
        return pos, start_of(pos, starts)

    bounds = (lanes(bases[: GROUP // 2]), lanes(bases[GROUP // 2 :]))
    top = g * (span // wide)
    first = jnp.minimum(lax.div(start_of(bases[0], starts), wide), top)
    last_start = start_of(bases[GROUP - 1] + RUN - 1, starts)
    plain = jnp.maximum(jnp.minimum(lax.div(last_start + wide - 1, wide), top), first)
    q = jnp.concatenate(
        [
            q_ref[i * half_rows : (i + 1) * half_rows, h * HD : (h + 1) * HD]
            for i in range(2)
            for h in range(heads)
        ],
        axis=0,
    )
    scale = HD**-0.5 * LOG2E
    key_row = lax.broadcasted_iota(jnp.int32, (BK, LANE), 0)
    ones = jnp.ones((16, BK), BF16)

    def score(into, i, low=0):
        keys = kv_ref[pl.ds(pl.multiple_of(i * BK, BK), BK), pl.ds(0, HD)]
        into[:, low:count] = lax.dot_general(
            keys, q[low:], (((1,), (1,)), ((), ())), preferred_element_type=F32
        )

    def absorb(taken, i, carried, masked, low=0):
        begin = pl.multiple_of(i * BK, BK)
        best, summed = carried
        scores = taken[:, low:count]
        if masked:
            visible = [(key_row <= pos - begin) & (key_row >= at - begin) for pos, at in bounds]
            scores = jnp.concatenate(
                [
                    jnp.where(visible[(j + low) // half], scores[:, j : j + LANE], MASKED)
                    for j in range(0, count - low, LANE)
                ],
                axis=1,
            )
        new_best = jnp.maximum(best, jnp.max(scores, axis=0, keepdims=True) * scale)
        weights = jnp.exp2(scores * scale - new_best).astype(BF16)
        rescale = jnp.exp2(best - new_best)
        values = jnp.concatenate(
            [kv_ref[pl.ds(begin + j, HD), pl.ds(HD, HD)] for j in range(0, BK, HD)], axis=1
        )
        values = jnp.concatenate([values, ones], axis=0)
        product = jnp.dot(values, weights, preferred_element_type=F32)
        return new_best, summed * rescale + product

    def pair(i, carried, masked):
        score(scores_b, 2 * i + 1)
        carried = absorb(scores_a, 2 * i, carried, masked)
        score(scores_a, 2 * i + 2)
        return absorb(scores_b, 2 * i + 1, carried, masked)

    carried = (jnp.full((1, count), MASKED * scale, F32), jnp.zeros((HD + 16, count), F32))
    load(g).wait()
    score(scores_a, 2 * first)
    carried = lax.fori_loop(first, plain, lambda i, v: pair(i, v, True), carried)
    carried = lax.fori_loop(plain, top, lambda i, v: pair(i, v, False), carried)
    score(scores_b, 2 * top + 1)
    carried = absorb(scores_a, 2 * top, carried, True)
    score(scores_a, 2 * top + 2, half)
    best, summed = absorb(scores_b, 2 * top + 1, carried, True)
    later = (best[:, half:], summed[:, half:])
    score(scores_b, 2 * top + 3, half)
    later = absorb(scores_a, 2 * top + 2, later, True, half)
    later = absorb(scores_b, 2 * top + 3, later, True, half)
    for i, total in enumerate((summed[:, :half], later[1])):
        result = (total[:HD] / total[HD : HD + 1]).T.astype(BF16)
        for h in range(heads):
            out[i * half_rows : (i + 1) * half_rows, h * HD : (h + 1) * HD] = result[
                h * half_rows : (h + 1) * half_rows
            ]


def attend(positions, lengths, q, kv, mamba):
    rows = GROUP * RUN
    return pl.pallas_call(
        attend_kernel,
        out_shape=(jax.ShapeDtypeStruct((TOK, CH), BF16),) * 2,
        grid=(NSEQ // GROUP,),
        in_specs=[
            whole(pltpu.SMEM),
            whole(pltpu.SMEM),
            pl.BlockSpec((rows, CH), lambda g: (g, 0)),
            whole(pl.ANY),
            pl.BlockSpec((rows, CH), lambda g: (g, 0)),
        ],
        out_specs=(pl.BlockSpec((rows, CH), lambda g: (g, 0)),) * 2,
        scratch_shapes=[VM((BK, CH // HD * rows), F32)] * 2
        + [VM((TOKENS, 2 * HD), BF16), pltpu.SemaphoreType.DMA((NSEQ // GROUP,))],
        compiler_params=pltpu.CompilerParams(vmem_limit_bytes=VLIM),
        name="attend",
    )(positions, lengths, q, kv, mamba)


def local(
    x_branch,
    z_branch,
    conv_weight,
    conv_bias,
    xproj_weight,
    dt_weight,
    dt_bias,
    decay_rate,
    skip_gain,
    query_rows,
    key_rows,
    value_rows,
    lengths,
    destination,
):
    q, kv, positions, mamba_out = mix(
        destination.reshape(TOKENS // LANE, LANE),
        lengths,
        query_rows,
        key_rows,
        value_rows,
        x_branch,
        z_branch,
        conv_weight,
        conv_bias.reshape(1, CH),
        xproj_weight.T,
        dt_weight,
        dt_bias.reshape(1, CH),
        decay_rate,
        skip_gain.reshape(1, CH),
    )
    regrouped, mamba_out = attend(positions, lengths, q, kv, mamba_out)
    return (mamba_out, regrouped)


def solution(mesh):
    torus = Mesh(mesh.devices.reshape(NX, NY, NC, mesh.shape["mp"]), (*SEQ, "mp"))
    in_specs = (
        P(SEQ, "mp"),
        P(SEQ, "mp"),
        P(None, "mp"),
        P("mp"),
        P("mp", None),
        P(None, "mp"),
        P("mp"),
        P(None, "mp"),
        P("mp"),
        P(SEQ, "mp"),
        P(SEQ, "mp"),
        P(SEQ, "mp"),
        P(),
        P(),
    )
    out_specs = (P(SEQ, "mp"), P(SEQ, "mp"))
    return jax.shard_map(local, mesh=torus, in_specs=in_specs, out_specs=out_specs, check_vma=False)
```

```python
import math

import jax
import jax.numpy as jnp
from jax import lax
from jax.experimental import pallas as pl
from jax.experimental.pallas import tpu as pltpu
from jax.sharding import Mesh
from jax.sharding import PartitionSpec as P

SEQ = ("seq_0", "seq_1", "seq_2")
MESH = pl.DeviceIdType.MESH
VM = pltpu.VMEM
F32 = jnp.float32
BF16 = jnp.bfloat16
LOG2E = math.log2(math.e)
NX, NY, NC, NZ = 4, 4, 2, 8
NSEQ = NX * NY * NC
TOK = 256
TOK_BITS = 8
TOKENS = NSEQ * TOK
CH = 1024
LANE = 128
SUB = CH // LANE
NS = 16
RANK = 512
PROJ = RANK + 2 * NS
HD = 128
TAPS = 4
BIG_STEP = 1.0e7
MASKED = -1.0e30
GROUP = 8
RUN = TOK // NSEQ
BK = 512
VLIM = 60 * 1024 * 1024


def whole(space=VM):
    return pl.BlockSpec(memory_space=space)


def place():
    return (
        lax.axis_index("seq_0"),
        lax.axis_index("seq_1"),
        lax.axis_index("seq_2"),
        lax.axis_index("mp"),
    )


def seq_device(j, z):
    chip = lax.div(j, NC)
    return (lax.div(chip, NY), lax.rem(chip, NY), lax.rem(j, NC), z)


def doc_starts(len_ref):
    s1 = len_ref[0]
    s2 = s1 + len_ref[1]
    return s1, s2, s2 + len_ref[2]


def start_of(pos, starts):
    s1, s2, s3 = starts
    return jnp.where(pos >= s3, s3, jnp.where(pos >= s2, s2, jnp.where(pos >= s1, s1, 0)))


def silu(x):
    half = 0.5 * x
    return half * jnp.tanh(half) + half


def mixer_kernel(
    dest_ref,
    len_ref,
    q_hbm,
    k_ref,
    v_ref,
    x_hbm,
    z_hbm,
    cw_ref,
    cb_ref,
    xw_hbm,
    dtw_hbm,
    dtb_ref,
    rate_ref,
    skip_ref,
    q_out,
    kv_out,
    pos_out,
    out,
    kvs,
    qs,
    halo,
    ext,
    inner,
    part,
    taken,
    onward,
    proj,
    steps,
    drives,
    rates,
    spread,
    gains,
    ys,
    sums,
    st_own,
    st_pair,
    st_y,
    st_x,
    decays,
    gates,
    picks,
    q_ref,
    x_ref,
    z_ref,
    xw_ref,
    dtw_ref,
    loc_sem,
    halo_sem,
    kv_send,
    kv_recv,
    q_send,
    q_recv,
    rs_send,
    rs_recv,
    ag_send,
    ag_recv,
    st_send,
    st_recv,
):
    x, y, c, z = place()
    me = (x * NY + y) * NC + c
    anchor = me * TOK
    load_rows = pltpu.make_async_copy(x_hbm, x_ref, loc_sem.at[5])
    load_rows.start()
    load_q = pltpu.make_async_copy(q_hbm, q_ref, loc_sem.at[6])
    load_q.start()
    load_k = pltpu.make_async_copy(k_ref, kvs.at[:, pl.ds(0, HD)], loc_sem.at[0])
    load_k.start()
    load_x = pltpu.make_async_copy(xw_hbm, xw_ref, loc_sem.at[2])
    load_x.start()
    load_d = pltpu.make_async_copy(dtw_hbm, dtw_ref, loc_sem.at[3])
    load_d.start()
    load_z = pltpu.make_async_copy(z_hbm, z_ref, loc_sem.at[4])
    load_z.start()
    barrier = pltpu.get_barrier_semaphore()
    near_x = [lax.rem(x + d, NX) for d in range(NX)]
    near_y = [lax.rem(y + d, NY) for d in range(NY)]
    near_z = [lax.rem(z + d, NZ) for d in range(NZ)]
    near_c = [c, 1 - c]
    far_first = (2, 1, 3)
    peers = [
        (dx, dy, dc) for dx in (*far_first, 0) for dy in (*far_first, 0) for dc in range(NC)
    ][:-2] + [(0, 0, 1)]
    for dx, dy, dc in peers:
        pl.semaphore_signal(
            barrier, inc=1, device_id=(near_x[dx], near_y[dy], near_c[dc], z), device_id_type=MESH
        )
    for k in range(1, NZ):
        pl.semaphore_signal(barrier, inc=1, device_id=(x, y, c, near_z[k]), device_id_type=MESH)
    starts = doc_starts(len_ref)
    token = anchor + lax.broadcasted_iota(jnp.int32, (TOK, LANE), 0)
    depth = token - start_of(token, starts)

    def convolve(count, cols, far):
        total = cb_ref[:, cols] + cw_ref[pl.ds(0, 1), cols] * ext[pl.ds(8, count), cols]
        for lag in range(1, TAPS):
            window = ext[pl.ds(8 - lag, count), cols]
            total = total + cw_ref[pl.ds(lag, 1), cols] * jnp.where(far >= lag, window, 0.0)
        inner[pl.ds(0, count), cols] = silu(total).astype(BF16)

    def conv_columns(i, carry):
        cols = pl.ds(pl.multiple_of(i * LANE, LANE), LANE)
        ext[pl.ds(0, 8), cols] = jnp.zeros((8, LANE), F32)
        ext[pl.ds(8, TOK), cols] = x_ref[:, cols].astype(F32)
        convolve(TOK, cols, depth)
        return carry

    load_rows.wait()
    lax.fori_loop(0, SUB, conv_columns, 0)
    pl.semaphore_wait(barrier, NSEQ - 1 + NZ - 1)

    def remote(src, dst, send, recv, device):
        return pltpu.make_async_remote_copy(
            src_ref=src,
            dst_ref=dst,
            send_sem=send,
            recv_sem=recv,
            device_id=device,
            device_id_type=MESH,
        )

    def offset(a, b, core):
        a, b = a % NX, b % NY
        return (
            lax.rem(x + a * (1 - core) + b * core, NX),
            lax.rem(y + a * core + b * (1 - core), NY),
        )

    def rows_of(a, b, core):
        px, py = offset(a, b, core)
        return pl.ds(pl.multiple_of(((px * NY + py) * NC + core) * TOK, TOK), TOK)

    partner = (x, y, 1 - c, z)
    after = lax.rem(me + 1, NSEQ)
    halo_copy = remote(
        x_ref.at[pl.ds(TOK - 16, 16)], halo, halo_sem.at[0], halo_sem.at[1], seq_device(after, z)
    )
    halo_copy.start()
    for half in range(TOK // HD):
        kvs[pl.ds(half * HD, HD), pl.ds(HD, HD)] = v_ref[pl.ds(half * HD, HD), :].T

    load_q.wait()
    halves = TOK // LANE
    goal = lax.shift_right_logical(dest_ref[pl.ds(me * halves, halves), :], TOK_BITS) * RUN
    goal = goal + lax.broadcasted_iota(jnp.int32, (halves, LANE), 1) % RUN
    slot = lax.broadcasted_iota(jnp.int32, (TOK, LANE), 0)
    choice = jnp.concatenate(
        [jnp.where(slot == goal[i : i + 1], 1.0, 0.0) for i in range(halves)], axis=1
    )
    staged = jnp.dot(choice.astype(BF16), q_ref[...], preferred_element_type=F32)
    qs[...] = staged.astype(BF16).reshape(NSEQ, RUN, CH)
    load_k.wait()
    mine = kv_out.at[rows_of(0, 0, c)]
    sends = []
    for a in far_first:
        px, py = offset(a, 0, c)
        copy = remote(kvs, mine, kv_send.at[a], kv_recv.at[a], (px, py, c, z))
        copy.start()
        sends.append(copy)
    copy = remote(kvs, mine, kv_send.at[16], kv_recv.at[16], partner)
    copy.start()
    sends.append(copy)
    keep_kv = pltpu.make_async_copy(kvs, mine, loc_sem.at[0])
    keep_kv.start()
    q_rows = pl.ds(pl.multiple_of(me * RUN, RUN), RUN)
    for dx, dy, dc in peers:
        k = (dx * NY + dy) * NC + dc
        j = (near_x[dx] * NY + near_y[dy]) * NC + near_c[dc]
        device = (near_x[dx], near_y[dy], near_c[dc], z)
        copy = remote(qs.at[j], q_out.at[q_rows], q_send.at[k], q_recv.at[k], device)
        copy.start()
        sends.append(copy)
    keep_q = pltpu.make_async_copy(qs.at[me], q_out.at[q_rows], loc_sem.at[1])
    keep_q.start()

    slice_rows = TOK // NZ
    load_x.wait()

    def project(rows):
        return lax.dot_general(
            rows, xw_ref[...], (((1,), (1,)), ((), ())), preferred_element_type=F32
        ).astype(BF16)

    later = project(inner[pl.ds(slice_rows, TOK - slice_rows), :])
    part[pl.ds(1, NZ - 1)] = later.reshape(NZ - 1, slice_rows, PROJ)
    halo_copy.wait()
    ext[pl.ds(0, 8), :] = halo[pl.ds(8, 8), :].astype(F32)
    near = anchor + lax.broadcasted_iota(jnp.int32, (16, CH), 0)
    convolve(16, pl.ds(0, CH), near - start_of(near, starts))

    part[0] = project(inner[pl.ds(0, slice_rows), :])

    def begin(copy):
        copy.start()
        sends.append(copy)
        return copy

    def to_sum(src, slot, d):
        return remote(
            src, taken.at[slot], rs_send.at[slot], rs_recv.at[slot], (x, y, c, near_z[d % NZ])
        )

    far_up = begin(to_sum(part.at[near_z[4]], 1, -2))
    mid_up = begin(to_sum(part.at[near_z[5]], 0, -1))
    mid_down = begin(to_sum(part.at[near_z[3]], 2, 1))
    last = [begin(to_sum(part.at[near_z[7]], 3, -1)), begin(to_sum(part.at[near_z[1]], 4, 1))]

    def wait_kv(slot_rows, index):
        remote(kvs, kv_out.at[slot_rows], kv_send.at[0], kv_recv.at[index], partner).wait_recv()

    mid_down.wait_recv()
    onward[1] = (part[near_z[2]].astype(F32) + taken[2].astype(F32)).astype(BF16)
    last.append(begin(to_sum(onward.at[1], 6, 2)))
    mid_up.wait_recv()
    far_up.wait_recv()
    merged = part[near_z[6]].astype(F32) + taken[0].astype(F32) + taken[1].astype(F32)
    onward[0] = merged.astype(BF16)
    last.append(begin(to_sum(onward.at[0], 5, -2)))
    for a in range(NX):
        if a > 0:
            wait_kv(rows_of(-a, 0, c), a)
        block = kv_out.at[rows_of(-a, 0, c)] if a > 0 else kvs
        target = kv_out.at[rows_of(-a, 0, c)]
        for b in far_first:
            px, py = offset(0, b, c)
            index = b * NX + a
            copy = remote(
                block, target, kv_send.at[index], kv_recv.at[index], (px, py, c, z)
            )
            copy.start()
            sends.append(copy)
        if a > 0:
            copy = remote(
                block, target, kv_send.at[16 + a], kv_recv.at[16 + a], partner
            )
            copy.start()
            sends.append(copy)


    total = part[z].astype(F32)
    for copy in last:
        copy.wait_recv()
    for slot in range(3, 7):
        total = total + taken[slot].astype(F32)

    def proj_rows(d):
        return pl.ds(pl.multiple_of(near_z[d % NZ] * slice_rows, slice_rows), slice_rows)

    def to_gather(chunk, index, d):
        rows = proj.at[proj_rows(chunk)]
        return remote(
            rows, rows, ag_send.at[index], ag_recv.at[index], (x, y, c, near_z[d % NZ])
        )

    proj[proj_rows(0), :] = total.astype(BF16)
    begin(to_gather(0, 0, 2))
    begin(to_gather(0, 1, -2))
    begin(to_gather(0, 2, 1))
    begin(to_gather(0, 3, -1))
    to_gather(-2, 0, 2).wait_recv()
    begin(to_gather(-2, 4, 2))
    begin(to_gather(-2, 5, 1))
    to_gather(2, 1, -2).wait_recv()
    begin(to_gather(2, 6, -1))
    row = lax.broadcasted_iota(jnp.int32, (2 * NS, NS * LANE), 0)
    col = lax.div(lax.broadcasted_iota(jnp.int32, (2 * NS, NS * LANE), 1), LANE)
    for i in range(2):
        picks[i] = jnp.where(col + i * NS == row, 1.0, 0.0).astype(BF16)
    spots = (TOKENS // LANE, LANE)
    spot = lax.broadcasted_iota(jnp.int32, spots, 1)
    ours = (lax.shift_right_logical(dest_ref[...], TOK_BITS) == me) & (spot % RUN == 0)
    spot = spot + LANE * lax.broadcasted_iota(jnp.int32, spots, 0)
    found = jnp.sum(jnp.where(ours, spot, 0).astype(F32), axis=1, keepdims=True)
    pos_out[...] = jnp.broadcast_to(found, spots).astype(jnp.int32)
    for j in range(SUB):
        cols = pl.ds(j * LANE, LANE)
        rates[pl.ds(j, NS, stride=SUB), :] = rate_ref[:, cols] * (-LOG2E)
    for chunk, index in ((-1, 2), (1, 3), (-4, 4), (-3, 5), (3, 6)):
        to_gather(chunk, index, 1).wait_recv()

    load_d.wait()
    begins = depth == 0
    low = proj[:, pl.ds(0, RANK)]
    for j in range(SUB):
        cols = pl.ds(j * LANE, LANE)
        if j % 2 == 0:
            both = pl.ds(j * LANE, 2 * LANE)
            raw = jnp.dot(low, dtw_ref[:, both], preferred_element_type=F32)
        value = raw[:, j % 2 * LANE : (j % 2 + 1) * LANE] + dtb_ref[:, cols]
        fade = jnp.exp2(jnp.abs(value) * (-LOG2E))
        series = fade - (0.5 * fade) * fade
        tail = jnp.where(fade < 1.0e-3, series, jnp.log(1.0 + fade))
        step = jnp.maximum(value, 0.0) + tail
        drives[pl.ds(j, TOK, stride=SUB), :] = step * inner[:, cols].astype(F32)
        step = jnp.where(begins, BIG_STEP, step)
        sums[pl.ds(j, 1), :] = jnp.sum(step, axis=0, keepdims=True)
        steps[pl.ds(j, TOK, stride=SUB), :] = step

    def widen(first):
        pick = picks[first // NS]
        wide = jnp.dot(proj[:, pl.ds(RANK, 2 * NS)], pick, preferred_element_type=F32)
        for n in range(NS):
            spread[pl.ds((first + n) * TOK, TOK), :] = wide[:, n * LANE : (n + 1) * LANE]

    widen(0)
    rate = [rates[pl.ds(n * SUB, SUB), :] for n in range(NS)]

    def advance(t, carried):
        rows = pl.ds(pl.multiple_of(t * SUB, SUB), SUB)
        step = steps[rows, :]
        drive = drives[rows, :]
        result = []
        for n in range(NS):
            b = spread[pl.ds(n * TOK + t, SUB, stride=0), :]
            decay = jnp.exp2(step * rate[n])
            decays[t, pl.ds(n * SUB, SUB), :] = decay
            result.append(decay * carried[n] + b * drive)
        return tuple(result)

    zero = jnp.zeros((SUB, LANE), F32)
    state = lax.fori_loop(0, TOK, advance, (zero,) * NS, unroll=8)

    def pack(into, states, total):
        for n in range(0, NS, 2):
            pair = jnp.concatenate([states[n], states[n + 1]], axis=0)
            into[pl.ds(n * SUB, 2 * SUB), :] = pair.astype(BF16)
        high = total.astype(BF16).astype(F32)
        pair = jnp.concatenate([high, total - high], axis=0)
        into[pl.ds(NS * SUB, 2 * SUB), :] = pair.astype(BF16)

    def unpack(taken):
        block = taken[...].astype(F32).reshape(NS + 2, SUB, LANE)
        return [block[n] for n in range(NS)], block[NS] + block[NS + 1]

    def follow(states, block, total, passed=None):
        result = []
        for n in range(NS):
            moved = jnp.exp2(rate[n] * total) * states[n] + block[n]
            result.append(moved if passed is None else jnp.where(passed, moved, states[n]))
        return result

    pack(st_own, state, sums[...])
    pair_copy = remote(st_own, st_pair, st_send.at[0], st_recv.at[0], partner)
    pair_copy.start()
    sends.append(pair_copy)

    widen(NS)

    def local_token(t, carried):
        so_far, states = carried
        rows = pl.ds(pl.multiple_of(t * SUB, SUB), SUB)
        drive = drives[rows, :]
        passed = []
        result = []
        total = None
        for n in range(NS):
            decay = decays[t, pl.ds(n * SUB, SUB), :]
            b = spread[pl.ds(n * TOK + t, SUB, stride=0), :]
            weight = spread[pl.ds((NS + n) * TOK + t, SUB, stride=0), :]
            new = decay * states[n] + b * drive
            result.append(new)
            total = weight * new if total is None else total + weight * new
            left = so_far[n] * decay
            passed.append(left)
            gains[t, pl.ds(n * SUB, SUB), :] = weight * left
        ys[rows, :] = total
        return tuple(passed), tuple(result)

    carried = ((jnp.ones((SUB, LANE), F32),) * NS, (zero,) * NS)
    cuts = (0, 40, 144, TOK)
    carried = lax.fori_loop(cuts[0], cuts[1], local_token, carried, unroll=4)

    pair_copy.wait_recv()
    own_state, own_total = unpack(st_own)
    other_state, other_total = unpack(st_pair)
    first_core = c == 0
    early = [jnp.where(first_core, p, q) for p, q in zip(own_state, other_state)]
    late = [jnp.where(first_core, q, p) for p, q in zip(own_state, other_state)]
    late_total = jnp.where(first_core, other_total, own_total)
    chip_state = follow(early, late, late_total)
    pack(st_y.at[0], chip_state, own_total + other_total)
    level = []
    for k in far_first:
        copy = remote(
            st_y.at[0], st_y.at[k], st_send.at[k], st_recv.at[k], (x, near_y[k], c, z)
        )
        copy.start()
        level.append(copy)
    sends += level
    carried = lax.fori_loop(cuts[1], cuts[2], local_token, carried, unroll=4)

    for copy in level:
        copy.wait_recv()
    column, column_total = unpack(st_y.at[lax.rem(y + NY, NY)])
    for j in range(1, NY):
        block, total = unpack(st_y.at[lax.rem(y + NY - j, NY)])
        column = follow(column, block, total)
        column_total = column_total + total
    pack(st_x.at[0], column, column_total)
    level = []
    for k in far_first:
        copy = remote(
            st_x.at[0], st_x.at[k], st_send.at[4 + k], st_recv.at[4 + k], (near_x[k], y, c, z)
        )
        copy.start()
        level.append(copy)
    sends += level
    carried = lax.fori_loop(cuts[2], cuts[3], local_token, carried, unroll=4)

    for b in range(1, NY):
        for a in range(NX):
            index = b * NX + a
            wait_kv(rows_of(-a, -b, c), index)
            block = kv_out.at[rows_of(-a, -b, c)]
            copy = remote(block, block, kv_send.at[16 + index], kv_recv.at[16 + index], partner)
            copy.start()
            sends.append(copy)

    load_z.wait()
    for j in range(SUB):
        cols = pl.ds(j * LANE, LANE)
        gates[:, cols] = silu(z_ref[:, cols].astype(F32))
        inner_gain = skip_ref[:, cols] * inner[:, cols].astype(F32)
        kept = ys[pl.ds(j, TOK, stride=SUB), :]
        ys[pl.ds(j, TOK, stride=SUB), :] = kept + inner_gain
    for dx, dy, dc in peers:
        k = (dx * NY + dy) * NC + dc
        source = (near_x[-dx % NX] * NY + near_y[-dy % NY]) * NC + near_c[dc]
        rows = pl.ds(pl.multiple_of(source * RUN, RUN), RUN)
        remote(qs.at[0], q_out.at[rows], q_send.at[k], q_recv.at[k], partner).wait_recv()
    for copy in level:
        copy.wait_recv()
    entering = [zero] * NS
    for j in range(NX - 1):
        block, total = unpack(st_x.at[lax.rem(x + NX - j, NX)])
        entering = follow(entering, block, total, x > j)
    for j in range(NY - 1):
        block, total = unpack(st_y.at[lax.rem(y + NY - j, NY)])
        entering = follow(entering, block, total, y > j)
    entering = follow(entering, early, jnp.where(first_core, own_total, other_total), c > 0)

    def correct(t, carry):
        rows = pl.ds(pl.multiple_of(t * SUB, SUB), SUB)
        total = ys[rows, :]
        for n in range(NS):
            total = total + gains[t, pl.ds(n * SUB, SUB), :] * entering[n]
        ys[rows, :] = total
        return carry

    lax.fori_loop(0, TOK, correct, 0, unroll=8)
    for j in range(SUB):
        cols = pl.ds(j * LANE, LANE)
        out[:, cols] = (ys[pl.ds(j, TOK, stride=SUB), :] * gates[:, cols]).astype(BF16)

    for b in range(NY):
        for a in range(NX):
            wait_kv(rows_of(-a, -b, 1 - c), 16 + b * NX + a)
    for copy in sends:
        copy.wait_send()
    keep_kv.wait()
    keep_q.wait()


def mix(dest, lengths, q, k, v, x, z, cw, cb, xw, dtw, dtb, rate, skip):
    dma = pltpu.SemaphoreType.DMA
    states = ((NS + 2) * SUB, LANE)
    chunk = (TOK // NZ, PROJ)
    return pl.pallas_call(
        mixer_kernel,
        out_shape=(
            jax.ShapeDtypeStruct((TOK, CH), BF16),
            jax.ShapeDtypeStruct((NSEQ * TOK, 2 * HD), BF16),
            jax.ShapeDtypeStruct((TOKENS // LANE, LANE), jnp.int32),
            jax.ShapeDtypeStruct((TOK, CH), BF16),
        ),
        in_specs=[
            whole(),
            whole(pltpu.SMEM),
            whole(pl.ANY),
            whole(pl.ANY),
            whole(),
            whole(pl.ANY),
            whole(pl.ANY),
            whole(),
            whole(),
            whole(pl.ANY),
            whole(pl.ANY),
        ]
        + [whole()] * 3,
        out_specs=(whole(pl.ANY), whole(pl.ANY), whole(), whole()),
        scratch_shapes=[
            VM((TOK, 2 * HD), BF16),
            VM((NSEQ, RUN, CH), BF16),
            VM((16, CH), BF16),
            VM((TOK + 8, CH), F32),
            VM((TOK, CH), BF16),
            VM((NZ, *chunk), BF16),
            VM((NZ, *chunk), BF16),
            VM((2, *chunk), BF16),
            VM((TOK, PROJ), BF16),
            VM((TOK * SUB, LANE), F32),
            VM((TOK * SUB, LANE), F32),
            VM((NS * SUB, LANE), F32),
            VM((2 * NS * TOK, LANE), F32),
            VM((TOK, NS * SUB, LANE), F32),
            VM((TOK * SUB, LANE), F32),
            VM((SUB, LANE), F32),
            VM(states, BF16),
            VM(states, BF16),
            VM((NY, *states), BF16),
            VM((NX, *states), BF16),
            VM((TOK, NS * SUB, LANE), F32),
            VM((TOK, CH), F32),
            VM((2, 2 * NS, NS * LANE), BF16),
            VM((TOK, CH), BF16),
            VM((TOK, CH), BF16),
            VM((TOK, CH), BF16),
            VM((PROJ, CH), BF16),
            VM((RANK, CH), BF16),
            dma((7,)),
            dma((2,)),
            dma((32,)),
            dma((32,)),
            dma((NSEQ,)),
            dma((NSEQ,)),
            dma((NZ,)),
            dma((NZ,)),
            dma((NZ,)),
            dma((NZ,)),
            dma((NZ,)),
            dma((NZ,)),
        ],
        compiler_params=pltpu.CompilerParams(
            collective_id=0, has_side_effects=True, vmem_limit_bytes=VLIM
        ),
        name="mixer",
    )(dest, lengths, q, k, v, x, z, cw, cb, xw, dtw, dtb, rate, skip)


def attend_kernel(pos_ref, len_ref, q_ref, kv_hbm, mamba_ref, out, mamba_out, scores_a, scores_b, kv_ref, sems):
    g = pl.program_id(0)
    mamba_out[...] = mamba_ref[...]
    heads = CH // HD
    rows = GROUP * RUN
    count = heads * rows
    half = count // 2
    half_rows = rows // 2
    wide = 2 * BK
    span = TOK * GROUP
    halves = TOK // LANE

    def load(i):
        part = pl.ds(pl.multiple_of(i * span, span), span)
        return pltpu.make_async_copy(kv_hbm.at[part], kv_ref.at[part], sems.at[i])

    @pl.when(g == 0)
    def _():
        for i in range(NSEQ // GROUP):
            load(i).start()

    starts = doc_starts(len_ref)
    bases = [
        sum(pos_ref[(g * GROUP + i) * halves + j, 0] for j in range(halves)) for i in range(GROUP)
    ]
    lane = lax.broadcasted_iota(jnp.int32, (1, LANE), 1) % half_rows

    def lanes(firsts):
        base = firsts[0]
        for i in range(1, GROUP // 2):
            base = jnp.where(lane >= i * RUN, firsts[i], base)
        pos = base + lane % RUN
        return pos, start_of(pos, starts)

    bounds = (lanes(bases[: GROUP // 2]), lanes(bases[GROUP // 2 :]))
    top = g * (span // wide)
    first = jnp.minimum(lax.div(start_of(bases[0], starts), wide), top)
    last_start = start_of(bases[GROUP - 1] + RUN - 1, starts)
    plain = jnp.maximum(jnp.minimum(lax.div(last_start + wide - 1, wide), top), first)
    q = jnp.concatenate(
        [
            q_ref[i * half_rows : (i + 1) * half_rows, h * HD : (h + 1) * HD]
            for i in range(2)
            for h in range(heads)
        ],
        axis=0,
    )
    scale = HD**-0.5 * LOG2E
    key_row = lax.broadcasted_iota(jnp.int32, (BK, LANE), 0)
    ones = jnp.ones((16, BK), BF16)

    def score(into, i, low=0):
        keys = kv_ref[pl.ds(pl.multiple_of(i * BK, BK), BK), pl.ds(0, HD)]
        into[:, low:count] = lax.dot_general(
            keys, q[low:], (((1,), (1,)), ((), ())), preferred_element_type=F32
        )

    def absorb(taken, i, carried, masked, low=0):
        begin = pl.multiple_of(i * BK, BK)
        best, summed = carried
        scores = taken[:, low:count]
        if masked:
            visible = [(key_row <= pos - begin) & (key_row >= at - begin) for pos, at in bounds]
            scores = jnp.concatenate(
                [
                    jnp.where(visible[(j + low) // half], scores[:, j : j + LANE], MASKED)
                    for j in range(0, count - low, LANE)
                ],
                axis=1,
            )
        new_best = jnp.maximum(best, jnp.max(scores, axis=0, keepdims=True) * scale)
        weights = jnp.exp2(scores * scale - new_best).astype(BF16)
        rescale = jnp.exp2(best - new_best)
        values = jnp.concatenate(
            [kv_ref[pl.ds(begin + j, HD), pl.ds(HD, HD)] for j in range(0, BK, HD)], axis=1
        )
        values = jnp.concatenate([values, ones], axis=0)
        product = jnp.dot(values, weights, preferred_element_type=F32)
        return new_best, summed * rescale + product

    def pair(i, carried, masked):
        score(scores_b, 2 * i + 1)
        carried = absorb(scores_a, 2 * i, carried, masked)
        score(scores_a, 2 * i + 2)
        return absorb(scores_b, 2 * i + 1, carried, masked)

    carried = (jnp.full((1, count), MASKED * scale, F32), jnp.zeros((HD + 16, count), F32))
    load(g).wait()
    score(scores_a, 2 * first)
    carried = lax.fori_loop(first, plain, lambda i, v: pair(i, v, True), carried)
    carried = lax.fori_loop(plain, top, lambda i, v: pair(i, v, False), carried)
    score(scores_b, 2 * top + 1)
    carried = absorb(scores_a, 2 * top, carried, True)
    score(scores_a, 2 * top + 2, half)
    best, summed = absorb(scores_b, 2 * top + 1, carried, True)
    later = (best[:, half:], summed[:, half:])
    score(scores_b, 2 * top + 3, half)
    later = absorb(scores_a, 2 * top + 2, later, True, half)
    later = absorb(scores_b, 2 * top + 3, later, True, half)
    for i, total in enumerate((summed[:, :half], later[1])):
        result = (total[:HD] / total[HD : HD + 1]).T.astype(BF16)
        for h in range(heads):
            out[i * half_rows : (i + 1) * half_rows, h * HD : (h + 1) * HD] = result[
                h * half_rows : (h + 1) * half_rows
            ]


def attend(positions, lengths, q, kv, mamba):
    rows = GROUP * RUN
    return pl.pallas_call(
        attend_kernel,
        out_shape=(jax.ShapeDtypeStruct((TOK, CH), BF16),) * 2,
        grid=(NSEQ // GROUP,),
        in_specs=[
            whole(pltpu.SMEM),
            whole(pltpu.SMEM),
            pl.BlockSpec((rows, CH), lambda g: (g, 0)),
            whole(pl.ANY),
            pl.BlockSpec((rows, CH), lambda g: (g, 0)),
        ],
        out_specs=(pl.BlockSpec((rows, CH), lambda g: (g, 0)),) * 2,
        scratch_shapes=[VM((BK, CH // HD * rows), F32)] * 2
        + [VM((TOKENS, 2 * HD), BF16), pltpu.SemaphoreType.DMA((NSEQ // GROUP,))],
        compiler_params=pltpu.CompilerParams(vmem_limit_bytes=VLIM),
        name="attend",
    )(positions, lengths, q, kv, mamba)


def local(
    x_branch,
    z_branch,
    conv_weight,
    conv_bias,
    xproj_weight,
    dt_weight,
    dt_bias,
    decay_rate,
    skip_gain,
    query_rows,
    key_rows,
    value_rows,
    lengths,
    destination,
):
    q, kv, positions, mamba_out = mix(
        destination.reshape(TOKENS // LANE, LANE),
        lengths,
        query_rows,
        key_rows,
        value_rows,
        x_branch,
        z_branch,
        conv_weight,
        conv_bias.reshape(1, CH),
        xproj_weight.T,
        dt_weight,
        dt_bias.reshape(1, CH),
        decay_rate,
        skip_gain.reshape(1, CH),
    )
    regrouped, mamba_out = attend(positions, lengths, q, kv, mamba_out)
    return (mamba_out, regrouped)


def solution(mesh):
    torus = Mesh(mesh.devices.reshape(NX, NY, NC, mesh.shape["mp"]), (*SEQ, "mp"))
    in_specs = (
        P(SEQ, "mp"),
        P(SEQ, "mp"),
        P(None, "mp"),
        P("mp"),
        P("mp", None),
        P(None, "mp"),
        P("mp"),
        P(None, "mp"),
        P("mp"),
        P(SEQ, "mp"),
        P(SEQ, "mp"),
        P(SEQ, "mp"),
        P(),
        P(),
    )
    out_specs = (P(SEQ, "mp"), P(SEQ, "mp"))
    return jax.shard_map(local, mesh=torus, in_specs=in_specs, out_specs=out_specs, check_vma=False)
```
